32 devices in a mesh: groups: 2 (over x), sect: 8 (over z, y), head: 2 (over core).
Axes of the slice: x: 2, y: 2, z: 4, core: 2. Of those that a mesh axis runs over, the one named last changes fastest.
Arguments:
- queries: bfloat16 [2048, 8192], P(('groups', 'sect'), 'head'), parts along dimension 0, may hold values from -200 to 200
- packed_key_rows: bfloat16 [2048, 512], P(('groups', 'sect'), 'head'), parts along dimension 0, may hold values from -7 to 7
- values: bfloat16 [2048, 512], P(('groups', 'sect'), 'head'), parts along dimension 0, may hold values from -12 to 12
- segments: int32 [2048], P('groups'), parts along dimension 0, may hold values from 0 to 7, never falling along the last dimension, each value on 1 to 512 neighbouring positions
- proj_weight: bfloat16 [8192, 2048], P('head', 'sect'), may hold values from -0.0625 to 0.0625
- residual: bfloat16 [2048, 2048], P(('groups', 'sect', 'head')), parts along dimension 0, may hold values from -2 to 2
- norm_gain: bfloat16 [2048], replicated, may hold values from 0.5 to 1.5
- expert_ids: int32 [2048, 8], P(('groups', 'sect', 'head')), parts along dimension 0, may hold values from 0 to 15, all different within a row; in each aligned block of 64 rows (0 to 63, 64 to 127, ...) at most 48 rows name the same one
- route_weights: float32 [2048, 8], P(('groups', 'sect', 'head')), parts along dimension 0, may hold values from 0.05 to 1
- gate_weight: bfloat16 [16, 2048, 768], P(('sect', 'head')), may hold values from -0.125 to 0.125
- up_weight: bfloat16 [16, 2048, 768], P(('sect', 'head')), may hold values from -0.125 to 0.125
- down_weight: bfloat16 [16, 768, 2048], P(('sect', 'head')), may hold values from -0.21875 to 0.21875
Outputs:
- hidden_mid: bfloat16 [2048, 2048], P(('groups', 'sect', 'head')), parts along dimension 0
- expert_mix: bfloat16 [2048, 2048], P(('groups', 'sect', 'head')), parts along dimension 0
The draws below stay inside these ranges and needn't reach their ends.
There are 2 independent parts, one for each index of `groups`. The reference program is written for one: setup_inputs(seed, part) draws one part's arguments, and reference() takes and returns one part's arrays. A program takes and returns all parts, laid end to end along the dimension named above; an argument that names none is the same for every part. Nothing has to cross between parts.
Inputs may be any that keep to these rules, and one draw needn't show every extreme that they name: `segments`: ids never fall along the rows; each of the 8 prompts has 1 to 512 rows, and one has exactly that many. `expert_ids`: each row names 8 different experts. Within the rows of one device (aligned blocks of 64 rows) no expert is named by more than 48 rows.
All inputs are finite; a program needn't handle non-finite values.
Results may differ from the reference program's by a relative error of at most 0.02.
Values may be sent and summed in bfloat16 or wider, within the bound.
A program may use at most 256 MiB of HBM per device.

```python
import math
import jax
import jax.numpy as jnp
import numpy as np
from jax import lax

D = 2048
FF = 768
QUERY_HEADS = 64
KEY_VALUE_HEADS = 4
HEAD_WIDTH = 128
TOPK = 8
PROMPTS = 8
SECTION_ROWS = 128
TOKEN_TOTAL = 1024
MOE_ROWS = 64
EXPERTS = 16
CAP = 48
N_SECT = 8
N_HEAD = 2


def base_keys(key):
    unshaped_draw = jax.random.normal(jax.random.fold_in(key, 11), (TOKEN_TOTAL, KEY_VALUE_HEADS, HEAD_WIDTH), jnp.float32)
    return jnp.clip(unshaped_draw, -6.0, 6.0)


def draw_packed_key_rows(key, part):
    key_random_draw = base_keys(key)
    return key_random_draw.reshape(TOKEN_TOTAL, KEY_VALUE_HEADS * HEAD_WIDTH).astype(jnp.bfloat16)


def draw_queries(key, part):
    query_draw = jnp.clip(jax.random.normal(jax.random.fold_in(key, 12), (TOKEN_TOTAL, QUERY_HEADS, HEAD_WIDTH), jnp.float32), -6.0, 6.0)
    return query_draw.reshape(TOKEN_TOTAL, QUERY_HEADS * HEAD_WIDTH).astype(jnp.bfloat16)


def steps_of(key, extent, split, low, top_value):
    factor_of = 1.0
    for position, parts in split:
        draws = jax.random.uniform(jax.random.fold_in(jax.random.fold_in(key, 6), position), (parts,), jnp.float32, low / len(split), top_value / len(split))
        factor_of = factor_of * jnp.repeat(jnp.exp(draws), extent[position] // parts).reshape((-1,) + (1,) * (len(extent) - 1 - position))
    return factor_of


def length_profile(number_of, total, most, slope):
    loads = [(1 << 20) // math.isqrt(standing ** slope) + 1 for standing in range(2, number_of + 1)]
    rest, given = total - most - (number_of - 1), [1] * (number_of - 1)
    while rest > 0:
        movable = [i for i in range(number_of - 1) if given[i] < most]
        whole, budget = sum([loads[i] for i in movable]), rest
        for i in movable:
            addition = min(most - given[i], max(1, budget * loads[i] // whole), rest)
            given[i] = given[i] + addition
            rest = rest - addition
    return np.array([most] + given)


def ragged_sizes(own_key, count, total, most, slope):
    if count == 2:
        one = jax.random.randint(own_key, (), max(1, total - most), min(most, total - 1) + 1)
        return jnp.stack([one, total - one])
    sizes = jnp.asarray(length_profile(count, total, most, slope), jnp.int32)
    pairs = (count - 1) // 2
    giver, receiver = sizes[1:1 + 2 * pairs:2], sizes[2:2 + 2 * pairs:2]
    slack = jnp.minimum(giver - 1, most - receiver)
    shifted = jax.random.randint(jax.random.fold_in(own_key, 1), (pairs,), 0, 1 << 20) % (slack + 1)
    sizes = sizes.at[1:1 + 2 * pairs:2].set(giver - shifted).at[2:2 + 2 * pairs:2].set(receiver + shifted)
    return sizes[jax.random.permutation(jax.random.fold_in(own_key, 2), count)]


def deal_out(key, own, number, rows, count, top, most, skew):
    order = jax.random.permutation(key, count)
    heavy_load, usual = portions_of(count, rows * top, most, skew, True), portions_of(count, rows * top, most, skew, False)
    places = jnp.arange(count)

    def named(sizes, turn):
        used = int((sizes > 0).sum())
        fixed = max(1, used // 4)
        moved = fixed + (places - fixed + turn * (used - fixed)) % max(1, count - fixed)
        return jnp.zeros((count,), jnp.int32).at[order[jnp.where(places < fixed, places, moved)]].set(jnp.asarray(sizes, jnp.int32))

    sizes = jnp.where(number % 4 == 0, named(heavy_load, number // 4), named(usual, number - number // 4 - 1))
    mixed = jax.random.permutation(jax.random.fold_in(own, 3), count)
    donor, receiver = mixed[0:count // 2 * 2:2], mixed[1:count // 2 * 2:2]
    slack = jnp.minimum(sizes[donor] - 1, most - sizes[receiver]) // 2
    slack = jnp.where((donor == order[0]) | (receiver == order[0]) | (sizes[receiver] == 0), 0, jnp.maximum(slack, 0))
    moved = jax.random.randint(jax.random.fold_in(own, 4), (count // 2,), 0, 1 << 20) % (slack + 1)
    sizes = sizes.at[donor].add(-moved).at[receiver].add(moved)
    items = jnp.searchsorted(jnp.cumsum(sizes), jnp.arange(rows * top), side="right").astype(jnp.int32)
    table = items.reshape(top, rows).T
    table = table[jax.random.permutation(jax.random.fold_in(own, 1), rows)]
    turn = jax.random.randint(jax.random.fold_in(own, 2), (rows, 1), 0, top)
    return jnp.take_along_axis(table, (jnp.arange(top)[None, :] + turn) % top, axis=1)


def portions_of(number_of, total, bound, skew, full):
    weights = [(1 << 20) // math.isqrt(rank ** skew) + 1 for rank in range(1, number_of + 1)]
    largest = bound if full else min(bound, max(-(-total // number_of), total * weights[0] // sum(weights)))
    least = 1 if total - largest >= number_of - 1 else 0
    counts, surplus = [largest] + [least] * (number_of - 1), total - largest - least * (number_of - 1)
    while surplus > 0:
        candidates = [i for i in range(1, number_of) if counts[i] < largest] or [i for i in range(1, number_of) if counts[i] < bound]
        mass, remaining = sum([weights[i] for i in candidates]), surplus
        for i in candidates:
            extra = min(bound - counts[i], max(1, remaining * weights[i] // mass), surplus)
            counts[i] = counts[i] + extra
            surplus = surplus - extra
    return np.array(counts)


def scatter_about(key, shape, width, reach, split=(), kind=jnp.bfloat16):
    entries = width * jax.random.normal(key, shape, jnp.float32)
    if split:
        entries = entries * steps_of(key, shape, split, -0.22, 0.18)
    return jnp.clip(entries, -reach, reach).astype(kind)


def setup_inputs(seed: int = 0, part: int = 0) -> dict:
    keys = jax.random.split(jax.random.key(seed), 13)
    part_splits = jax.random.split(jax.random.fold_in(keys[12], part), 13)
    queries = draw_queries(jax.random.fold_in(jax.random.fold_in(keys[12], part), 71), part)
    packed_key_rows = draw_packed_key_rows(jax.random.fold_in(jax.random.fold_in(keys[12], part), 71), part)
    values = scatter_about(part_splits[2], (TOKEN_TOTAL, KEY_VALUE_HEADS * HEAD_WIDTH), 2.0, 12.0, ((0, 8), (1, 2)))
    segments = jnp.searchsorted(jnp.cumsum(ragged_sizes(part_splits[3], PROMPTS, TOKEN_TOTAL, TOKEN_TOTAL // 2, 2)), jnp.arange(TOKEN_TOTAL), side="right").astype(jnp.int32)
    proj_weight = scatter_about(keys[4], (QUERY_HEADS * HEAD_WIDTH, D), (QUERY_HEADS * HEAD_WIDTH) ** -0.5, 0.0625, ((0, 2), (1, 8)))
    residual = scatter_about(part_splits[5], (TOKEN_TOTAL, D), 0.25, 2.0, ((0, 16),))
    norm_gain = jnp.clip(1.0 + 0.1 * jax.random.normal(keys[6], (D,), jnp.float32), 0.5, 1.5).astype(jnp.bfloat16)
    expert_ids_keys = jax.random.split(jax.random.fold_in(part_splits[7], 1), TOKEN_TOTAL // MOE_ROWS)
    expert_ids_turns = jax.random.permutation(jax.random.fold_in(part_splits[7], 3), TOKEN_TOTAL // MOE_ROWS)
    expert_ids = jax.vmap(lambda own, number: deal_out(jax.random.fold_in(part_splits[7], 2), own, number, MOE_ROWS, EXPERTS, TOPK, CAP, 2))(expert_ids_keys, expert_ids_turns).reshape((TOKEN_TOTAL, TOPK))
    route_weights = jnp.clip(jnp.exp(math.log(1.0) - 2.9957323 * jax.random.uniform(part_splits[8], (TOKEN_TOTAL, TOPK), jnp.float32) ** steps_of(part_splits[8], (TOKEN_TOTAL, TOPK), ((0, 16),), -0.2, 0.2)), 0.05, 1.0)
    gate_weight = scatter_about(keys[9], (EXPERTS, D, FF), D ** -0.5, 0.125, ((0, 16),))
    up_weight = scatter_about(keys[10], (EXPERTS, D, FF), D ** -0.5, 0.125, ((0, 16),))
    down_weight = scatter_about(keys[11], (EXPERTS, FF, D), FF ** -0.5, 0.21875, ((0, 16),))
    return {"queries": queries, "packed_key_rows": packed_key_rows, "values": values, "segments": segments, "proj_weight": proj_weight, "residual": residual, "norm_gain": norm_gain, "expert_ids": expert_ids, "route_weights": route_weights, "gate_weight": gate_weight, "up_weight": up_weight, "down_weight": down_weight}


negative_large = -1e+30
norm_eps = 1e-06

def attention_block(block_pos, queries, packed_key_rows, values, segments):
    query_group_width = QUERY_HEADS // KEY_VALUE_HEADS
    key_window_length = min(128, TOKEN_TOTAL)
    key_block_count = TOKEN_TOTAL // key_window_length
    beginning_row = (block_pos * SECTION_ROWS).astype(jnp.int32)
    query_tensor_four = lax.dynamic_slice_in_dim(queries, beginning_row, SECTION_ROWS, 0).astype(jnp.float32).reshape(SECTION_ROWS, KEY_VALUE_HEADS, query_group_width, HEAD_WIDTH)
    query_pos = beginning_row + jnp.arange(SECTION_ROWS, dtype=jnp.int32)
    query_seg = lax.dynamic_slice_in_dim(segments, beginning_row, SECTION_ROWS, 0)
    seg_start = lax.optimization_barrier(jnp.sum((segments[None, :] < query_seg[:, None]).astype(jnp.int32), axis=1))
    lowest = jnp.min(seg_start)
    highest = jnp.max(query_pos)
    score_scale = 1.0 / math.sqrt(HEAD_WIDTH)

    def piece_scores(block_index):
        key_begin_index = (block_index * key_window_length).astype(jnp.int32)
        key_tensor_three = lax.dynamic_slice_in_dim(packed_key_rows, key_begin_index, key_window_length, 0).astype(jnp.float32).reshape(key_window_length, KEY_VALUE_HEADS, HEAD_WIDTH)
        scores = jnp.einsum('rkgd,pkd->rkgp', query_tensor_four, key_tensor_three, precision=lax.Precision.HIGHEST) * score_scale
        key_pos = key_begin_index + jnp.arange(key_window_length, dtype=jnp.int32)
        key_seg = lax.dynamic_slice_in_dim(segments, key_begin_index, key_window_length, 0)
        allowed = jnp.logical_and(key_seg[None, :] == query_seg[:, None], key_pos[None, :] <= query_pos[:, None])
        return (scores, allowed[:, None, None, :], key_begin_index)

    def needed(block_index):
        key_begin_index = block_index * key_window_length
        return jnp.logical_and(key_begin_index <= highest, key_begin_index + key_window_length - 1 >= lowest)

    def maximum_update(block_index, run_max):

        def compute(current):
            scores, allowed, key_begin_index = piece_scores(block_index)
            return jnp.maximum(current, lax.optimization_barrier(jnp.max(jnp.where(allowed, scores, negative_large), axis=-1)))
        return lax.cond(needed(block_index), compute, lambda running: running, run_max)
    row_maximum = lax.fori_loop(0, key_block_count, maximum_update, jnp.full((SECTION_ROWS, KEY_VALUE_HEADS, query_group_width), negative_large, jnp.float32))

    def sum_step(block_index, running):

        def compute(current):
            weight_sum, run_acc = current
            scores, allowed, key_begin_index = piece_scores(block_index)
            weights = jnp.where(allowed, jnp.exp(scores - row_maximum[..., None]), 0.0).astype(jnp.bfloat16)
            weights = lax.optimization_barrier(weights).astype(jnp.float32)
            value_tensor_three = lax.dynamic_slice_in_dim(values, key_begin_index, key_window_length, 0).astype(jnp.float32).reshape(key_window_length, KEY_VALUE_HEADS, HEAD_WIDTH)
            run_acc = run_acc + jnp.einsum('rkgp,pkd->rkgd', weights, value_tensor_three, precision=lax.Precision.HIGHEST)
            return (weight_sum + lax.optimization_barrier(jnp.sum(weights, axis=-1)), run_acc)
        return lax.cond(needed(block_index), compute, lambda kept: kept, running)
    initial_state = (jnp.zeros((SECTION_ROWS, KEY_VALUE_HEADS, query_group_width), jnp.float32), jnp.zeros((SECTION_ROWS, KEY_VALUE_HEADS, query_group_width, HEAD_WIDTH), jnp.float32))
    weight_sum, run_acc = lax.fori_loop(0, key_block_count, sum_step, initial_state)
    return (run_acc / weight_sum[..., None]).reshape(SECTION_ROWS, QUERY_HEADS * HEAD_WIDTH).astype(jnp.bfloat16)

def reference(queries, packed_key_rows, values, segments, proj_weight, residual, norm_gain, expert_ids, route_weights, gate_weight, up_weight, down_weight):
    attended = lax.map(lambda block_pos: attention_block(block_pos, queries, packed_key_rows, values, segments), jnp.arange(TOKEN_TOTAL // SECTION_ROWS, dtype=jnp.int32))
    attended = attended.reshape(TOKEN_TOTAL, QUERY_HEADS * HEAD_WIDTH)
    projected = jnp.dot(attended, proj_weight, preferred_element_type=jnp.float32)
    hidden_mid = (residual.astype(jnp.float32) + projected).astype(jnp.bfloat16)
    mid_float = lax.optimization_barrier(hidden_mid).astype(jnp.float32)
    inverse = lax.rsqrt(lax.optimization_barrier(jnp.mean(mid_float * mid_float, axis=1, keepdims=True)) + norm_eps)
    normed = (mid_float * inverse * norm_gain.astype(jnp.float32)[None, :]).astype(jnp.bfloat16)
    route_share = (route_weights / lax.optimization_barrier(jnp.sum(route_weights, axis=1, keepdims=True))).reshape(-1)
    flat_ids = expert_ids.reshape(-1)
    slot_total = N_SECT * N_HEAD * CAP

    def expert_step(mixture, expert):
        named = flat_ids == expert
        picked = jnp.nonzero(named, size=slot_total, fill_value=0)[0].astype(jnp.int32)
        valid_slot = jnp.arange(slot_total, dtype=jnp.int32) < jnp.sum(named.astype(jnp.int32))
        row_ids = picked // TOPK
        inputs = normed[row_ids]
        gate_act = jnp.dot(inputs, gate_weight[expert], preferred_element_type=jnp.float32)
        up_act = jnp.dot(inputs, up_weight[expert], preferred_element_type=jnp.float32)
        hidden = (jax.nn.silu(gate_act) * up_act).astype(jnp.bfloat16)
        result = jnp.dot(hidden, down_weight[expert], preferred_element_type=jnp.float32).astype(jnp.bfloat16)
        result = lax.optimization_barrier(result).astype(jnp.float32)
        weight = jnp.where(valid_slot, route_share[picked], 0.0)
        mixture = mixture.at[row_ids].add(weight[:, None] * result)
        return (mixture, None)
    mixture, unused = lax.scan(expert_step, jnp.zeros((TOKEN_TOTAL, D), jnp.float32), jnp.arange(EXPERTS, dtype=jnp.int32))
    return (hidden_mid, mixture.astype(jnp.bfloat16))
```

```python
import functools
import math

import jax
import jax.numpy as jnp
from jax import lax
from jax.experimental import pallas as pl
from jax.experimental.pallas import tpu as pltpu
from jax.sharding import PartitionSpec as P

HEAD_WIDTH = 128
MASKED = -1e30
NORM_EPS = 1e-06
VMEM_ROOM = 64 << 20
LAYER_ROOM = 52 << 20

MESH = pl.DeviceIdType.MESH
VMEM_SPEC = pl.BlockSpec(memory_space=pltpu.VMEM)
ANY_SPEC = pl.BlockSpec(memory_space=pl.ANY)
DMA = pltpu.SemaphoreType.DMA

def greet(devices):
    barrier = pltpu.get_barrier_semaphore()
    for device in devices:
        pl.semaphore_signal(barrier, inc=1, device_id=device, device_id_type=MESH)
    pl.semaphore_wait(barrier, len(devices))

def remote(src, dst, send_sem, recv_sem, device):
    return pltpu.make_async_remote_copy(
        src_ref=src,
        dst_ref=dst,
        send_sem=send_sem,
        recv_sem=recv_sem,
        device_id=device,
        device_id_type=MESH,
    )

def attention_body(
    extra,
    groups,
    sects,
    kv_heads,
    q_ref,
    k_ref,
    v_ref,
    seg_ref,
    w_ref,
    a_out,
    w_out,
    kv_ref,
    kv_all,
    att,
    bias,
    kz_send,
    kz_recv,
    ky_send,
    ky_recv,
    a_send,
    a_recv,
    w_send,
    w_recv,
    f_send,
    f_recv,
    local_sem,
):
    g = lax.axis_index("groups")
    s = lax.axis_index("sect")
    halves = sects // 2
    h = s // 2
    low = lax.rem(s, 2)
    rows = q_ref.shape[0]
    cols = q_ref.shape[1] // sects
    w_cols = w_ref.shape[1]
    w_rows = w_ref.shape[0] // sects
    part = w_rows // groups
    other_y = 2 * h + 1 - low
    sect_peers = [lax.rem(s + i, sects) for i in range(1, sects)]
    group_peers = [lax.rem(g + i, groups) for i in range(1, groups)]
    half = k_ref.shape[1]
    own_k = pltpu.make_async_copy(k_ref, kv_ref.at[:, pl.ds(0, half)], local_sem.at[3])
    own_v = pltpu.make_async_copy(v_ref, kv_ref.at[:, pl.ds(half, half)], local_sem.at[4])
    own_k.start()
    own_v.start()
    greet(
        [{"sect": t} for t in sect_peers] + [{"groups": t} for t in group_peers] + extra
    )
    started = []
    own_k.wait()
    own_v.wait()

    def kv_cross(t):
        return remote(
            kv_ref if t is None else kv_all.at[2 * t + low],
            kv_all.at[s if t is None else 2 * t + low],
            ky_send.at[h if t is None else t],
            ky_recv.at[h if t is None else t],
            {"sect": other_y},
        )

    for i in range(1, halves):
        t = lax.rem(h + i, halves)
        copy = remote(
            kv_ref, kv_all.at[s], kz_send.at[t], kz_recv.at[h], {"sect": 2 * t + low}
        )
        copy.start()
        started.append(copy)
    copy = kv_cross(None)
    copy.start()
    started.append(copy)
    own_kv = pltpu.make_async_copy(kv_ref, kv_all.at[s], local_sem.at[0])
    own_kv.start()

    def w_piece(t):
        return w_ref.at[pl.ds(pl.multiple_of(t * w_rows + g * part, part), part), :]

    def w_place(group, t):
        span = pl.ds(pl.multiple_of(group * part, part), part)
        if len(w_out.shape) == 3:
            return w_out.at[t, span, :]
        return w_out.at[span, pl.ds(pl.multiple_of(t * w_cols, w_cols), w_cols)]

    for t in sect_peers:
        copy = remote(
            w_piece(t), w_place(g, s), w_send.at[t], w_recv.at[s], {"sect": t}
        )
        copy.start()
        started.append(copy)
    own_w = pltpu.make_async_copy(w_piece(s), w_place(g, s), local_sem.at[1])
    own_w.start()
    for i, t in enumerate(group_peers):
        copy = remote(
            w_piece(s), w_place(g, s), f_send.at[i, s], f_recv.at[g, s], {"groups": t}
        )
        copy.start()
        started.append(copy)

    for i in range(1, halves):
        t = lax.rem(h + i, halves)
        remote(
            kv_ref, kv_all.at[2 * t + low], kz_send.at[t], kz_recv.at[t], {"sect": 2 * t + low}
        ).wait_recv()
        copy = kv_cross(t)
        copy.start()
        started.append(copy)

    window = bias.shape[1]
    blocks = window // rows
    first = jnp.maximum(s - (blocks - 1), 0)
    row_of = lax.broadcasted_iota(jnp.int32, (rows, rows), 0)
    col_of = lax.broadcasted_iota(jnp.int32, (rows, rows), 1)
    seg_q = jnp.sum(
        jnp.where(row_of == col_of, seg_ref[s].astype(jnp.float32), 0.0), axis=1, keepdims=True
    )
    for b in range(blocks):
        behind = (s - first - b) * rows + row_of - col_of
        same = seg_q == seg_ref[first + b].astype(jnp.float32)
        bias[:, b * rows : (b + 1) * rows] = jnp.where(
            jnp.logical_and(same, behind >= 0), 0.0, MASKED
        )

    for i in range(halves):
        t = lax.rem(h + i, halves)
        remote(
            kv_ref, kv_all.at[2 * t + 1 - low], ky_send.at[t], ky_recv.at[t], {"sect": other_y}
        ).wait_recv()
    own_kv.wait()

    scale = 1.0 / math.sqrt(HEAD_WIDTH)
    kv_width = kv_heads * HEAD_WIDTH
    per_kv = q_ref.shape[1] // kv_heads

    def attend(i, carry):
        t = lax.rem(s + 1 + i, sects)
        kv_head = (t * cols) // per_kv
        k_col = pl.multiple_of(kv_head * HEAD_WIDTH, HEAD_WIDTH)
        v_col = pl.multiple_of(kv_width + kv_head * HEAD_WIDTH, HEAD_WIDTH)
        span = pl.ds(first, blocks)
        keys = kv_all[span, :, pl.ds(k_col, HEAD_WIDTH)].reshape(window, HEAD_WIDTH)
        vals = kv_all[span, :, pl.ds(v_col, HEAD_WIDTH)].reshape(window, HEAD_WIDTH)
        for j in range(cols // HEAD_WIDTH):
            q_col = pl.multiple_of(t * cols + j * HEAD_WIDTH, HEAD_WIDTH)
            q = q_ref[:, pl.ds(q_col, HEAD_WIDTH)]
            scores = lax.dot_general(
                q, keys, (((1,), (1,)), ((), ())), preferred_element_type=jnp.float32
            )
            scores = scores * scale + bias[...]
            top = jnp.max(scores, axis=1, keepdims=True)
            weights = jnp.exp(scores - top).astype(jnp.bfloat16)
            total = jnp.sum(weights.astype(jnp.float32), axis=1, keepdims=True)
            mixed = jnp.dot(weights, vals, preferred_element_type=jnp.float32)
            att[t, :, j * HEAD_WIDTH : (j + 1) * HEAD_WIDTH] = (mixed / total).astype(
                jnp.bfloat16
            )
        return carry

    def a_place(t):
        return a_out.at[pl.ds(pl.multiple_of(t * rows, rows), rows), :]

    def a_copy(t):
        return remote(att.at[t], a_place(s), a_send.at[t], a_recv.at[s], {"sect": t})

    def step(i, carry):
        attend(i, carry)

        @pl.when(i >= 1)
        def _():
            a_copy(lax.rem(s + i, sects)).start()

        return carry

    lax.fori_loop(0, sects, step, 0)
    own_a = pltpu.make_async_copy(att.at[s], a_place(s), local_sem.at[2])
    own_a.start()

    for t in sect_peers:
        remote(
            w_piece(s), w_place(g, t), w_send.at[t], w_recv.at[t], {"sect": t}
        ).wait_recv()
        for i, u in enumerate(group_peers):
            copy = remote(
                w_place(g, t), w_place(g, t), f_send.at[i, t], f_recv.at[g, t], {"groups": u}
            )
            copy.start()
            started.append(copy)

    def wait_rows(t):
        remote(att.at[t], a_place(t), a_send.at[t], a_recv.at[t], {"sect": t}).wait_recv()

    def wait_weight():
        for u in group_peers:
            for t in [s] + sect_peers:
                remote(
                    w_place(g, t),
                    w_place(u, t),
                    f_send.at[0, t],
                    f_recv.at[u, t],
                    {"groups": u},
                ).wait_recv()
        own_w.wait()

    def drain():
        for copy in started:
            copy.wait_send()
        for t in sect_peers:
            a_copy(t).wait_send()

    return sect_peers, wait_rows, wait_weight, own_a.wait, drain

def attention_kernel(*arguments):
    sect_peers, wait_rows, wait_weight, wait_own, drain = attention_body([], *arguments)
    for t in sect_peers:
        wait_rows(t)
    wait_weight()
    wait_own()
    drain()

def attention_scratch(groups, sects, rows, cols, kv_shape, window):
    return [
        pltpu.VMEM(kv_shape, jnp.bfloat16),
        pltpu.VMEM((sects,) + kv_shape, jnp.bfloat16),
        pltpu.VMEM((sects, rows, cols), jnp.bfloat16),
        pltpu.VMEM((rows, window), jnp.float32),
        DMA((sects // 2,)),
        DMA((sects // 2,)),
        DMA((sects // 2,)),
        DMA((sects // 2,)),
        DMA((sects,)),
        DMA((sects,)),
        DMA((sects,)),
        DMA((sects,)),
        DMA((groups, sects)),
        DMA((groups, sects)),
        DMA((5,)),
    ]

def exchange_attention(queries, keys, values, segments, proj_weight):
    kv_heads = keys.shape[1] // HEAD_WIDTH
    groups = lax.axis_size("groups")
    sects = lax.axis_size("sect")
    rows, width = queries.shape
    cols = width // sects
    w_rows = proj_weight.shape[0] // sects
    w_cols = proj_weight.shape[1]
    blocks = min(sects, -(-segments.shape[0] // (2 * rows)) + 1)
    kv_shape = (rows, 2 * keys.shape[1])
    aligned = w_cols % 128 == 0
    w_shape = (w_rows, w_cols * sects) if aligned else (sects, w_rows, w_cols)
    attended, weight = pl.pallas_call(
        functools.partial(attention_kernel, groups, sects, kv_heads),
        out_shape=(
            jax.ShapeDtypeStruct((rows * sects, cols), jnp.bfloat16),
            jax.ShapeDtypeStruct(w_shape, jnp.bfloat16),
        ),
        in_specs=[VMEM_SPEC, VMEM_SPEC, VMEM_SPEC, VMEM_SPEC, ANY_SPEC],
        out_specs=(ANY_SPEC, ANY_SPEC),
        scratch_shapes=attention_scratch(groups, sects, rows, cols, kv_shape, blocks * rows),
        compiler_params=pltpu.CompilerParams(collective_id=0, has_side_effects=True),
        name="attention",
    )(queries, keys, values, segments.reshape(sects, 1, rows), proj_weight)
    if not aligned:
        weight = weight.transpose(1, 0, 2).reshape(w_rows, w_cols * sects)
    return attended, weight

def positions():
    s = lax.axis_index("sect")
    c = lax.axis_index("head")
    halves = lax.axis_size("sect") // 2
    h = s // 2
    low = lax.rem(s, 2)
    partner = {"head": 1 - c}
    across = {"sect": 2 * h + 1 - low}
    others = [lax.rem(h + i, halves) for i in range(1, halves)]
    return s, c, h, low, halves, partner, across, others

def sum_kernel(
    p_ref, o_ref, rp, cs, ry, zs, rz, p_send, p_recv, y_send, y_recv, z_send, z_recv
):
    s, c, h, low, halves, partner, across, others = positions()
    greet([partner, across] + [{"sect": 2 * t + low} for t in others])
    order = others + [h]
    started = []

    def widen(x):
        return x.astype(jnp.float32)

    for t in order:
        copy = remote(
            p_ref.at[pl.ds(2 * t, 2), 1 - c], rp.at[t], p_send.at[t], p_recv.at[t], partner
        )
        copy.start()
        started.append(copy)
    for t in order:
        remote(
            p_ref.at[pl.ds(2 * t, 2), 1 - c], rp.at[t], p_send.at[t], p_recv.at[t], partner
        ).wait_recv()
        cs[t] = (widen(p_ref[2 * t + 1 - low, c]) + widen(rp[t, 1 - low])).astype(jnp.bfloat16)
        copy = remote(cs.at[t], ry.at[t], y_send.at[t], y_recv.at[t], across)
        copy.start()
        started.append(copy)
    for t in order:
        remote(cs.at[t], ry.at[t], y_send.at[t], y_recv.at[t], across).wait_recv()
        total = widen(p_ref[2 * t + low, c]) + widen(rp[t, low]) + widen(ry[t])
        if t is h:
            o_ref[...] = total
        else:
            zs[t] = total.astype(jnp.bfloat16)
            copy = remote(
                zs.at[t], rz.at[h], z_send.at[t], z_recv.at[h], {"sect": 2 * t + low}
            )
            copy.start()
            started.append(copy)
    for t in others:
        remote(
            zs.at[t], rz.at[t], z_send.at[t], z_recv.at[t], {"sect": 2 * t + low}
        ).wait_recv()
        o_ref[...] += widen(rz[t])
    for copy in started:
        copy.wait_send()

def sum_scatter(partial_rows, moe_rows, collective_id):
    sects = lax.axis_size("sect")
    heads = lax.axis_size("head")
    width = partial_rows.shape[1]
    halves = sects // 2
    block = (moe_rows, width)
    return pl.pallas_call(
        sum_kernel,
        out_shape=jax.ShapeDtypeStruct(block, jnp.float32),
        in_specs=[VMEM_SPEC],
        out_specs=VMEM_SPEC,
        scratch_shapes=[
            pltpu.VMEM((halves, 2) + block, jnp.bfloat16),
            pltpu.VMEM((halves,) + block, jnp.bfloat16),
            pltpu.VMEM((halves,) + block, jnp.bfloat16),
            pltpu.VMEM((halves,) + block, jnp.bfloat16),
            pltpu.VMEM((halves,) + block, jnp.bfloat16),
        ]
        + [DMA((halves,))] * 6,
        compiler_params=pltpu.CompilerParams(
            collective_id=collective_id, has_side_effects=True
        ),
        name="sum_scatter",
    )(partial_rows.reshape((sects, heads) + block))

def gather_kernel(
    x_ref, o_ref, p_send, p_recv, y_send, y_recv, z_send, z_recv, local_sem
):
    s, c, h, low, halves, partner, across, others = positions()
    greet([partner, across] + [{"sect": 2 * t + low} for t in others])
    started = []

    def send(src, row, send_sem, recv_sem, device):
        copy = remote(src, o_ref.at[row, c], send_sem, recv_sem, device)
        copy.start()
        started.append(copy)

    for t in others:
        send(x_ref, s, z_send.at[t], z_recv.at[h], {"sect": 2 * t + low})
    send(x_ref, s, y_send.at[h], y_recv.at[h], across)
    send(x_ref, s, p_send.at[s], p_recv.at[s], partner)
    own = pltpu.make_async_copy(x_ref, o_ref.at[s, c], local_sem)
    own.start()
    for t in others:
        row = 2 * t + low
        remote(x_ref, o_ref.at[row, c], z_send.at[t], z_recv.at[t], {"sect": row}).wait_recv()
        send(o_ref.at[row, c], row, y_send.at[t], y_recv.at[t], across)
        send(o_ref.at[row, c], row, p_send.at[row], p_recv.at[row], partner)
    for t in [h] + others:
        row = 2 * t + 1 - low
        remote(x_ref, o_ref.at[row, c], y_send.at[t], y_recv.at[t], across).wait_recv()
        send(o_ref.at[row, c], row, p_send.at[row], p_recv.at[row], partner)
    for t in [h] + others:
        for row in (2 * t + low, 2 * t + 1 - low):
            remote(
                x_ref, o_ref.at[row, 1 - c], p_send.at[row], p_recv.at[row], partner
            ).wait_recv()
    own.wait()
    for copy in started:
        copy.wait_send()

def gather_rows(x, collective_id):
    sects = lax.axis_size("sect")
    heads = lax.axis_size("head")
    halves = sects // 2
    out = pl.pallas_call(
        gather_kernel,
        out_shape=jax.ShapeDtypeStruct((sects, heads) + x.shape, x.dtype),
        in_specs=[VMEM_SPEC],
        out_specs=VMEM_SPEC,
        scratch_shapes=[
            DMA((sects,)),
            DMA((sects,)),
            DMA((halves,)),
            DMA((halves,)),
            DMA((halves,)),
            DMA((halves,)),
            DMA,
        ],
        compiler_params=pltpu.CompilerParams(
            collective_id=collective_id, has_side_effects=True
        ),
        name="gather_rows",
    )(x)
    return out.reshape(-1, x.shape[1])

def reducer(place, mine, sect_of, p_ref, acc, rp, cs, ry, zs, rz, sems):
    s, c, h, low, halves, partner, across, others = place
    p_send, p_recv, y_send, y_recv, z_send, z_recv = sems

    def widen(x):
        return x.astype(jnp.float32)

    def to_partner(t, q, cut):
        return remote(
            p_ref.at[pl.ds(2 * t, 2), 1 - c, :, cut],
            rp.at[t, :, :, cut],
            p_send.at[0],
            p_recv.at[q, t],
            partner,
        )

    def to_across(t, q, cut):
        return remote(
            cs.at[t, :, cut], ry.at[t, :, cut], y_send.at[0], y_recv.at[q, t], across
        )

    def enter(t, q, cut):
        to_partner(t, q, cut).start()

    def cross(t, q, cut):
        to_partner(t, q, cut).wait_recv()
        cs[t, :, cut] = (
            widen(p_ref[2 * t + 1 - low, c, :, cut]) + widen(rp[t, 1 - low, :, cut])
        ).astype(jnp.bfloat16)
        to_across(t, q, cut).start()

    def along(t, q, cut):
        to_across(t, q, cut).wait_recv()
        total = (
            widen(p_ref[2 * t + low, c, :, cut])
            + widen(rp[t, low, :, cut])
            + widen(ry[t, :, cut])
        )
        if t is mine:
            acc[:, cut] = total
        else:
            zs[t, :, cut] = total.astype(jnp.bfloat16)
            remote(
                zs.at[t, :, cut],
                rz.at[mine, :, cut],
                z_send.at[0],
                z_recv.at[q, mine],
                {"sect": sect_of(t)},
            ).start()

    def collect(t, q, cut):
        if t is mine:
            return
        remote(
            zs.at[t, :, cut],
            rz.at[t, :, cut],
            z_send.at[0],
            z_recv.at[q, t],
            {"sect": sect_of(t)},
        ).wait_recv()
        acc[:, cut] += widen(rz[t, :, cut])

    def drain():
        remote(
            p_ref.at[:, 1 - c], p_ref.at[:, c], p_send.at[0], p_recv.at[0, 0], partner
        ).wait_send()
        remote(cs, ry, y_send.at[0], y_recv.at[0, 0], across).wait_send()
        some = pl.ds(0, cs.shape[0] - 1)
        remote(zs.at[some], rz.at[some], z_send.at[0], z_recv.at[0, 0], across).wait_send()

    return enter, cross, along, collect, drain

def layer_kernel(
    groups,
    sects,
    kv_heads,
    q_hbm,
    k_hbm,
    v_hbm,
    seg_hbm,
    proj_ref,
    res_hbm,
    gain_hbm,
    ids_hbm,
    route_hbm,
    gate_hbm,
    up_hbm,
    down_hbm,
    out_ref,
    q_ref,
    seg_ref,
    res_ref,
    gain_ref,
    ids_ref,
    route_ref,
    in_sems,
    gate_ref,
    up_ref,
    down_ref,
    hidden,
    xg,
    acc,
    p_first,
    p_second,
    rp_first,
    rp_second,
    first_bufs,
    cross_bufs,
    x_sems,
    tx_sems,
    rx_first,
    rx_second,
    z_second,
    w_sems,
    a_ref,
    w_all,
    kv_ref,
    kv_all,
    att,
    bias,
    kz_send,
    kz_recv,
    ky_send,
    ky_recv,
    a_send,
    a_recv,
    w_send,
    w_recv,
    f_send,
    f_recv,
    local_sem,
    own_w_sem,
    own_a_sem,
):
    place = positions()
    s, c, h, low, halves, partner, across, others = place
    g = lax.axis_index("groups")
    experts = lax.axis_size("sect") * lax.axis_size("head")
    moe_rows, width = res_ref.shape
    rows = q_ref.shape[0]
    chunk = 4 * moe_rows
    team = sects // 2
    line = team // 2
    j = lax.rem(s, team)
    base = s - j
    line_at = lax.rem(h, line)
    line_others = [lax.rem(line_at + i, line) for i in range(1, line)]
    sect_peers = [lax.rem(s + i, sects) for i in range(1, sects)]
    group_peers = [lax.rem(g + i, groups) for i in range(1, groups)]

    def teammate(i):
        return base + lax.rem(j + team + i, team)

    def opposite(i):
        return team - base + lax.rem(j + team + i, team)

    half = k_hbm.shape[1]
    own_k = pltpu.make_async_copy(k_hbm, kv_ref.at[:, pl.ds(0, half)], local_sem.at[0])
    own_v = pltpu.make_async_copy(v_hbm, kv_ref.at[:, pl.ds(half, half)], local_sem.at[1])
    own_k.start()
    own_v.start()
    inputs = [
        pltpu.make_async_copy(src, dst, in_sems.at[i])
        for i, (src, dst) in enumerate(
            (
                (seg_hbm, seg_ref),
                (q_hbm, q_ref),
                (res_hbm, res_ref),
                (gain_hbm, gain_ref),
                (ids_hbm, ids_ref),
                (route_hbm, route_ref),
            )
        )
    ]
    for copy in inputs:
        copy.start()
    greet(
        [{"sect": t} for t in sect_peers] + [{"groups": t} for t in group_peers] + [partner]
    )
    started = []

    def send(copy):
        copy.start()
        started.append(copy)

    own_k.wait()
    own_v.wait()

    window = bias.shape[1]
    blocks = window // rows
    first = jnp.maximum(s - (blocks - 1), 0)
    reach = min(blocks // 2, halves - 1)

    def kv_up(i):
        return remote(
            kv_ref, kv_all.at[s], kz_send.at[i], kz_recv.at[i], {"sect": s + 2 * i}
        )

    def kv_over(i):
        row = s - 2 * i
        return remote(
            kv_ref if i == 0 else kv_all.at[row],
            kv_all.at[row],
            ky_send.at[i],
            ky_recv.at[i],
            across,
        )

    for i in range(1, reach + 1):
        pl.when(h + i < halves)(kv_up(i).start)
    kv_over(0).start()
    own_kv = pltpu.make_async_copy(kv_ref, kv_all.at[s], local_sem.at[2])
    own_kv.start()

    pieces, w_rows, w_width = w_all.shape
    part = w_rows // groups
    w_cols = w_width // sects

    def w_piece(t, q):
        start = pl.multiple_of(lax.rem(t, team) * w_rows + g * part, part)
        return proj_ref.at[pl.ds(start, part), pl.ds(q * w_cols, w_cols)]

    def w_place(group, t, q):
        return w_all.at[
            q,
            pl.ds(pl.multiple_of(group * part, part), part),
            pl.ds(pl.multiple_of(t * w_cols, w_cols), w_cols),
        ]

    def w_side(group):
        return w_all.at[:, pl.ds(pl.multiple_of(group * part, part), part), :]

    def drain_weight():
        for i, u in enumerate(group_peers):
            remote(
                w_side(g), w_side(u), f_send.at[i], f_recv.at[g, 0], {"groups": u}
            ).wait_send()
        span = pl.ds(0, (sects - 1) * w_cols)
        side = w_all.at[:, pl.ds(0, part), span]
        remote(side, side, w_send.at[0], w_recv.at[0, 0], across).wait_send()

    def own_w(q):
        return pltpu.make_async_copy(w_piece(s, q), w_place(g, s, q), own_w_sem.at[q])

    def start_own(q):
        for i, u in enumerate(group_peers):
            remote(
                w_piece(s, q), w_place(g, s, q), f_send.at[i], f_recv.at[g, q], {"groups": u}
            ).start()
        own_w(q).start()

    def start_weight(q, targets):
        for t in targets:
            remote(
                w_piece(t, q), w_place(g, s, q), w_send.at[0], w_recv.at[q, s], {"sect": t}
            ).start()

    inside = [teammate(i) for i in range(1, team)]
    outside = [opposite(i) for i in range(team)]
    mixed = [outside[0]]
    for i in range(1, team):
        mixed += [inside[i - 1], outside[i]]
    ends = [jnp.where(base > 0, i, halves - 1 - i) for i in range(line)]
    far = [2 * z + y for z in ends for y in (low, 1 - low)]
    w_sources = far[:1] + [teammate(-i) for i in range(1, team)] + far[1:]

    def forward_weight(q, t):
        remote(
            w_piece(t, q), w_place(g, t, q), w_send.at[0], w_recv.at[q, t], {"sect": t}
        ).wait_recv()
        for i, u in enumerate(group_peers):
            remote(
                w_place(g, t, q), w_place(g, t, q), f_send.at[i], f_recv.at[g, q], {"groups": u}
            ).start()

    def wait_weight(q):
        for u in group_peers:
            remote(
                w_side(g).at[q], w_side(u).at[q], f_send.at[0], f_recv.at[u, q], {"groups": u}
            ).wait_recv()
        own_w(q).wait()

    loads = [
        pltpu.make_async_copy(src.at[0], dst, w_sems.at[i])
        for i, (src, dst) in enumerate(
            ((gate_hbm, gate_ref), (up_hbm, up_ref), (down_hbm, down_ref))
        )
    ]
    for load in loads:
        load.start()

    for q in range(pieces):
        start_own(q)
    start_weight(0, inside)
    start_weight(0, outside)
    for copy in inputs:
        copy.wait()
    row_of = lax.broadcasted_iota(jnp.int32, (rows, rows), 0)
    col_of = lax.broadcasted_iota(jnp.int32, (rows, rows), 1)
    seg_q = jnp.sum(
        jnp.where(row_of == col_of, seg_ref[s].astype(jnp.float32), 0.0), axis=1, keepdims=True
    )
    for b in range(blocks):
        behind = (s - first - b) * rows + row_of - col_of
        same = seg_q == seg_ref[first + b].astype(jnp.float32)
        bias[:, b * rows : (b + 1) * rows] = jnp.where(
            jnp.logical_and(same, behind >= 0), 0.0, MASKED
        )

        @pl.when(first + b > 2 * h + 1)
        def _(b=b):
            kv_all[first + b] = jnp.zeros(kv_all.shape[1:], kv_all.dtype)

    def relay_kv(i):
        remote(
            kv_ref, kv_all.at[s - 2 * i], kz_send.at[i], kz_recv.at[i], across
        ).wait_recv()
        kv_over(i).start()

    for i in range(1, reach + 1):
        pl.when(h - i >= 0)(functools.partial(relay_kv, i))

    def wait_kv(i):
        row = 2 * (h - i) + 1 - low
        remote(kv_ref, kv_all.at[row], ky_send.at[i], ky_recv.at[i], across).wait_recv()

    near = [teammate(-i) for i in range(1, team)]
    waiting = [(q, t) for q in range(pieces) for t in near]
    waiting += [(q, t) for q in range(pieces) for t in far]
    for i in range(reach + 1):
        pl.when(h - i >= 0)(functools.partial(wait_kv, i))
    if pieces > 1:
        start_weight(1, inside)
        start_weight(1, outside)
    own_kv.wait()

    scale = 1.0 / math.sqrt(HEAD_WIDTH)
    kv_width = kv_heads * HEAD_WIDTH
    per_kv = q_ref.shape[1] // kv_heads
    per, step_cols = att.shape[1], att.shape[3]
    cols = per * step_cols

    def attend(i):
        t = lax.rem(j + 1 + i // per, team)
        u = lax.rem(i, per)
        at = t * cols + u * step_cols
        kv_head = at // per_kv
        k_col = pl.multiple_of(kv_head * HEAD_WIDTH, HEAD_WIDTH)
        v_col = pl.multiple_of(kv_width + kv_head * HEAD_WIDTH, HEAD_WIDTH)
        span = pl.ds(first, blocks)
        keys = kv_all[span, :, pl.ds(k_col, HEAD_WIDTH)].reshape(window, HEAD_WIDTH)
        vals = kv_all[span, :, pl.ds(v_col, HEAD_WIDTH)].reshape(window, HEAD_WIDTH)
        for k in range(step_cols // HEAD_WIDTH):
            q_col = pl.multiple_of(at + k * HEAD_WIDTH, HEAD_WIDTH)
            q = q_ref[:, pl.ds(q_col, HEAD_WIDTH)]
            scores = lax.dot_general(
                q, keys, (((1,), (1,)), ((), ())), preferred_element_type=jnp.float32
            )
            scores = scores * scale + bias[...]
            top = jnp.max(scores, axis=1, keepdims=True)
            weights = jnp.exp(scores - top).astype(jnp.bfloat16)
            total = jnp.sum(weights.astype(jnp.float32), axis=1, keepdims=True)
            mixed = jnp.dot(weights, vals, preferred_element_type=jnp.float32)
            att[t, u, :, k * HEAD_WIDTH : (k + 1) * HEAD_WIDTH] = (mixed / total).astype(
                jnp.bfloat16
            )

    def a_place(t, u):
        return a_ref.at[
            pl.ds(pl.multiple_of(t * rows, rows), rows),
            pl.ds(pl.multiple_of(u * step_cols, step_cols), step_cols),
        ]

    def a_copy(t, u):
        return remote(
            att.at[t, u], a_place(j, u), a_send.at[0], a_recv.at[j, u], {"sect": base + t}
        )

    def step(i, carry):
        attend(i)
        last = i - 1

        @pl.when(jnp.logical_and(last >= 0, last < (team - 1) * per))
        def _():
            a_copy(lax.rem(j + 1 + last // per, team), lax.rem(last, per)).start()

        return carry

    steps = team * per
    segments = 4 if steps % 4 == 0 else 1
    for i in range(segments):
        lax.fori_loop(i * steps // segments, (i + 1) * steps // segments, step, 0)
        if i + 1 < segments:
            for _ in range(2):
                forward_weight(*waiting.pop(0))
    own_a = [
        pltpu.make_async_copy(att.at[j, u], a_place(j, u), own_a_sem.at[u]) for u in range(per)
    ]
    for copy in own_a:
        copy.start()
    while len(waiting) > (pieces - 1) * len(far):
        forward_weight(*waiting.pop(0))

    for _ in range(min(2, len(waiting))):
        forward_weight(*waiting.pop(0))
    team_peers = [lax.rem(j + i, team) for i in range(1, team)]
    for t in team_peers:
        for u in range(per):
            remote(
                att.at[t, u], a_place(t, u), a_send.at[0], a_recv.at[t, u], across
            ).wait_recv()
    for copy in own_a:
        copy.wait()

    tile = 512
    subs = 2 if w_width % (2 * tile) == 0 else 1

    def project(t, q, cut):
        left = a_ref[pl.ds(pl.multiple_of(t * chunk, chunk), chunk), :]
        which = cut.start // w_width
        for n in range(cut.start, cut.stop, tile):
            at = n - which * w_width
            part = jnp.dot(
                left, w_all[which, :, at : at + tile], preferred_element_type=jnp.float32
            )
            p_first[pl.ds(2 * t, 2), :, :, n : n + tile] = part.astype(jnp.bfloat16).reshape(
                2, 2, moe_rows, tile
            )

    enter, cross, along, collect, drain_first = reducer(
        place,
        line_at,
        lambda t: base + 2 * t + low,
        p_first,
        acc,
        rp_first,
        *[first_bufs.at[k] for k in range(4)],
        [tx_sems.at[pl.ds(0, 1)], rx_first.at[0]]
        + [tx_sems.at[pl.ds(1, 1)], rx_first.at[1]]
        + [tx_sems.at[pl.ds(2, 1)], rx_first.at[2]],
    )
    span = w_width // subs
    def cuts(q):
        return [
            (t, q * subs + i, slice(q * w_width + i * span, q * w_width + (i + 1) * span))
            for i in range(subs)
            for t in line_others + [line_at]
        ]

    behind = []
    for q in range(pieces):
        items = cuts(q)
        wait_weight(q)
        for i, item in enumerate(items):
            project(*item)
            enter(*item)
            if i >= 1 and q + 1 < pieces:
                cross(*items[i - 1])
        if q + 1 < pieces:
            cross(*items[-1])
            while waiting:
                forward_weight(*waiting.pop(0))
            behind += items
            continue
        n = len(behind)
        for i, item in enumerate(items):
            cross(*item)
            for other in behind[i * n // len(items) : (i + 1) * n // len(items)]:
                along(*other)
        for item in items:
            along(*item)
        for item in behind + items:
            collect(*item)

    summed = jnp.concatenate(
        [
            acc[:, q * w_width + t * w_cols : q * w_width + (t + 1) * w_cols]
            for t in range(sects)
            for q in range(pieces)
        ],
        axis=1,
    )
    mid = (res_ref[...].astype(jnp.float32) + summed).astype(jnp.bfloat16)
    out_ref[0] = mid
    wide = mid.astype(jnp.float32)
    inverse = lax.rsqrt(jnp.mean(wide * wide, axis=1, keepdims=True) + NORM_EPS)
    normed = wide * inverse * gain_ref[...].astype(jnp.float32).reshape(1, width)
    lanes = xg.shape[3] - width
    lane = lax.broadcasted_iota(jnp.int32, (moe_rows, lanes), 1)
    place_of = lax.broadcasted_iota(jnp.int32, (lanes, moe_rows), 0)
    route = route_ref[...]
    route = route / jnp.sum(route, axis=0, keepdims=True)
    share = jnp.zeros((lanes, moe_rows), jnp.float32)
    for k in range(route.shape[0]):
        ids = ids_ref[k : k + 1, :]
        named = jnp.logical_or(place_of == ids, place_of == ids + experts)
        share = share + jnp.where(named, route[k : k + 1, :], 0.0)
    share = share.T
    high = share.astype(jnp.bfloat16).astype(jnp.float32)
    xg[s, c, :, width:] = jnp.where(lane < experts, high, share - high).astype(jnp.bfloat16)
    xg[s, c, :, :width] = normed.astype(jnp.bfloat16)

    pg_send, pg_recv, yg_send, yg_recv, zg_send, zg_recv = [x_sems.at[j] for j in range(6)]

    def send_rows(row, send_sem, recv_sem, device):
        send(remote(xg.at[row, c], xg.at[row, c], send_sem, recv_sem, device))

    def arrived(row, core, recv_sem):
        remote(xg.at[row, core], xg.at[row, core], pg_send.at[row], recv_sem, partner).wait_recv()

    guarded = []

    def send_if(when, copy):
        pl.when(when)(copy.start)
        guarded.append((when, copy))

    def pass_up(t, slot):
        row = 2 * t + low
        return remote(
            xg.at[row, c], xg.at[row, c], zg_send.at[slot], zg_recv.at[t], {"sect": s + 2}
        )

    def pass_down(t, slot):
        row = 2 * t + low
        return remote(
            xg.at[row, c], xg.at[row, c], zg_send.at[slot], zg_recv.at[t], {"sect": s - 2}
        )

    paired = jnp.minimum(h, halves - 1 - h)
    away = jnp.where(2 * h < halves - 1, 1, -1)
    order = [h]
    hops = [0]
    for k in range(1, halves):
        near = (k + 1) // 2 * (-1 if k % 2 else 1)
        order.append(h + away * jnp.where(k <= 2 * paired, near, k - paired))
        hops.append(jnp.where(k <= 2 * paired, (k + 1) // 2, k - paired))

    def onward(k):
        t = order[k]
        row = 2 * t + low
        block = xg.at[row, c]
        return [
            (jnp.logical_and(t < h, h + 1 < halves), pass_up(t, t)),
            (jnp.logical_and(t > h, h >= 1), pass_down(t, t)),
        ], [
            remote(block, block, yg_send.at[t], yg_recv.at[t], across),
            remote(block, block, pg_send.at[row], pg_recv.at[row], partner),
        ]

    def relay_rows(k):
        t = order[k]
        arrived(2 * t + low, c, zg_recv.at[t])
        maybe, always = onward(k)
        for when, copy in maybe:
            pl.when(when)(copy.start)
        for copy in always:
            copy.start()

    for k in range(1, halves):
        maybe, always = onward(k)
        guarded.extend(maybe)
        started.extend(always)

    def relay_step(i):
        for k in range(i + 1, halves):
            if (k + 1) // 2 <= i + 1:
                pl.when(hops[k] == i + 1)(functools.partial(relay_rows, k))

    send_if(h + 1 < halves, pass_up(h, h))
    send_if(h >= 1, pass_down(h, halves + h))
    send_rows(s, yg_send.at[h], yg_recv.at[h], across)
    send_rows(s, pg_send.at[s], pg_recv.at[s], partner)
    for load in loads:
        load.wait()

    def experts_of(i, t, q, cut):
        if q == 0:
            hidden_of(i, t)
        for n in range(cut.start, cut.stop, tile):
            part = jnp.dot(
                hidden[...], down_ref[:, n : n + tile], preferred_element_type=jnp.float32
            )
            p_second[pl.ds(2 * t, 2), :, :, n : n + tile] = (
                (part * own_share(t)).astype(jnp.bfloat16).reshape(2, 2, moe_rows, tile)
            )

    def own_share(t):
        pair = xg[pl.ds(2 * t, 2), :, :, width:].astype(jnp.float32).reshape(chunk, lanes)
        expert = s * 2 + c
        at = lax.broadcasted_iota(jnp.int32, (chunk, lanes), 1)
        mine = jnp.logical_or(at == expert, at == expert + experts)
        return jnp.sum(jnp.where(mine, pair, 0.0), axis=1, keepdims=True)

    def hidden_of(i, t):
        relay_step(i)
        row = 2 * t + 1 - low
        arrived(row, c, yg_recv.at[t])
        send_rows(row, pg_send.at[row], pg_recv.at[row], partner)
        for row in (2 * t + low, 2 * t + 1 - low):
            arrived(row, 1 - c, pg_recv.at[row])
        x = xg[pl.ds(2 * t, 2), :, :, :width].reshape(chunk, width)
        step = 256
        for n in range(0, hidden.shape[1], step):
            gate_act = jnp.dot(
                x, gate_ref[:, n : n + step], preferred_element_type=jnp.float32
            )
            up_act = jnp.dot(x, up_ref[:, n : n + step], preferred_element_type=jnp.float32)
            silu = gate_act / (1.0 + jnp.exp(-gate_act))
            hidden[:, n : n + step] = (silu * up_act).astype(jnp.bfloat16)

    cs, ry, zs = [cross_bufs.at[k, pl.ds(0, halves)] for k in range(3)]
    rz = cross_bufs.at[3]
    y_send, y_recv = tx_sems.at[pl.ds(4, 1)], rx_second.at[1]
    z_send, z_recv = tx_sems.at[pl.ds(5, 1)], z_second
    sems = [tx_sems.at[pl.ds(3, 1)], rx_second.at[0], y_send, y_recv, z_send, z_recv]
    enter, cross, _, _, drain_second = reducer(
        place, h, None, p_second, acc, rp_second, cs, ry, zs, rz, sems
    )
    parts = 2 if width % 1024 == 0 else 1
    size = width // parts
    cuts_of = [(q, slice(q * size, (q + 1) * size)) for q in range(parts)]

    def own_sum(t, q, cut):
        return (
            p_second[2 * t + low, c, :, cut].astype(jnp.float32)
            + rp_second[t, low, :, cut].astype(jnp.float32)
            + ry[t, :, cut].astype(jnp.float32)
        )

    def wait_across(t, q, cut):
        remote(
            cs.at[t, :, cut], ry.at[t, :, cut], y_send.at[0], y_recv.at[q, t], across
        ).wait_recv()

    def wait_along(slot, row, t, q, cut):
        remote(
            zs.at[t, :, cut], rz.at[slot, :, cut], z_send.at[0], z_recv.at[row, t], across
        ).wait_recv()

    def chain(t, q, cut):
        wait_across(t, q, cut)
        joined = jnp.where(t > h, h >= 1, h + 1 < halves)

        @pl.when(jnp.logical_not(joined))
        def _():
            zs[t, :, cut] = own_sum(t, q, cut).astype(jnp.bfloat16)

        @pl.when(joined)
        def _():
            wait_along(t, q, t, q, cut)
            zs[t, :, cut] = (
                own_sum(t, q, cut) + rz[t, :, cut].astype(jnp.float32)
            ).astype(jnp.bfloat16)

        landed = h - 1 == t
        remote(
            zs.at[t, :, cut],
            rz.at[jnp.where(landed, halves, t), :, cut],
            z_send.at[0],
            z_recv.at[q + jnp.where(landed, parts, 0), t],
            {"sect": s + jnp.where(t > h, 2, -2)},
        ).start()

    def finish(q, cut):
        wait_across(h, q, cut)
        acc[:, cut] = own_sum(h, q, cut)

        @pl.when(h >= 1)
        def _():
            wait_along(h, q, h, q, cut)
            acc[:, cut] += rz[h, :, cut].astype(jnp.float32)

        @pl.when(h + 1 < halves)
        def _():
            wait_along(halves, q + parts, h, q, cut)
            acc[:, cut] += rz[halves, :, cut].astype(jnp.float32)

    lower = h < halves // 2
    targets = [
        jnp.where(lower, halves // 2 + i, halves // 2 - 1 - i) for i in range(halves // 2)
    ]
    targets += [h - line_at + t for t in line_others]

    def each(step, t):
        for q, cut in cuts_of:
            step(t, q, cut)

    for i, t in enumerate(order):
        for q, cut in cuts_of:
            experts_of(i, t, q, cut)
            enter(t, q, cut)
        if i == halves - 2:
            each(cross, targets[0])
    for i, t in enumerate(targets[1:] + [h]):
        each(cross, t)
        if i < 0:
            each(chain, targets[i])
    for t in targets[0:]:
        each(chain, t)
    for q, cut in cuts_of:
        finish(q, cut)
    out_ref[1] = acc[...].astype(jnp.bfloat16)
    for i in range(1, reach + 1):
        pl.when(h + i < halves)(kv_up(i).wait_send)
    for i in range(reach + 1):
        pl.when(h - i >= 0)(kv_over(i).wait_send)
    some = pl.ds(0, team - 1)
    remote(att.at[some], att.at[some], a_send.at[0], a_recv.at[0, 0], across).wait_send()
    drain_weight()
    drain_first()
    drain_second()
    for when, copy in guarded:
        pl.when(when)(copy.wait_send)
    for copy in started:
        copy.wait_send()

def fused_layer(
    queries, keys, values, segments, proj, residual, gain, ids, route, gate, up, down
):
    groups = lax.axis_size("groups")
    sects = lax.axis_size("sect")
    heads = lax.axis_size("head")
    rows = queries.shape[0]
    team = sects // 2
    cols = queries.shape[1] // team
    step_cols = min(cols, 4 * HEAD_WIDTH)
    per = cols // step_cols
    pieces = 2 if proj.shape[1] % 256 == 0 else 1
    w_rows = proj.shape[0] // team
    blocks = min(sects, -(-segments.shape[0] // (2 * rows)) + 1)
    halves = sects // 2
    block = residual.shape
    lanes = -(-2 * sects * heads // 128) * 128
    bf16 = jnp.bfloat16
    kv_shape = (rows, 2 * keys.shape[1])
    operands = (
        queries,
        keys,
        values,
        segments.reshape(sects, 1, rows),
        proj,
        residual,
        gain,
        ids.T,
        route.T,
        gate,
        up,
        down,
    )
    both = pl.pallas_call(
        functools.partial(layer_kernel, groups, sects, keys.shape[1] // HEAD_WIDTH),
        out_shape=jax.ShapeDtypeStruct((2,) + block, bf16),
        in_specs=[pl.BlockSpec(memory_space=pltpu.HBM)] * len(operands),
        out_specs=VMEM_SPEC,
        scratch_shapes=[
            pltpu.VMEM(queries.shape, bf16),
            pltpu.VMEM((sects, 1, rows), jnp.int32),
            pltpu.VMEM(block, bf16),
            pltpu.VMEM(gain.shape, bf16),
            pltpu.VMEM(ids.shape[::-1], jnp.int32),
            pltpu.VMEM(route.shape[::-1], jnp.float32),
            DMA((6,)),
            pltpu.VMEM(gate.shape[1:], bf16),
            pltpu.VMEM(up.shape[1:], bf16),
            pltpu.VMEM(down.shape[1:], bf16),
            pltpu.VMEM((4 * block[0], gate.shape[2]), bf16),
            pltpu.VMEM((sects, heads, block[0], block[1] + lanes), bf16),
            pltpu.VMEM(block, jnp.float32),
            pltpu.VMEM((team, heads) + block, bf16),
            pltpu.VMEM((sects, heads) + block, bf16),
            pltpu.VMEM((team // 2, 2) + block, bf16),
            pltpu.VMEM((halves, 2) + block, bf16),
            pltpu.VMEM((4, team // 2) + block, bf16),
            pltpu.VMEM((4, halves + 1) + block, bf16),
            DMA((6, sects)),
            DMA((6,)),
            DMA((3, 2 * pieces, team // 2)),
            DMA((2, 2, halves)),
            DMA((4, halves)),
            DMA((3,)),
            pltpu.VMEM((rows * team, cols), bf16),
            pltpu.VMEM((pieces, w_rows, proj.shape[1] // pieces * sects), bf16),
            pltpu.VMEM(kv_shape, bf16),
            pltpu.VMEM((sects,) + kv_shape, bf16),
            pltpu.VMEM((team, per, rows, step_cols), bf16),
            pltpu.VMEM((rows, blocks * rows), jnp.float32),
            DMA((halves,)),
            DMA((halves,)),
            DMA((halves,)),
            DMA((halves,)),
            DMA((1,)),
            DMA((team, per)),
            DMA((1,)),
            DMA((pieces, sects)),
            DMA((groups,)),
            DMA((groups, pieces)),
            DMA((3,)),
            DMA((pieces,)),
            DMA((per,)),
        ],
        compiler_params=pltpu.CompilerParams(
            collective_id=4, has_side_effects=True, vmem_limit_bytes=LAYER_ROOM
        ),
        name="layer",
    )(*[pltpu.with_memory_space_constraint(x, pltpu.HBM) for x in operands])
    return both[0], both[1]

def shards(
    queries,
    packed_key_rows,
    values,
    segments,
    proj_weight,
    residual,
    norm_gain,
    expert_ids,
    route_weights,
    gate_weight,
    up_weight,
    down_weight,
):
    sects = lax.axis_size("sect")
    heads = lax.axis_size("head")
    s = lax.axis_index("sect")
    c = lax.axis_index("head")
    experts = sects * heads
    moe_rows, width = residual.shape
    fits = experts * moe_rows * width * 24 <= VMEM_ROOM
    if fits and sects % 4 == 0 and proj_weight.shape[1] % 128 == 0:
        return fused_layer(
            queries,
            packed_key_rows,
            values,
            segments,
            proj_weight,
            residual,
            norm_gain,
            expert_ids,
            route_weights,
            gate_weight,
            up_weight,
            down_weight,
        )
    attended, weight = exchange_attention(
        queries, packed_key_rows, values, segments, proj_weight
    )
    partial_rows = jnp.dot(attended, weight, preferred_element_type=jnp.float32)
    projected = sum_scatter(partial_rows.astype(jnp.bfloat16), moe_rows, 1)

    hidden_mid = (residual.astype(jnp.float32) + projected).astype(jnp.bfloat16)
    mid_float = lax.optimization_barrier(hidden_mid).astype(jnp.float32)
    inverse = lax.rsqrt(jnp.mean(mid_float * mid_float, axis=1, keepdims=True) + NORM_EPS)
    normed = (mid_float * inverse * norm_gain.astype(jnp.float32)[None, :]).astype(jnp.bfloat16)

    route_share = route_weights / jnp.sum(route_weights, axis=1, keepdims=True)
    named = expert_ids[:, :, None] == jnp.arange(experts, dtype=jnp.int32)[None, None, :]
    share = jnp.sum(jnp.where(named, route_share[:, :, None], 0.0), axis=1)
    share_high = lax.reduce_precision(share, 8, 7)
    share_low = (share - share_high).astype(jnp.bfloat16)
    pad = -(2 * experts) % 128
    sent = jnp.concatenate(
        [
            normed,
            share_high.astype(jnp.bfloat16),
            share_low,
            jnp.zeros((moe_rows, pad), jnp.bfloat16),
        ],
        axis=1,
    )
    gathered = gather_rows(sent, 2)
    expert = s * heads + c
    all_rows = gathered[:, :width]
    pair = gathered[:, width:].astype(jnp.float32)
    lane = jnp.arange(pair.shape[1], dtype=jnp.int32)[None, :]
    mine = jnp.logical_or(lane == expert, lane == expert + experts)
    own_share = jnp.sum(jnp.where(mine, pair, 0.0), axis=1, keepdims=True)
    gate_act = jnp.dot(all_rows, gate_weight[0], preferred_element_type=jnp.float32)
    up_act = jnp.dot(all_rows, up_weight[0], preferred_element_type=jnp.float32)
    hidden = (jax.nn.silu(gate_act) * up_act).astype(jnp.bfloat16)
    result = jnp.dot(hidden, down_weight[0], preferred_element_type=jnp.float32)
    mixed = (result * own_share).astype(jnp.bfloat16)
    mixture = sum_scatter(mixed, moe_rows, 3)
    return (hidden_mid, mixture.astype(jnp.bfloat16))

def solution(mesh):
    rows = P(("groups", "sect", "head"), None)
    split = P(("groups", "sect"), "head")
    expert = P(("sect", "head"), None, None)
    placed = (
        split,
        split,
        split,
        P("groups"),
        P("head", "sect"),
        rows,
        P(),
        rows,
        rows,
        expert,
        expert,
        expert,
    )
    return jax.shard_map(
        shards, mesh=mesh, in_specs=placed, out_specs=(rows, rows), check_vma=False
    )
```

```python
import functools
import math

import jax
import jax.numpy as jnp
from jax import lax
from jax.experimental import pallas as pl
from jax.experimental.pallas import tpu as pltpu
from jax.sharding import PartitionSpec as P

HEAD_WIDTH = 128
MASKED = -1e30
NORM_EPS = 1e-06
VMEM_ROOM = 64 << 20
LAYER_ROOM = 52 << 20

MESH = pl.DeviceIdType.MESH
VMEM_SPEC = pl.BlockSpec(memory_space=pltpu.VMEM)
ANY_SPEC = pl.BlockSpec(memory_space=pl.ANY)
DMA = pltpu.SemaphoreType.DMA

def greet(devices):
    barrier = pltpu.get_barrier_semaphore()
    for device in devices:
        pl.semaphore_signal(barrier, inc=1, device_id=device, device_id_type=MESH)
    pl.semaphore_wait(barrier, len(devices))

def remote(src, dst, send_sem, recv_sem, device):
    return pltpu.make_async_remote_copy(
        src_ref=src,
        dst_ref=dst,
        send_sem=send_sem,
        recv_sem=recv_sem,
        device_id=device,
        device_id_type=MESH,
    )

def attention_body(
    extra,
    groups,
    sects,
    kv_heads,
    q_ref,
    k_ref,
    v_ref,
    seg_ref,
    w_ref,
    a_out,
    w_out,
    kv_ref,
    kv_all,
    att,
    bias,
    kz_send,
    kz_recv,
    ky_send,
    ky_recv,
    a_send,
    a_recv,
    w_send,
    w_recv,
    f_send,
    f_recv,
    local_sem,
):
    g = lax.axis_index("groups")
    s = lax.axis_index("sect")
    halves = sects // 2
    h = s // 2
    low = lax.rem(s, 2)
    rows = q_ref.shape[0]
    cols = q_ref.shape[1] // sects
    w_cols = w_ref.shape[1]
    w_rows = w_ref.shape[0] // sects
    part = w_rows // groups
    other_y = 2 * h + 1 - low
    sect_peers = [lax.rem(s + i, sects) for i in range(1, sects)]
    group_peers = [lax.rem(g + i, groups) for i in range(1, groups)]
    half = k_ref.shape[1]
    own_k = pltpu.make_async_copy(k_ref, kv_ref.at[:, pl.ds(0, half)], local_sem.at[3])
    own_v = pltpu.make_async_copy(v_ref, kv_ref.at[:, pl.ds(half, half)], local_sem.at[4])
    own_k.start()
    own_v.start()
    greet(
        [{"sect": t} for t in sect_peers] + [{"groups": t} for t in group_peers] + extra
    )
    started = []
    own_k.wait()
    own_v.wait()

    def kv_cross(t):
        return remote(
            kv_ref if t is None else kv_all.at[2 * t + low],
            kv_all.at[s if t is None else 2 * t + low],
            ky_send.at[h if t is None else t],
            ky_recv.at[h if t is None else t],
            {"sect": other_y},
        )

    for i in range(1, halves):
        t = lax.rem(h + i, halves)
        copy = remote(
            kv_ref, kv_all.at[s], kz_send.at[t], kz_recv.at[h], {"sect": 2 * t + low}
        )
        copy.start()
        started.append(copy)
    copy = kv_cross(None)
    copy.start()
    started.append(copy)
    own_kv = pltpu.make_async_copy(kv_ref, kv_all.at[s], local_sem.at[0])
    own_kv.start()

    def w_piece(t):
        return w_ref.at[pl.ds(pl.multiple_of(t * w_rows + g * part, part), part), :]

    def w_place(group, t):
        span = pl.ds(pl.multiple_of(group * part, part), part)
        if len(w_out.shape) == 3:
            return w_out.at[t, span, :]
        return w_out.at[span, pl.ds(pl.multiple_of(t * w_cols, w_cols), w_cols)]

    for t in sect_peers:
        copy = remote(
            w_piece(t), w_place(g, s), w_send.at[t], w_recv.at[s], {"sect": t}
        )
        copy.start()
        started.append(copy)
    own_w = pltpu.make_async_copy(w_piece(s), w_place(g, s), local_sem.at[1])
    own_w.start()
    for i, t in enumerate(group_peers):
        copy = remote(
            w_piece(s), w_place(g, s), f_send.at[i, s], f_recv.at[g, s], {"groups": t}
        )
        copy.start()
        started.append(copy)

    for i in range(1, halves):
        t = lax.rem(h + i, halves)
        remote(
            kv_ref, kv_all.at[2 * t + low], kz_send.at[t], kz_recv.at[t], {"sect": 2 * t + low}
        ).wait_recv()
        copy = kv_cross(t)
        copy.start()
        started.append(copy)

    window = bias.shape[1]
    blocks = window // rows
    first = jnp.maximum(s - (blocks - 1), 0)
    row_of = lax.broadcasted_iota(jnp.int32, (rows, rows), 0)
    col_of = lax.broadcasted_iota(jnp.int32, (rows, rows), 1)
    seg_q = jnp.sum(
        jnp.where(row_of == col_of, seg_ref[s].astype(jnp.float32), 0.0), axis=1, keepdims=True
    )
    for b in range(blocks):
        behind = (s - first - b) * rows + row_of - col_of
        same = seg_q == seg_ref[first + b].astype(jnp.float32)
        bias[:, b * rows : (b + 1) * rows] = jnp.where(
            jnp.logical_and(same, behind >= 0), 0.0, MASKED
        )

    for i in range(halves):
        t = lax.rem(h + i, halves)
        remote(
            kv_ref, kv_all.at[2 * t + 1 - low], ky_send.at[t], ky_recv.at[t], {"sect": other_y}
        ).wait_recv()
    own_kv.wait()

    scale = 1.0 / math.sqrt(HEAD_WIDTH)
    kv_width = kv_heads * HEAD_WIDTH
    per_kv = q_ref.shape[1] // kv_heads

    def attend(i, carry):
        t = lax.rem(s + 1 + i, sects)
        kv_head = (t * cols) // per_kv
        k_col = pl.multiple_of(kv_head * HEAD_WIDTH, HEAD_WIDTH)
        v_col = pl.multiple_of(kv_width + kv_head * HEAD_WIDTH, HEAD_WIDTH)
        span = pl.ds(first, blocks)
        keys = kv_all[span, :, pl.ds(k_col, HEAD_WIDTH)].reshape(window, HEAD_WIDTH)
        vals = kv_all[span, :, pl.ds(v_col, HEAD_WIDTH)].reshape(window, HEAD_WIDTH)
        for j in range(cols // HEAD_WIDTH):
            q_col = pl.multiple_of(t * cols + j * HEAD_WIDTH, HEAD_WIDTH)
            q = q_ref[:, pl.ds(q_col, HEAD_WIDTH)]
            scores = lax.dot_general(
                q, keys, (((1,), (1,)), ((), ())), preferred_element_type=jnp.float32
            )
            scores = scores * scale + bias[...]
            top = jnp.max(scores, axis=1, keepdims=True)
            weights = jnp.exp(scores - top).astype(jnp.bfloat16)
            total = jnp.sum(weights.astype(jnp.float32), axis=1, keepdims=True)
            mixed = jnp.dot(weights, vals, preferred_element_type=jnp.float32)
            att[t, :, j * HEAD_WIDTH : (j + 1) * HEAD_WIDTH] = (mixed / total).astype(
                jnp.bfloat16
            )
        return carry

    def a_place(t):
        return a_out.at[pl.ds(pl.multiple_of(t * rows, rows), rows), :]

    def a_copy(t):
        return remote(att.at[t], a_place(s), a_send.at[t], a_recv.at[s], {"sect": t})

    def step(i, carry):
        attend(i, carry)

        @pl.when(i >= 1)
        def _():
            a_copy(lax.rem(s + i, sects)).start()

        return carry

    lax.fori_loop(0, sects, step, 0)
    own_a = pltpu.make_async_copy(att.at[s], a_place(s), local_sem.at[2])
    own_a.start()

    for t in sect_peers:
        remote(
            w_piece(s), w_place(g, t), w_send.at[t], w_recv.at[t], {"sect": t}
        ).wait_recv()
        for i, u in enumerate(group_peers):
            copy = remote(
                w_place(g, t), w_place(g, t), f_send.at[i, t], f_recv.at[g, t], {"groups": u}
            )
            copy.start()
            started.append(copy)

    def wait_rows(t):
        remote(att.at[t], a_place(t), a_send.at[t], a_recv.at[t], {"sect": t}).wait_recv()

    def wait_weight():
        for u in group_peers:
            for t in [s] + sect_peers:
                remote(
                    w_place(g, t),
                    w_place(u, t),
                    f_send.at[0, t],
                    f_recv.at[u, t],
                    {"groups": u},
                ).wait_recv()
        own_w.wait()

    def drain():
        for copy in started:
            copy.wait_send()
        for t in sect_peers:
            a_copy(t).wait_send()

    return sect_peers, wait_rows, wait_weight, own_a.wait, drain

def attention_kernel(*arguments):
    sect_peers, wait_rows, wait_weight, wait_own, drain = attention_body([], *arguments)
    for t in sect_peers:
        wait_rows(t)
    wait_weight()
    wait_own()
    drain()

def attention_scratch(groups, sects, rows, cols, kv_shape, window):
    return [
        pltpu.VMEM(kv_shape, jnp.bfloat16),
        pltpu.VMEM((sects,) + kv_shape, jnp.bfloat16),
        pltpu.VMEM((sects, rows, cols), jnp.bfloat16),
        pltpu.VMEM((rows, window), jnp.float32),
        DMA((sects // 2,)),
        DMA((sects // 2,)),
        DMA((sects // 2,)),
        DMA((sects // 2,)),
        DMA((sects,)),
        DMA((sects,)),
        DMA((sects,)),
        DMA((sects,)),
        DMA((groups, sects)),
        DMA((groups, sects)),
        DMA((5,)),
    ]

def exchange_attention(queries, keys, values, segments, proj_weight):
    kv_heads = keys.shape[1] // HEAD_WIDTH
    groups = lax.axis_size("groups")
    sects = lax.axis_size("sect")
    rows, width = queries.shape
    cols = width // sects
    w_rows = proj_weight.shape[0] // sects
    w_cols = proj_weight.shape[1]
    blocks = min(sects, -(-segments.shape[0] // (2 * rows)) + 1)
    kv_shape = (rows, 2 * keys.shape[1])
    aligned = w_cols % 128 == 0
    w_shape = (w_rows, w_cols * sects) if aligned else (sects, w_rows, w_cols)
    attended, weight = pl.pallas_call(
        functools.partial(attention_kernel, groups, sects, kv_heads),
        out_shape=(
            jax.ShapeDtypeStruct((rows * sects, cols), jnp.bfloat16),
            jax.ShapeDtypeStruct(w_shape, jnp.bfloat16),
        ),
        in_specs=[VMEM_SPEC, VMEM_SPEC, VMEM_SPEC, VMEM_SPEC, ANY_SPEC],
        out_specs=(ANY_SPEC, ANY_SPEC),
        scratch_shapes=attention_scratch(groups, sects, rows, cols, kv_shape, blocks * rows),
        compiler_params=pltpu.CompilerParams(collective_id=0, has_side_effects=True),
        name="attention",
    )(queries, keys, values, segments.reshape(sects, 1, rows), proj_weight)
    if not aligned:
        weight = weight.transpose(1, 0, 2).reshape(w_rows, w_cols * sects)
    return attended, weight

def positions():
    s = lax.axis_index("sect")
    c = lax.axis_index("head")
    halves = lax.axis_size("sect") // 2
    h = s // 2
    low = lax.rem(s, 2)
    partner = {"head": 1 - c}
    across = {"sect": 2 * h + 1 - low}
    others = [lax.rem(h + i, halves) for i in range(1, halves)]
    return s, c, h, low, halves, partner, across, others

def sum_kernel(
    p_ref, o_ref, rp, cs, ry, zs, rz, p_send, p_recv, y_send, y_recv, z_send, z_recv
):
    s, c, h, low, halves, partner, across, others = positions()
    greet([partner, across] + [{"sect": 2 * t + low} for t in others])
    order = others + [h]
    started = []

    def widen(x):
        return x.astype(jnp.float32)

    for t in order:
        copy = remote(
            p_ref.at[pl.ds(2 * t, 2), 1 - c], rp.at[t], p_send.at[t], p_recv.at[t], partner
        )
        copy.start()
        started.append(copy)
    for t in order:
        remote(
            p_ref.at[pl.ds(2 * t, 2), 1 - c], rp.at[t], p_send.at[t], p_recv.at[t], partner
        ).wait_recv()
        cs[t] = (widen(p_ref[2 * t + 1 - low, c]) + widen(rp[t, 1 - low])).astype(jnp.bfloat16)
        copy = remote(cs.at[t], ry.at[t], y_send.at[t], y_recv.at[t], across)
        copy.start()
        started.append(copy)
    for t in order:
        remote(cs.at[t], ry.at[t], y_send.at[t], y_recv.at[t], across).wait_recv()
        total = widen(p_ref[2 * t + low, c]) + widen(rp[t, low]) + widen(ry[t])
        if t is h:
            o_ref[...] = total
        else:
            zs[t] = total.astype(jnp.bfloat16)
            copy = remote(
                zs.at[t], rz.at[h], z_send.at[t], z_recv.at[h], {"sect": 2 * t + low}
            )
            copy.start()
            started.append(copy)
    for t in others:
        remote(
            zs.at[t], rz.at[t], z_send.at[t], z_recv.at[t], {"sect": 2 * t + low}
        ).wait_recv()
        o_ref[...] += widen(rz[t])
    for copy in started:
        copy.wait_send()

def sum_scatter(partial_rows, moe_rows, collective_id):
    sects = lax.axis_size("sect")
    heads = lax.axis_size("head")
    width = partial_rows.shape[1]
    halves = sects // 2
    block = (moe_rows, width)
    return pl.pallas_call(
        sum_kernel,
        out_shape=jax.ShapeDtypeStruct(block, jnp.float32),
        in_specs=[VMEM_SPEC],
        out_specs=VMEM_SPEC,
        scratch_shapes=[
            pltpu.VMEM((halves, 2) + block, jnp.bfloat16),
            pltpu.VMEM((halves,) + block, jnp.bfloat16),
            pltpu.VMEM((halves,) + block, jnp.bfloat16),
            pltpu.VMEM((halves,) + block, jnp.bfloat16),
            pltpu.VMEM((halves,) + block, jnp.bfloat16),
        ]
        + [DMA((halves,))] * 6,
        compiler_params=pltpu.CompilerParams(
            collective_id=collective_id, has_side_effects=True
        ),
        name="sum_scatter",
    )(partial_rows.reshape((sects, heads) + block))

def gather_kernel(
    x_ref, o_ref, p_send, p_recv, y_send, y_recv, z_send, z_recv, local_sem
):
    s, c, h, low, halves, partner, across, others = positions()
    greet([partner, across] + [{"sect": 2 * t + low} for t in others])
    started = []

    def send(src, row, send_sem, recv_sem, device):
        copy = remote(src, o_ref.at[row, c], send_sem, recv_sem, device)
        copy.start()
        started.append(copy)

    for t in others:
        send(x_ref, s, z_send.at[t], z_recv.at[h], {"sect": 2 * t + low})
    send(x_ref, s, y_send.at[h], y_recv.at[h], across)
    send(x_ref, s, p_send.at[s], p_recv.at[s], partner)
    own = pltpu.make_async_copy(x_ref, o_ref.at[s, c], local_sem)
    own.start()
    for t in others:
        row = 2 * t + low
        remote(x_ref, o_ref.at[row, c], z_send.at[t], z_recv.at[t], {"sect": row}).wait_recv()
        send(o_ref.at[row, c], row, y_send.at[t], y_recv.at[t], across)
        send(o_ref.at[row, c], row, p_send.at[row], p_recv.at[row], partner)
    for t in [h] + others:
        row = 2 * t + 1 - low
        remote(x_ref, o_ref.at[row, c], y_send.at[t], y_recv.at[t], across).wait_recv()
        send(o_ref.at[row, c], row, p_send.at[row], p_recv.at[row], partner)
    for t in [h] + others:
        for row in (2 * t + low, 2 * t + 1 - low):
            remote(
                x_ref, o_ref.at[row, 1 - c], p_send.at[row], p_recv.at[row], partner
            ).wait_recv()
    own.wait()
    for copy in started:
        copy.wait_send()

def gather_rows(x, collective_id):
    sects = lax.axis_size("sect")
    heads = lax.axis_size("head")
    halves = sects // 2
    out = pl.pallas_call(
        gather_kernel,
        out_shape=jax.ShapeDtypeStruct((sects, heads) + x.shape, x.dtype),
        in_specs=[VMEM_SPEC],
        out_specs=VMEM_SPEC,
        scratch_shapes=[
            DMA((sects,)),
            DMA((sects,)),
            DMA((halves,)),
            DMA((halves,)),
            DMA((halves,)),
            DMA((halves,)),
            DMA,
        ],
        compiler_params=pltpu.CompilerParams(
            collective_id=collective_id, has_side_effects=True
        ),
        name="gather_rows",
    )(x)
    return out.reshape(-1, x.shape[1])

def reducer(place, mine, sect_of, p_ref, acc, rp, cs, ry, zs, rz, sems):
    s, c, h, low, halves, partner, across, others = place
    p_send, p_recv, y_send, y_recv, z_send, z_recv = sems

    def widen(x):
        return x.astype(jnp.float32)

    def to_partner(t, q, cut):
        return remote(
            p_ref.at[pl.ds(2 * t, 2), 1 - c, :, cut],
            rp.at[t, :, :, cut],
            p_send.at[0],
            p_recv.at[q, t],
            partner,
        )

    def to_across(t, q, cut):
        return remote(
            cs.at[t, :, cut], ry.at[t, :, cut], y_send.at[0], y_recv.at[q, t], across
        )

    def enter(t, q, cut):
        to_partner(t, q, cut).start()

    def cross(t, q, cut):
        to_partner(t, q, cut).wait_recv()
        cs[t, :, cut] = (
            widen(p_ref[2 * t + 1 - low, c, :, cut]) + widen(rp[t, 1 - low, :, cut])
        ).astype(jnp.bfloat16)
        to_across(t, q, cut).start()

    def along(t, q, cut):
        to_across(t, q, cut).wait_recv()
        total = (
            widen(p_ref[2 * t + low, c, :, cut])
            + widen(rp[t, low, :, cut])
            + widen(ry[t, :, cut])
        )
        if t is mine:
            acc[:, cut] = total
        else:
            zs[t, :, cut] = total.astype(jnp.bfloat16)
            remote(
                zs.at[t, :, cut],
                rz.at[mine, :, cut],
                z_send.at[0],
                z_recv.at[q, mine],
                {"sect": sect_of(t)},
            ).start()

    def collect(t, q, cut):
        if t is mine:
            return
        remote(
            zs.at[t, :, cut],
            rz.at[t, :, cut],
            z_send.at[0],
            z_recv.at[q, t],
            {"sect": sect_of(t)},
        ).wait_recv()
        acc[:, cut] += widen(rz[t, :, cut])

    def drain():
        remote(
            p_ref.at[:, 1 - c], p_ref.at[:, c], p_send.at[0], p_recv.at[0, 0], partner
        ).wait_send()
        remote(cs, ry, y_send.at[0], y_recv.at[0, 0], across).wait_send()
        some = pl.ds(0, cs.shape[0] - 1)
        remote(zs.at[some], rz.at[some], z_send.at[0], z_recv.at[0, 0], across).wait_send()

    return enter, cross, along, collect, drain

def layer_kernel(
    groups,
    sects,
    kv_heads,
    q_hbm,
    k_hbm,
    v_hbm,
    seg_hbm,
    proj_ref,
    res_hbm,
    gain_hbm,
    ids_hbm,
    route_hbm,
    gate_hbm,
    up_hbm,
    down_hbm,
    out_ref,
    q_ref,
    seg_ref,
    res_ref,
    gain_ref,
    ids_ref,
    route_ref,
    in_sems,
    gate_ref,
    up_ref,
    down_ref,
    hidden,
    xg,
    acc,
    p_first,
    p_second,
    rp_first,
    rp_second,
    first_bufs,
    cross_bufs,
    row_tx,
    row_pair,
    row_over,
    row_tx_along,
    row_along,
    tx_sems,
    rx_first,
    rx_second,
    z_second,
    w_sems,
    a_ref,
    w_all,
    kv_ref,
    kv_all,
    att,
    bias,
    kz_send,
    kz_recv,
    ky_send,
    ky_recv,
    a_send,
    a_recv,
    w_send,
    w_recv,
    f_send,
    f_recv,
    local_sem,
    own_w_sem,
    own_a_sem,
):
    place = positions()
    s, c, h, low, halves, partner, across, others = place
    g = lax.axis_index("groups")
    experts = lax.axis_size("sect") * lax.axis_size("head")
    moe_rows, width = res_ref.shape
    rows = q_ref.shape[0]
    chunk = 4 * moe_rows
    team = sects // 2
    line = team // 2
    j = lax.rem(s, team)
    base = s - j
    line_at = lax.rem(h, line)
    line_others = [lax.rem(line_at + i, line) for i in range(1, line)]
    sect_peers = [lax.rem(s + i, sects) for i in range(1, sects)]
    group_peers = [lax.rem(g + i, groups) for i in range(1, groups)]

    def teammate(i):
        return base + lax.rem(j + team + i, team)

    def opposite(i):
        return team - base + lax.rem(j + team + i, team)

    half = k_hbm.shape[1]
    own_k = pltpu.make_async_copy(k_hbm, kv_ref.at[:, pl.ds(0, half)], local_sem.at[0])
    own_v = pltpu.make_async_copy(v_hbm, kv_ref.at[:, pl.ds(half, half)], local_sem.at[1])
    own_k.start()
    own_v.start()
    inputs = [
        pltpu.make_async_copy(src, dst, in_sems.at[i])
        for i, (src, dst) in enumerate(
            (
                (seg_hbm, seg_ref),
                (q_hbm, q_ref),
                (res_hbm, res_ref),
                (gain_hbm, gain_ref),
                (ids_hbm, ids_ref),
                (route_hbm, route_ref),
            )
        )
    ]
    for copy in inputs:
        copy.start()
    greet(
        [{"sect": t} for t in sect_peers] + [{"groups": t} for t in group_peers] + [partner]
    )
    started = []

    def send(copy):
        copy.start()
        started.append(copy)

    own_k.wait()
    own_v.wait()

    window = bias.shape[1]
    blocks = window // rows
    first = jnp.maximum(s - (blocks - 1), 0)
    reach = min(blocks // 2, halves - 1)

    def kv_up(i):
        return remote(
            kv_ref, kv_all.at[s], kz_send.at[i], kz_recv.at[i], {"sect": s + 2 * i}
        )

    def kv_over(i):
        row = s - 2 * i
        return remote(
            kv_ref if i == 0 else kv_all.at[row],
            kv_all.at[row],
            ky_send.at[i],
            ky_recv.at[i],
            across,
        )

    for i in range(1, reach + 1):
        pl.when(h + i < halves)(kv_up(i).start)
    kv_over(0).start()
    own_kv = pltpu.make_async_copy(kv_ref, kv_all.at[s], local_sem.at[2])
    own_kv.start()

    pieces, w_rows, w_width = w_all.shape
    part = w_rows // groups
    w_cols = w_width // sects

    def w_piece(t, q):
        start = pl.multiple_of(lax.rem(t, team) * w_rows + g * part, part)
        return proj_ref.at[pl.ds(start, part), pl.ds(q * w_cols, w_cols)]

    def w_place(group, t, q):
        return w_all.at[
            q,
            pl.ds(pl.multiple_of(group * part, part), part),
            pl.ds(pl.multiple_of(t * w_cols, w_cols), w_cols),
        ]

    def w_side(group):
        return w_all.at[:, pl.ds(pl.multiple_of(group * part, part), part), :]

    def drain_weight():
        for i, u in enumerate(group_peers):
            remote(
                w_side(g), w_side(u), f_send.at[i], f_recv.at[g, 0], {"groups": u}
            ).wait_send()
        span = pl.ds(0, (sects - 1) * w_cols)
        side = w_all.at[:, pl.ds(0, part), span]
        remote(side, side, w_send.at[0], w_recv.at[0, 0], across).wait_send()

    def own_w(q):
        return pltpu.make_async_copy(w_piece(s, q), w_place(g, s, q), own_w_sem.at[q])

    def start_own(q):
        for i, u in enumerate(group_peers):
            remote(
                w_piece(s, q), w_place(g, s, q), f_send.at[i], f_recv.at[g, q], {"groups": u}
            ).start()
        own_w(q).start()

    def start_weight(q, targets):
        for t in targets:
            remote(
                w_piece(t, q), w_place(g, s, q), w_send.at[0], w_recv.at[q, s], {"sect": t}
            ).start()

    inside = [teammate(i) for i in range(1, team)]
    outside = [opposite(i) for i in range(team)]
    mixed = [outside[0]]
    for i in range(1, team):
        mixed += [inside[i - 1], outside[i]]
    ends = [jnp.where(base > 0, i, halves - 1 - i) for i in range(line)]
    far = [2 * z + y for z in ends for y in (low, 1 - low)]
    w_sources = far[:1] + [teammate(-i) for i in range(1, team)] + far[1:]

    def forward_weight(q, t):
        remote(
            w_piece(t, q), w_place(g, t, q), w_send.at[0], w_recv.at[q, t], {"sect": t}
        ).wait_recv()
        for i, u in enumerate(group_peers):
            remote(
                w_place(g, t, q), w_place(g, t, q), f_send.at[i], f_recv.at[g, q], {"groups": u}
            ).start()

    def wait_weight(q):
        for u in group_peers:
            remote(
                w_side(g).at[q], w_side(u).at[q], f_send.at[0], f_recv.at[u, q], {"groups": u}
            ).wait_recv()
        own_w(q).wait()

    loads = [
        pltpu.make_async_copy(src.at[0], dst, w_sems.at[i])
        for i, (src, dst) in enumerate(
            ((gate_hbm, gate_ref), (up_hbm, up_ref), (down_hbm, down_ref))
        )
    ]
    for load in loads:
        load.start()

    for q in range(pieces):
        start_own(q)
    start_weight(0, inside)
    start_weight(0, outside)
    for copy in inputs:
        copy.wait()
    row_of = lax.broadcasted_iota(jnp.int32, (rows, rows), 0)
    col_of = lax.broadcasted_iota(jnp.int32, (rows, rows), 1)
    seg_q = jnp.sum(
        jnp.where(row_of == col_of, seg_ref[s].astype(jnp.float32), 0.0), axis=1, keepdims=True
    )
    for b in range(blocks):
        behind = (s - first - b) * rows + row_of - col_of
        same = seg_q == seg_ref[first + b].astype(jnp.float32)
        bias[:, b * rows : (b + 1) * rows] = jnp.where(
            jnp.logical_and(same, behind >= 0), 0.0, MASKED
        )

        @pl.when(first + b > 2 * h + 1)
        def _(b=b):
            kv_all[first + b] = jnp.zeros(kv_all.shape[1:], kv_all.dtype)

    def relay_kv(i):
        remote(
            kv_ref, kv_all.at[s - 2 * i], kz_send.at[i], kz_recv.at[i], across
        ).wait_recv()
        kv_over(i).start()

    for i in range(1, reach + 1):
        pl.when(h - i >= 0)(functools.partial(relay_kv, i))

    def wait_kv(i):
        row = 2 * (h - i) + 1 - low
        remote(kv_ref, kv_all.at[row], ky_send.at[i], ky_recv.at[i], across).wait_recv()

    near = [teammate(-i) for i in range(1, team)]
    waiting = [(q, t) for q in range(pieces) for t in near]
    waiting += [(q, t) for q in range(pieces) for t in far]
    for i in range(reach + 1):
        pl.when(h - i >= 0)(functools.partial(wait_kv, i))
    if pieces > 1:
        start_weight(1, inside)
        start_weight(1, outside)
    own_kv.wait()

    scale = 1.0 / math.sqrt(HEAD_WIDTH)
    kv_width = kv_heads * HEAD_WIDTH
    per_kv = q_ref.shape[1] // kv_heads
    per, step_cols = att.shape[1], att.shape[3]
    cols = per * step_cols

    def attend(i):
        t = lax.rem(j + 1 + i // per, team)
        u = lax.rem(i, per)
        at = t * cols + u * step_cols
        kv_head = at // per_kv
        k_col = pl.multiple_of(kv_head * HEAD_WIDTH, HEAD_WIDTH)
        v_col = pl.multiple_of(kv_width + kv_head * HEAD_WIDTH, HEAD_WIDTH)
        span = pl.ds(first, blocks)
        keys = kv_all[span, :, pl.ds(k_col, HEAD_WIDTH)].reshape(window, HEAD_WIDTH)
        vals = kv_all[span, :, pl.ds(v_col, HEAD_WIDTH)].reshape(window, HEAD_WIDTH)
        for k in range(step_cols // HEAD_WIDTH):
            q_col = pl.multiple_of(at + k * HEAD_WIDTH, HEAD_WIDTH)
            q = q_ref[:, pl.ds(q_col, HEAD_WIDTH)]
            scores = lax.dot_general(
                q, keys, (((1,), (1,)), ((), ())), preferred_element_type=jnp.float32
            )
            scores = scores * scale + bias[...]
            top = jnp.max(scores, axis=1, keepdims=True)
            weights = jnp.exp(scores - top).astype(jnp.bfloat16)
            total = jnp.sum(weights.astype(jnp.float32), axis=1, keepdims=True)
            mixed = jnp.dot(weights, vals, preferred_element_type=jnp.float32)
            att[t, u, :, k * HEAD_WIDTH : (k + 1) * HEAD_WIDTH] = (mixed / total).astype(
                jnp.bfloat16
            )

    def a_place(t, u):
        return a_ref.at[
            pl.ds(pl.multiple_of(t * rows, rows), rows),
            pl.ds(pl.multiple_of(u * step_cols, step_cols), step_cols),
        ]

    def a_copy(t, u):
        return remote(
            att.at[t, u], a_place(j, u), a_send.at[0], a_recv.at[j, u], {"sect": base + t}
        )

    def step(i, carry):
        attend(i)
        last = i - 1

        @pl.when(jnp.logical_and(last >= 0, last < (team - 1) * per))
        def _():
            a_copy(lax.rem(j + 1 + last // per, team), lax.rem(last, per)).start()

        return carry

    steps = team * per
    segments = 4 if steps % 4 == 0 else 1
    for i in range(segments):
        lax.fori_loop(i * steps // segments, (i + 1) * steps // segments, step, 0)
        if i + 1 < segments:
            for _ in range(2):
                forward_weight(*waiting.pop(0))
    own_a = [
        pltpu.make_async_copy(att.at[j, u], a_place(j, u), own_a_sem.at[u]) for u in range(per)
    ]
    for copy in own_a:
        copy.start()
    while len(waiting) > (pieces - 1) * len(far):
        forward_weight(*waiting.pop(0))

    for _ in range(min(2, len(waiting))):
        forward_weight(*waiting.pop(0))
    team_peers = [lax.rem(j + i, team) for i in range(1, team)]
    for t in team_peers:
        for u in range(per):
            remote(
                att.at[t, u], a_place(t, u), a_send.at[0], a_recv.at[t, u], across
            ).wait_recv()
    for copy in own_a:
        copy.wait()

    tile = 512
    subs = 2 if w_width % (2 * tile) == 0 else 1

    def project(t, q, cut):
        left = a_ref[pl.ds(pl.multiple_of(t * chunk, chunk), chunk), :]
        which = cut.start // w_width
        for n in range(cut.start, cut.stop, tile):
            at = n - which * w_width
            part = jnp.dot(
                left, w_all[which, :, at : at + tile], preferred_element_type=jnp.float32
            )
            p_first[pl.ds(2 * t, 2), :, :, n : n + tile] = part.astype(jnp.bfloat16).reshape(
                2, 2, moe_rows, tile
            )

    enter, cross, along, collect, drain_first = reducer(
        place,
        line_at,
        lambda t: base + 2 * t + low,
        p_first,
        acc,
        rp_first,
        *[first_bufs.at[k] for k in range(4)],
        [tx_sems.at[pl.ds(0, 1)], rx_first.at[0]]
        + [tx_sems.at[pl.ds(1, 1)], rx_first.at[1]]
        + [tx_sems.at[pl.ds(2, 1)], rx_first.at[2]],
    )
    span = w_width // subs
    def cuts(q):
        return [
            (t, q * subs + i, slice(q * w_width + i * span, q * w_width + (i + 1) * span))
            for i in range(subs)
            for t in line_others + [line_at]
        ]

    behind = []
    for q in range(pieces):
        items = cuts(q)
        wait_weight(q)
        for i, item in enumerate(items):
            project(*item)
            enter(*item)
            if i >= 1 and q + 1 < pieces:
                cross(*items[i - 1])
        if q + 1 < pieces:
            cross(*items[-1])
            while waiting:
                forward_weight(*waiting.pop(0))
            behind += items
            continue
        n = len(behind)
        for i, item in enumerate(items):
            cross(*item)
            for other in behind[i * n // len(items) : (i + 1) * n // len(items)]:
                along(*other)
        for item in items:
            along(*item)
        for item in behind + items:
            collect(*item)

    summed = jnp.concatenate(
        [
            acc[:, q * w_width + t * w_cols : q * w_width + (t + 1) * w_cols]
            for t in range(sects)
            for q in range(pieces)
        ],
        axis=1,
    )
    mid = (res_ref[...].astype(jnp.float32) + summed).astype(jnp.bfloat16)
    out_ref[0] = mid
    wide = mid.astype(jnp.float32)
    inverse = lax.rsqrt(jnp.mean(wide * wide, axis=1, keepdims=True) + NORM_EPS)
    normed = wide * inverse * gain_ref[...].astype(jnp.float32).reshape(1, width)
    lanes = xg.shape[3] - width
    lane = lax.broadcasted_iota(jnp.int32, (moe_rows, lanes), 1)
    place_of = lax.broadcasted_iota(jnp.int32, (lanes, moe_rows), 0)
    route = route_ref[...]
    route = route / jnp.sum(route, axis=0, keepdims=True)
    share = jnp.zeros((lanes, moe_rows), jnp.float32)
    for k in range(route.shape[0]):
        ids = ids_ref[k : k + 1, :]
        named = jnp.logical_or(place_of == ids, place_of == ids + experts)
        share = share + jnp.where(named, route[k : k + 1, :], 0.0)
    share = share.T
    high = share.astype(jnp.bfloat16).astype(jnp.float32)
    xg[s, c, :, width:] = jnp.where(lane < experts, high, share - high).astype(jnp.bfloat16)
    xg[s, c, :, :width] = normed.astype(jnp.bfloat16)

    guarded = []
    total = xg.shape[3]
    middle = total // 256 * 128
    row_cuts = [slice(0, middle), slice(middle, total)]

    def hop(t, p, slot, step):
        block = xg.at[2 * t + low, c, :, row_cuts[p]]
        return remote(
            block, block, row_tx_along.at[p, slot], row_along.at[p, t], {"sect": s + step}
        )

    def over(t, p):
        block = xg.at[2 * t + low, c, :, row_cuts[p]]
        return remote(block, block, row_tx.at[0], row_over.at[p, t], across)

    def to_pair(row):
        block = xg.at[row, c]
        remote(block, block, row_tx.at[1], row_pair.at[row], partner).start()

    def from_pair(row):
        block = xg.at[row, 1 - c]
        remote(block, block, row_tx.at[1], row_pair.at[row], partner).wait_recv()

    def from_over(t):
        for p, cut in enumerate(row_cuts):
            block = xg.at[2 * t + 1 - low, c, :, cut]
            remote(block, block, row_tx.at[0], row_over.at[p, t], across).wait_recv()

    paired = jnp.minimum(h, halves - 1 - h)
    away = jnp.where(2 * h < halves - 1, 1, -1)
    order = [h]
    hops = [0]
    for k in range(1, halves):
        near = (k + 1) // 2 * (-1 if k % 2 else 1)
        order.append(h + away * jnp.where(k <= 2 * paired, near, k - paired))
        hops.append(jnp.where(k <= 2 * paired, (k + 1) // 2, k - paired))

    def onward(k, p):
        t = order[k]
        return [
            (jnp.logical_and(t < h, h + 1 < halves), hop(t, p, t, 2)),
            (jnp.logical_and(t > h, h >= 1), hop(t, p, t, -2)),
        ]

    def relay_rows(k):
        t = order[k]
        for p in range(2):
            block = xg.at[2 * t + low, c, :, row_cuts[p]]
            remote(
                block, block, row_tx_along.at[p, t], row_along.at[p, t], across
            ).wait_recv()
            for when, copy in onward(k, p):
                pl.when(when)(copy.start)
            over(t, p).start()
        to_pair(2 * t + low)

    for k in range(1, halves):
        for p in range(2):
            guarded.extend(onward(k, p))

    def relay_step(i):
        for k in range(i + 1, halves):
            if (k + 1) // 2 <= i + 1:
                pl.when(hops[k] == i + 1)(functools.partial(relay_rows, k))

    for p in range(2):
        for when, copy in (
            (h + 1 < halves, hop(h, p, h, 2)),
            (h >= 1, hop(h, p, halves + h, -2)),
        ):
            pl.when(when)(copy.start)
            guarded.append((when, copy))
        over(h, p).start()
    to_pair(s)
    for load in loads:
        load.wait()

    def experts_of(i, t, q, cut):
        if q == 0:
            hidden_of(i, t)
        for n in range(cut.start, cut.stop, tile):
            part = jnp.dot(
                hidden[...], down_ref[:, n : n + tile], preferred_element_type=jnp.float32
            )
            p_second[pl.ds(2 * t, 2), :, :, n : n + tile] = (
                (part * own_share(t)).astype(jnp.bfloat16).reshape(2, 2, moe_rows, tile)
            )

    def own_share(t):
        pair = xg[pl.ds(2 * t, 2), :, :, width:].astype(jnp.float32).reshape(chunk, lanes)
        expert = s * 2 + c
        at = lax.broadcasted_iota(jnp.int32, (chunk, lanes), 1)
        mine = jnp.logical_or(at == expert, at == expert + experts)
        return jnp.sum(jnp.where(mine, pair, 0.0), axis=1, keepdims=True)

    def hidden_of(i, t):
        relay_step(i)
        from_over(t)
        to_pair(2 * t + 1 - low)
        for row in (2 * t + low, 2 * t + 1 - low):
            from_pair(row)
        x = xg[pl.ds(2 * t, 2), :, :, :width].reshape(chunk, width)
        step = 256
        for n in range(0, hidden.shape[1], step):
            gate_act = jnp.dot(
                x, gate_ref[:, n : n + step], preferred_element_type=jnp.float32
            )
            up_act = jnp.dot(x, up_ref[:, n : n + step], preferred_element_type=jnp.float32)
            silu = gate_act / (1.0 + jnp.exp(-gate_act))
            hidden[:, n : n + step] = (silu * up_act).astype(jnp.bfloat16)

    cs, ry, zs = [cross_bufs.at[k, pl.ds(0, halves)] for k in range(3)]
    rz = cross_bufs.at[3]
    y_send, y_recv = tx_sems.at[pl.ds(4, 1)], rx_second.at[1]
    z_send, z_recv = tx_sems.at[pl.ds(5, 1)], z_second
    sems = [tx_sems.at[pl.ds(3, 1)], rx_second.at[0], y_send, y_recv, z_send, z_recv]
    enter, cross, _, _, drain_second = reducer(
        place, h, None, p_second, acc, rp_second, cs, ry, zs, rz, sems
    )
    parts = 2 if width % 1024 == 0 else 1
    size = width // parts
    cuts_of = [(q, slice(q * size, (q + 1) * size)) for q in range(parts)]

    def own_sum(t, q, cut):
        return (
            p_second[2 * t + low, c, :, cut].astype(jnp.float32)
            + rp_second[t, low, :, cut].astype(jnp.float32)
            + ry[t, :, cut].astype(jnp.float32)
        )

    def wait_across(t, q, cut):
        remote(
            cs.at[t, :, cut], ry.at[t, :, cut], y_send.at[0], y_recv.at[q, t], across
        ).wait_recv()

    def wait_along(slot, row, t, q, cut):
        remote(
            zs.at[t, :, cut], rz.at[slot, :, cut], z_send.at[0], z_recv.at[row, t], across
        ).wait_recv()

    def chain(t, q, cut):
        wait_across(t, q, cut)
        joined = jnp.where(t > h, h >= 1, h + 1 < halves)

        @pl.when(jnp.logical_not(joined))
        def _():
            zs[t, :, cut] = own_sum(t, q, cut).astype(jnp.bfloat16)

        @pl.when(joined)
        def _():
            wait_along(t, q, t, q, cut)
            zs[t, :, cut] = (
                own_sum(t, q, cut) + rz[t, :, cut].astype(jnp.float32)
            ).astype(jnp.bfloat16)

        landed = h - 1 == t
        remote(
            zs.at[t, :, cut],
            rz.at[jnp.where(landed, halves, t), :, cut],
            z_send.at[0],
            z_recv.at[q + jnp.where(landed, parts, 0), t],
            {"sect": s + jnp.where(t > h, 2, -2)},
        ).start()

    def finish(q, cut):
        wait_across(h, q, cut)
        acc[:, cut] = own_sum(h, q, cut)

        @pl.when(h >= 1)
        def _():
            wait_along(h, q, h, q, cut)
            acc[:, cut] += rz[h, :, cut].astype(jnp.float32)

        @pl.when(h + 1 < halves)
        def _():
            wait_along(halves, q + parts, h, q, cut)
            acc[:, cut] += rz[halves, :, cut].astype(jnp.float32)

    lower = h < halves // 2
    targets = [
        jnp.where(lower, halves // 2 + i, halves // 2 - 1 - i) for i in range(halves // 2)
    ]
    targets += [h - line_at + t for t in line_others]

    def each(step, t):
        for q, cut in cuts_of:
            step(t, q, cut)

    for i, t in enumerate(order):
        for q, cut in cuts_of:
            experts_of(i, t, q, cut)
            enter(t, q, cut)
        if i == halves - 2:
            each(cross, targets[0])
    for i, t in enumerate(targets[1:] + [h]):
        each(cross, t)
        if i < 0:
            each(chain, targets[i])
    for t in targets[0:]:
        each(chain, t)
    for q, cut in cuts_of:
        finish(q, cut)
    out_ref[1] = acc[...].astype(jnp.bfloat16)
    for i in range(1, reach + 1):
        pl.when(h + i < halves)(kv_up(i).wait_send)
    for i in range(reach + 1):
        pl.when(h - i >= 0)(kv_over(i).wait_send)
    some = pl.ds(0, team - 1)
    remote(att.at[some], att.at[some], a_send.at[0], a_recv.at[0, 0], across).wait_send()
    rows_sent = xg.at[pl.ds(0, halves), c]
    remote(rows_sent, rows_sent, row_tx.at[0], row_over.at[0, 0], across).wait_send()
    rows_sent = xg.at[:, c]
    remote(rows_sent, rows_sent, row_tx.at[1], row_pair.at[0], partner).wait_send()
    drain_weight()
    drain_first()
    drain_second()
    for when, copy in guarded:
        pl.when(when)(copy.wait_send)
    for copy in started:
        copy.wait_send()

def fused_layer(
    queries, keys, values, segments, proj, residual, gain, ids, route, gate, up, down
):
    groups = lax.axis_size("groups")
    sects = lax.axis_size("sect")
    heads = lax.axis_size("head")
    rows = queries.shape[0]
    team = sects // 2
    cols = queries.shape[1] // team
    step_cols = min(cols, 4 * HEAD_WIDTH)
    per = cols // step_cols
    pieces = 2 if proj.shape[1] % 256 == 0 else 1
    w_rows = proj.shape[0] // team
    blocks = min(sects, -(-segments.shape[0] // (2 * rows)) + 1)
    halves = sects // 2
    block = residual.shape
    lanes = -(-2 * sects * heads // 128) * 128
    bf16 = jnp.bfloat16
    kv_shape = (rows, 2 * keys.shape[1])
    operands = (
        queries,
        keys,
        values,
        segments.reshape(sects, 1, rows),
        proj,
        residual,
        gain,
        ids.T,
        route.T,
        gate,
        up,
        down,
    )
    both = pl.pallas_call(
        functools.partial(layer_kernel, groups, sects, keys.shape[1] // HEAD_WIDTH),
        out_shape=jax.ShapeDtypeStruct((2,) + block, bf16),
        in_specs=[pl.BlockSpec(memory_space=pltpu.HBM)] * len(operands),
        out_specs=VMEM_SPEC,
        scratch_shapes=[
            pltpu.VMEM(queries.shape, bf16),
            pltpu.VMEM((sects, 1, rows), jnp.int32),
            pltpu.VMEM(block, bf16),
            pltpu.VMEM(gain.shape, bf16),
            pltpu.VMEM(ids.shape[::-1], jnp.int32),
            pltpu.VMEM(route.shape[::-1], jnp.float32),
            DMA((6,)),
            pltpu.VMEM(gate.shape[1:], bf16),
            pltpu.VMEM(up.shape[1:], bf16),
            pltpu.VMEM(down.shape[1:], bf16),
            pltpu.VMEM((4 * block[0], gate.shape[2]), bf16),
            pltpu.VMEM((sects, heads, block[0], block[1] + lanes), bf16),
            pltpu.VMEM(block, jnp.float32),
            pltpu.VMEM((team, heads) + block, bf16),
            pltpu.VMEM((sects, heads) + block, bf16),
            pltpu.VMEM((team // 2, 2) + block, bf16),
            pltpu.VMEM((halves, 2) + block, bf16),
            pltpu.VMEM((4, team // 2) + block, bf16),
            pltpu.VMEM((4, halves + 1) + block, bf16),
            DMA((2,)),
            DMA((sects,)),
            DMA((2, halves)),
            DMA((2, sects)),
            DMA((2, halves)),
            DMA((6,)),
            DMA((3, 2 * pieces, team // 2)),
            DMA((2, 2, halves)),
            DMA((4, halves)),
            DMA((3,)),
            pltpu.VMEM((rows * team, cols), bf16),
            pltpu.VMEM((pieces, w_rows, proj.shape[1] // pieces * sects), bf16),
            pltpu.VMEM(kv_shape, bf16),
            pltpu.VMEM((sects,) + kv_shape, bf16),
            pltpu.VMEM((team, per, rows, step_cols), bf16),
            pltpu.VMEM((rows, blocks * rows), jnp.float32),
            DMA((halves,)),
            DMA((halves,)),
            DMA((halves,)),
            DMA((halves,)),
            DMA((1,)),
            DMA((team, per)),
            DMA((1,)),
            DMA((pieces, sects)),
            DMA((groups,)),
            DMA((groups, pieces)),
            DMA((3,)),
            DMA((pieces,)),
            DMA((per,)),
        ],
        compiler_params=pltpu.CompilerParams(
            collective_id=4, has_side_effects=True, vmem_limit_bytes=LAYER_ROOM
        ),
        name="layer",
    )(*[pltpu.with_memory_space_constraint(x, pltpu.HBM) for x in operands])
    return both[0], both[1]

def shards(
    queries,
    packed_key_rows,
    values,
    segments,
    proj_weight,
    residual,
    norm_gain,
    expert_ids,
    route_weights,
    gate_weight,
    up_weight,
    down_weight,
):
    sects = lax.axis_size("sect")
    heads = lax.axis_size("head")
    s = lax.axis_index("sect")
    c = lax.axis_index("head")
    experts = sects * heads
    moe_rows, width = residual.shape
    fits = experts * moe_rows * width * 24 <= VMEM_ROOM
    if fits and sects % 4 == 0 and proj_weight.shape[1] % 128 == 0:
        return fused_layer(
            queries,
            packed_key_rows,
            values,
            segments,
            proj_weight,
            residual,
            norm_gain,
            expert_ids,
            route_weights,
            gate_weight,
            up_weight,
            down_weight,
        )
    attended, weight = exchange_attention(
        queries, packed_key_rows, values, segments, proj_weight
    )
    partial_rows = jnp.dot(attended, weight, preferred_element_type=jnp.float32)
    projected = sum_scatter(partial_rows.astype(jnp.bfloat16), moe_rows, 1)

    hidden_mid = (residual.astype(jnp.float32) + projected).astype(jnp.bfloat16)
    mid_float = lax.optimization_barrier(hidden_mid).astype(jnp.float32)
    inverse = lax.rsqrt(jnp.mean(mid_float * mid_float, axis=1, keepdims=True) + NORM_EPS)
    normed = (mid_float * inverse * norm_gain.astype(jnp.float32)[None, :]).astype(jnp.bfloat16)

    route_share = route_weights / jnp.sum(route_weights, axis=1, keepdims=True)
    named = expert_ids[:, :, None] == jnp.arange(experts, dtype=jnp.int32)[None, None, :]
    share = jnp.sum(jnp.where(named, route_share[:, :, None], 0.0), axis=1)
    share_high = lax.reduce_precision(share, 8, 7)
    share_low = (share - share_high).astype(jnp.bfloat16)
    pad = -(2 * experts) % 128
    sent = jnp.concatenate(
        [
            normed,
            share_high.astype(jnp.bfloat16),
            share_low,
            jnp.zeros((moe_rows, pad), jnp.bfloat16),
        ],
        axis=1,
    )
    gathered = gather_rows(sent, 2)
    expert = s * heads + c
    all_rows = gathered[:, :width]
    pair = gathered[:, width:].astype(jnp.float32)
    lane = jnp.arange(pair.shape[1], dtype=jnp.int32)[None, :]
    mine = jnp.logical_or(lane == expert, lane == expert + experts)
    own_share = jnp.sum(jnp.where(mine, pair, 0.0), axis=1, keepdims=True)
    gate_act = jnp.dot(all_rows, gate_weight[0], preferred_element_type=jnp.float32)
    up_act = jnp.dot(all_rows, up_weight[0], preferred_element_type=jnp.float32)
    hidden = (jax.nn.silu(gate_act) * up_act).astype(jnp.bfloat16)
    result = jnp.dot(hidden, down_weight[0], preferred_element_type=jnp.float32)
    mixed = (result * own_share).astype(jnp.bfloat16)
    mixture = sum_scatter(mixed, moe_rows, 3)
    return (hidden_mid, mixture.astype(jnp.bfloat16))

def solution(mesh):
    rows = P(("groups", "sect", "head"), None)
    split = P(("groups", "sect"), "head")
    expert = P(("sect", "head"), None, None)
    placed = (
        split,
        split,
        split,
        P("groups"),
        P("head", "sect"),
        rows,
        P(),
        rows,
        rows,
        expert,
        expert,
        expert,
    )
    return jax.shard_map(
        shards, mesh=mesh, in_specs=placed, out_specs=(rows, rows), check_vma=False
    )
```

```python
import functools
import math

import jax
import jax.numpy as jnp
from jax import lax
from jax.experimental import pallas as pl
from jax.experimental.pallas import tpu as pltpu
from jax.sharding import PartitionSpec as P

HEAD_WIDTH = 128
MASKED = -1e30
NORM_EPS = 1e-06
VMEM_ROOM = 64 << 20
LAYER_ROOM = 52 << 20

MESH = pl.DeviceIdType.MESH
VMEM_SPEC = pl.BlockSpec(memory_space=pltpu.VMEM)
ANY_SPEC = pl.BlockSpec(memory_space=pl.ANY)
DMA = pltpu.SemaphoreType.DMA

def greet(devices):
    barrier = pltpu.get_barrier_semaphore()
    for device in devices:
        pl.semaphore_signal(barrier, inc=1, device_id=device, device_id_type=MESH)
    pl.semaphore_wait(barrier, len(devices))

def remote(src, dst, send_sem, recv_sem, device):
    return pltpu.make_async_remote_copy(
        src_ref=src,
        dst_ref=dst,
        send_sem=send_sem,
        recv_sem=recv_sem,
        device_id=device,
        device_id_type=MESH,
    )

def attention_body(
    extra,
    groups,
    sects,
    kv_heads,
    q_ref,
    k_ref,
    v_ref,
    seg_ref,
    w_ref,
    a_out,
    w_out,
    kv_ref,
    kv_all,
    att,
    bias,
    kz_send,
    kz_recv,
    ky_send,
    ky_recv,
    a_send,
    a_recv,
    w_send,
    w_recv,
    f_send,
    f_recv,
    local_sem,
):
    g = lax.axis_index("groups")
    s = lax.axis_index("sect")
    halves = sects // 2
    h = s // 2
    low = lax.rem(s, 2)
    rows = q_ref.shape[0]
    cols = q_ref.shape[1] // sects
    w_cols = w_ref.shape[1]
    w_rows = w_ref.shape[0] // sects
    part = w_rows // groups
    other_y = 2 * h + 1 - low
    sect_peers = [lax.rem(s + i, sects) for i in range(1, sects)]
    group_peers = [lax.rem(g + i, groups) for i in range(1, groups)]
    half = k_ref.shape[1]
    own_k = pltpu.make_async_copy(k_ref, kv_ref.at[:, pl.ds(0, half)], local_sem.at[3])
    own_v = pltpu.make_async_copy(v_ref, kv_ref.at[:, pl.ds(half, half)], local_sem.at[4])
    own_k.start()
    own_v.start()
    greet(
        [{"sect": t} for t in sect_peers] + [{"groups": t} for t in group_peers] + extra
    )
    started = []
    own_k.wait()
    own_v.wait()

    def kv_cross(t):
        return remote(
            kv_ref if t is None else kv_all.at[2 * t + low],
            kv_all.at[s if t is None else 2 * t + low],
            ky_send.at[h if t is None else t],
            ky_recv.at[h if t is None else t],
            {"sect": other_y},
        )

    for i in range(1, halves):
        t = lax.rem(h + i, halves)
        copy = remote(
            kv_ref, kv_all.at[s], kz_send.at[t], kz_recv.at[h], {"sect": 2 * t + low}
        )
        copy.start()
        started.append(copy)
    copy = kv_cross(None)
    copy.start()
    started.append(copy)
    own_kv = pltpu.make_async_copy(kv_ref, kv_all.at[s], local_sem.at[0])
    own_kv.start()

    def w_piece(t):
        return w_ref.at[pl.ds(pl.multiple_of(t * w_rows + g * part, part), part), :]

    def w_place(group, t):
        span = pl.ds(pl.multiple_of(group * part, part), part)
        if len(w_out.shape) == 3:
            return w_out.at[t, span, :]
        return w_out.at[span, pl.ds(pl.multiple_of(t * w_cols, w_cols), w_cols)]

    for t in sect_peers:
        copy = remote(
            w_piece(t), w_place(g, s), w_send.at[t], w_recv.at[s], {"sect": t}
        )
        copy.start()
        started.append(copy)
    own_w = pltpu.make_async_copy(w_piece(s), w_place(g, s), local_sem.at[1])
    own_w.start()
    for i, t in enumerate(group_peers):
        copy = remote(
            w_piece(s), w_place(g, s), f_send.at[i, s], f_recv.at[g, s], {"groups": t}
        )
        copy.start()
        started.append(copy)

    for i in range(1, halves):
        t = lax.rem(h + i, halves)
        remote(
            kv_ref, kv_all.at[2 * t + low], kz_send.at[t], kz_recv.at[t], {"sect": 2 * t + low}
        ).wait_recv()
        copy = kv_cross(t)
        copy.start()
        started.append(copy)

    window = bias.shape[1]
    blocks = window // rows
    first = jnp.maximum(s - (blocks - 1), 0)
    row_of = lax.broadcasted_iota(jnp.int32, (rows, rows), 0)
    col_of = lax.broadcasted_iota(jnp.int32, (rows, rows), 1)
    seg_q = jnp.sum(
        jnp.where(row_of == col_of, seg_ref[s].astype(jnp.float32), 0.0), axis=1, keepdims=True
    )
    for b in range(blocks):
        behind = (s - first - b) * rows + row_of - col_of
        same = seg_q == seg_ref[first + b].astype(jnp.float32)
        bias[:, b * rows : (b + 1) * rows] = jnp.where(
            jnp.logical_and(same, behind >= 0), 0.0, MASKED
        )

    for i in range(halves):
        t = lax.rem(h + i, halves)
        remote(
            kv_ref, kv_all.at[2 * t + 1 - low], ky_send.at[t], ky_recv.at[t], {"sect": other_y}
        ).wait_recv()
    own_kv.wait()

    scale = 1.0 / math.sqrt(HEAD_WIDTH)
    kv_width = kv_heads * HEAD_WIDTH
    per_kv = q_ref.shape[1] // kv_heads

    def attend(i, carry):
        t = lax.rem(s + 1 + i, sects)
        kv_head = (t * cols) // per_kv
        k_col = pl.multiple_of(kv_head * HEAD_WIDTH, HEAD_WIDTH)
        v_col = pl.multiple_of(kv_width + kv_head * HEAD_WIDTH, HEAD_WIDTH)
        span = pl.ds(first, blocks)
        keys = kv_all[span, :, pl.ds(k_col, HEAD_WIDTH)].reshape(window, HEAD_WIDTH)
        vals = kv_all[span, :, pl.ds(v_col, HEAD_WIDTH)].reshape(window, HEAD_WIDTH)
        for j in range(cols // HEAD_WIDTH):
            q_col = pl.multiple_of(t * cols + j * HEAD_WIDTH, HEAD_WIDTH)
            q = q_ref[:, pl.ds(q_col, HEAD_WIDTH)]
            scores = lax.dot_general(
                q, keys, (((1,), (1,)), ((), ())), preferred_element_type=jnp.float32
            )
            scores = scores * scale + bias[...]
            top = jnp.max(scores, axis=1, keepdims=True)
            weights = jnp.exp(scores - top).astype(jnp.bfloat16)
            total = jnp.sum(weights.astype(jnp.float32), axis=1, keepdims=True)
            mixed = jnp.dot(weights, vals, preferred_element_type=jnp.float32)
            att[t, :, j * HEAD_WIDTH : (j + 1) * HEAD_WIDTH] = (mixed / total).astype(
                jnp.bfloat16
            )
        return carry

    def a_place(t):
        return a_out.at[pl.ds(pl.multiple_of(t * rows, rows), rows), :]

    def a_copy(t):
        return remote(att.at[t], a_place(s), a_send.at[t], a_recv.at[s], {"sect": t})

    def step(i, carry):
        attend(i, carry)

        @pl.when(i >= 1)
        def _():
            a_copy(lax.rem(s + i, sects)).start()

        return carry

    lax.fori_loop(0, sects, step, 0)
    own_a = pltpu.make_async_copy(att.at[s], a_place(s), local_sem.at[2])
    own_a.start()

    for t in sect_peers:
        remote(
            w_piece(s), w_place(g, t), w_send.at[t], w_recv.at[t], {"sect": t}
        ).wait_recv()
        for i, u in enumerate(group_peers):
            copy = remote(
                w_place(g, t), w_place(g, t), f_send.at[i, t], f_recv.at[g, t], {"groups": u}
            )
            copy.start()
            started.append(copy)

    def wait_rows(t):
        remote(att.at[t], a_place(t), a_send.at[t], a_recv.at[t], {"sect": t}).wait_recv()

    def wait_weight():
        for u in group_peers:
            for t in [s] + sect_peers:
                remote(
                    w_place(g, t),
                    w_place(u, t),
                    f_send.at[0, t],
                    f_recv.at[u, t],
                    {"groups": u},
                ).wait_recv()
        own_w.wait()

    def drain():
        for copy in started:
            copy.wait_send()
        for t in sect_peers:
            a_copy(t).wait_send()

    return sect_peers, wait_rows, wait_weight, own_a.wait, drain

def attention_kernel(*arguments):
    sect_peers, wait_rows, wait_weight, wait_own, drain = attention_body([], *arguments)
    for t in sect_peers:
        wait_rows(t)
    wait_weight()
    wait_own()
    drain()

def attention_scratch(groups, sects, rows, cols, kv_shape, window):
    return [
        pltpu.VMEM(kv_shape, jnp.bfloat16),
        pltpu.VMEM((sects,) + kv_shape, jnp.bfloat16),
        pltpu.VMEM((sects, rows, cols), jnp.bfloat16),
        pltpu.VMEM((rows, window), jnp.float32),
        DMA((sects // 2,)),
        DMA((sects // 2,)),
        DMA((sects // 2,)),
        DMA((sects // 2,)),
        DMA((sects,)),
        DMA((sects,)),
        DMA((sects,)),
        DMA((sects,)),
        DMA((groups, sects)),
        DMA((groups, sects)),
        DMA((5,)),
    ]

def exchange_attention(queries, keys, values, segments, proj_weight):
    kv_heads = keys.shape[1] // HEAD_WIDTH
    groups = lax.axis_size("groups")
    sects = lax.axis_size("sect")
    rows, width = queries.shape
    cols = width // sects
    w_rows = proj_weight.shape[0] // sects
    w_cols = proj_weight.shape[1]
    blocks = min(sects, -(-segments.shape[0] // (2 * rows)) + 1)
    kv_shape = (rows, 2 * keys.shape[1])
    aligned = w_cols % 128 == 0
    w_shape = (w_rows, w_cols * sects) if aligned else (sects, w_rows, w_cols)
    attended, weight = pl.pallas_call(
        functools.partial(attention_kernel, groups, sects, kv_heads),
        out_shape=(
            jax.ShapeDtypeStruct((rows * sects, cols), jnp.bfloat16),
            jax.ShapeDtypeStruct(w_shape, jnp.bfloat16),
        ),
        in_specs=[VMEM_SPEC, VMEM_SPEC, VMEM_SPEC, VMEM_SPEC, ANY_SPEC],
        out_specs=(ANY_SPEC, ANY_SPEC),
        scratch_shapes=attention_scratch(groups, sects, rows, cols, kv_shape, blocks * rows),
        compiler_params=pltpu.CompilerParams(collective_id=0, has_side_effects=True),
        name="attention",
    )(queries, keys, values, segments.reshape(sects, 1, rows), proj_weight)
    if not aligned:
        weight = weight.transpose(1, 0, 2).reshape(w_rows, w_cols * sects)
    return attended, weight

def positions():
    s = lax.axis_index("sect")
    c = lax.axis_index("head")
    halves = lax.axis_size("sect") // 2
    h = s // 2
    low = lax.rem(s, 2)
    partner = {"head": 1 - c}
    across = {"sect": 2 * h + 1 - low}
    others = [lax.rem(h + i, halves) for i in range(1, halves)]
    return s, c, h, low, halves, partner, across, others

def sum_kernel(
    p_ref, o_ref, rp, cs, ry, zs, rz, p_send, p_recv, y_send, y_recv, z_send, z_recv
):
    s, c, h, low, halves, partner, across, others = positions()
    greet([partner, across] + [{"sect": 2 * t + low} for t in others])
    order = others + [h]
    started = []

    def widen(x):
        return x.astype(jnp.float32)

    for t in order:
        copy = remote(
            p_ref.at[pl.ds(2 * t, 2), 1 - c], rp.at[t], p_send.at[t], p_recv.at[t], partner
        )
        copy.start()
        started.append(copy)
    for t in order:
        remote(
            p_ref.at[pl.ds(2 * t, 2), 1 - c], rp.at[t], p_send.at[t], p_recv.at[t], partner
        ).wait_recv()
        cs[t] = (widen(p_ref[2 * t + 1 - low, c]) + widen(rp[t, 1 - low])).astype(jnp.bfloat16)
        copy = remote(cs.at[t], ry.at[t], y_send.at[t], y_recv.at[t], across)
        copy.start()
        started.append(copy)
    for t in order:
        remote(cs.at[t], ry.at[t], y_send.at[t], y_recv.at[t], across).wait_recv()
        total = widen(p_ref[2 * t + low, c]) + widen(rp[t, low]) + widen(ry[t])
        if t is h:
            o_ref[...] = total
        else:
            zs[t] = total.astype(jnp.bfloat16)
            copy = remote(
                zs.at[t], rz.at[h], z_send.at[t], z_recv.at[h], {"sect": 2 * t + low}
            )
            copy.start()
            started.append(copy)
    for t in others:
        remote(
            zs.at[t], rz.at[t], z_send.at[t], z_recv.at[t], {"sect": 2 * t + low}
        ).wait_recv()
        o_ref[...] += widen(rz[t])
    for copy in started:
        copy.wait_send()

def sum_scatter(partial_rows, moe_rows, collective_id):
    sects = lax.axis_size("sect")
    heads = lax.axis_size("head")
    width = partial_rows.shape[1]
    halves = sects // 2
    block = (moe_rows, width)
    return pl.pallas_call(
        sum_kernel,
        out_shape=jax.ShapeDtypeStruct(block, jnp.float32),
        in_specs=[VMEM_SPEC],
        out_specs=VMEM_SPEC,
        scratch_shapes=[
            pltpu.VMEM((halves, 2) + block, jnp.bfloat16),
            pltpu.VMEM((halves,) + block, jnp.bfloat16),
            pltpu.VMEM((halves,) + block, jnp.bfloat16),
            pltpu.VMEM((halves,) + block, jnp.bfloat16),
            pltpu.VMEM((halves,) + block, jnp.bfloat16),
        ]
        + [DMA((halves,))] * 6,
        compiler_params=pltpu.CompilerParams(
            collective_id=collective_id, has_side_effects=True
        ),
        name="sum_scatter",
    )(partial_rows.reshape((sects, heads) + block))

def gather_kernel(
    x_ref, o_ref, p_send, p_recv, y_send, y_recv, z_send, z_recv, local_sem
):
    s, c, h, low, halves, partner, across, others = positions()
    greet([partner, across] + [{"sect": 2 * t + low} for t in others])
    started = []

    def send(src, row, send_sem, recv_sem, device):
        copy = remote(src, o_ref.at[row, c], send_sem, recv_sem, device)
        copy.start()
        started.append(copy)

    for t in others:
        send(x_ref, s, z_send.at[t], z_recv.at[h], {"sect": 2 * t + low})
    send(x_ref, s, y_send.at[h], y_recv.at[h], across)
    send(x_ref, s, p_send.at[s], p_recv.at[s], partner)
    own = pltpu.make_async_copy(x_ref, o_ref.at[s, c], local_sem)
    own.start()
    for t in others:
        row = 2 * t + low
        remote(x_ref, o_ref.at[row, c], z_send.at[t], z_recv.at[t], {"sect": row}).wait_recv()
        send(o_ref.at[row, c], row, y_send.at[t], y_recv.at[t], across)
        send(o_ref.at[row, c], row, p_send.at[row], p_recv.at[row], partner)
    for t in [h] + others:
        row = 2 * t + 1 - low
        remote(x_ref, o_ref.at[row, c], y_send.at[t], y_recv.at[t], across).wait_recv()
        send(o_ref.at[row, c], row, p_send.at[row], p_recv.at[row], partner)
    for t in [h] + others:
        for row in (2 * t + low, 2 * t + 1 - low):
            remote(
                x_ref, o_ref.at[row, 1 - c], p_send.at[row], p_recv.at[row], partner
            ).wait_recv()
    own.wait()
    for copy in started:
        copy.wait_send()

def gather_rows(x, collective_id):
    sects = lax.axis_size("sect")
    heads = lax.axis_size("head")
    halves = sects // 2
    out = pl.pallas_call(
        gather_kernel,
        out_shape=jax.ShapeDtypeStruct((sects, heads) + x.shape, x.dtype),
        in_specs=[VMEM_SPEC],
        out_specs=VMEM_SPEC,
        scratch_shapes=[
            DMA((sects,)),
            DMA((sects,)),
            DMA((halves,)),
            DMA((halves,)),
            DMA((halves,)),
            DMA((halves,)),
            DMA,
        ],
        compiler_params=pltpu.CompilerParams(
            collective_id=collective_id, has_side_effects=True
        ),
        name="gather_rows",
    )(x)
    return out.reshape(-1, x.shape[1])

def reducer(place, mine, sect_of, p_ref, acc, rp, cs, ry, zs, rz, sems):
    s, c, h, low, halves, partner, across, others = place
    p_send, p_recv, y_send, y_recv, z_send, z_recv = sems

    def widen(x):
        return x.astype(jnp.float32)

    def to_partner(t, q, cut):
        return remote(
            p_ref.at[pl.ds(2 * t, 2), 1 - c, :, cut],
            rp.at[t, :, :, cut],
            p_send.at[0],
            p_recv.at[q, t],
            partner,
        )

    def to_across(t, q, cut):
        return remote(
            cs.at[t, :, cut], ry.at[t, :, cut], y_send.at[0], y_recv.at[q, t], across
        )

    def enter(t, q, cut):
        to_partner(t, q, cut).start()

    def cross(t, q, cut):
        to_partner(t, q, cut).wait_recv()
        cs[t, :, cut] = (
            widen(p_ref[2 * t + 1 - low, c, :, cut]) + widen(rp[t, 1 - low, :, cut])
        ).astype(jnp.bfloat16)
        to_across(t, q, cut).start()

    def along(t, q, cut):
        to_across(t, q, cut).wait_recv()
        total = (
            widen(p_ref[2 * t + low, c, :, cut])
            + widen(rp[t, low, :, cut])
            + widen(ry[t, :, cut])
        )
        if t is mine:
            acc[:, cut] = total
        else:
            zs[t, :, cut] = total.astype(jnp.bfloat16)
            remote(
                zs.at[t, :, cut],
                rz.at[mine, :, cut],
                z_send.at[0],
                z_recv.at[q, mine],
                {"sect": sect_of(t)},
            ).start()

    def collect(t, q, cut):
        if t is mine:
            return
        remote(
            zs.at[t, :, cut],
            rz.at[t, :, cut],
            z_send.at[0],
            z_recv.at[q, t],
            {"sect": sect_of(t)},
        ).wait_recv()
        acc[:, cut] += widen(rz[t, :, cut])

    def drain():
        remote(
            p_ref.at[:, 1 - c], p_ref.at[:, c], p_send.at[0], p_recv.at[0, 0], partner
        ).wait_send()
        remote(cs, ry, y_send.at[0], y_recv.at[0, 0], across).wait_send()
        some = pl.ds(0, cs.shape[0] - 1)
        remote(zs.at[some], rz.at[some], z_send.at[0], z_recv.at[0, 0], across).wait_send()

    return enter, cross, along, collect, drain

def layer_kernel(
    groups,
    sects,
    kv_heads,
    q_hbm,
    k_hbm,
    v_hbm,
    seg_hbm,
    proj_ref,
    res_hbm,
    gain_hbm,
    ids_hbm,
    route_hbm,
    gate_hbm,
    up_hbm,
    down_hbm,
    out_ref,
    q_ref,
    seg_ref,
    res_ref,
    gain_ref,
    ids_ref,
    route_ref,
    in_sems,
    gate_ref,
    up_ref,
    down_ref,
    hidden,
    xg,
    acc,
    p_first,
    p_second,
    rp_first,
    rp_second,
    first_bufs,
    cross_bufs,
    row_tx,
    row_pair,
    row_over,
    row_tx_along,
    row_along,
    tx_sems,
    rx_first,
    rx_second,
    z_second,
    w_sems,
    a_ref,
    w_all,
    kv_ref,
    kv_all,
    att,
    bias,
    kz_send,
    kz_recv,
    ky_send,
    ky_recv,
    a_send,
    a_recv,
    w_send,
    w_recv,
    f_send,
    f_recv,
    local_sem,
    own_w_sem,
    own_a_sem,
):
    place = positions()
    s, c, h, low, halves, partner, across, others = place
    g = lax.axis_index("groups")
    experts = lax.axis_size("sect") * lax.axis_size("head")
    moe_rows, width = res_ref.shape
    rows = q_ref.shape[0]
    chunk = 4 * moe_rows
    team = sects // 2
    line = team // 2
    j = lax.rem(s, team)
    base = s - j
    line_at = lax.rem(h, line)
    line_others = [lax.rem(line_at + i, line) for i in range(1, line)]
    sect_peers = [lax.rem(s + i, sects) for i in range(1, sects)]
    group_peers = [lax.rem(g + i, groups) for i in range(1, groups)]

    def teammate(i):
        return base + lax.rem(j + team + i, team)

    def opposite(i):
        return team - base + lax.rem(j + team + i, team)

    half = k_hbm.shape[1]
    own_k = pltpu.make_async_copy(k_hbm, kv_ref.at[:, pl.ds(0, half)], local_sem.at[0])
    own_v = pltpu.make_async_copy(v_hbm, kv_ref.at[:, pl.ds(half, half)], local_sem.at[1])
    own_k.start()
    own_v.start()
    inputs = [
        pltpu.make_async_copy(src, dst, in_sems.at[i])
        for i, (src, dst) in enumerate(
            (
                (seg_hbm, seg_ref),
                (q_hbm, q_ref),
                (res_hbm, res_ref),
                (gain_hbm, gain_ref),
                (ids_hbm, ids_ref),
                (route_hbm, route_ref),
            )
        )
    ]
    for copy in inputs:
        copy.start()
    greet(
        [{"sect": t} for t in sect_peers] + [{"groups": t} for t in group_peers] + [partner]
    )
    started = []

    def send(copy):
        copy.start()
        started.append(copy)

    own_k.wait()
    own_v.wait()

    window = bias.shape[1]
    blocks = window // rows
    first = jnp.maximum(s - (blocks - 1), 0)
    reach = min(blocks // 2, halves - 1)

    def kv_up(i):
        return remote(
            kv_ref, kv_all.at[s], kz_send.at[i], kz_recv.at[i], {"sect": s + 2 * i}
        )

    def kv_over(i):
        row = s - 2 * i
        return remote(
            kv_ref if i == 0 else kv_all.at[row],
            kv_all.at[row],
            ky_send.at[i],
            ky_recv.at[i],
            across,
        )

    for i in range(1, reach + 1):
        pl.when(h + i < halves)(kv_up(i).start)
    kv_over(0).start()
    own_kv = pltpu.make_async_copy(kv_ref, kv_all.at[s], local_sem.at[2])
    own_kv.start()

    pieces, w_rows, w_width = w_all.shape
    part = w_rows // groups
    w_cols = w_width // sects

    def w_piece(t, q):
        start = pl.multiple_of(lax.rem(t, team) * w_rows + g * part, part)
        return proj_ref.at[pl.ds(start, part), pl.ds(q * w_cols, w_cols)]

    def w_place(group, t, q, home=base):
        return w_all.at[
            q,
            pl.ds(pl.multiple_of(group * part, part), part),
            pl.ds(pl.multiple_of(lax.rem(t - home + sects, sects) * w_cols, w_cols), w_cols),
        ]

    def w_side(group):
        return w_all.at[:, pl.ds(pl.multiple_of(group * part, part), part), :]

    def w_half(group, q, which):
        return w_all.at[
            q,
            pl.ds(pl.multiple_of(group * part, part), part),
            pl.ds(which * team * w_cols, team * w_cols),
        ]

    def drain_weight():
        for i, u in enumerate(group_peers):
            remote(
                w_side(g), w_side(u), f_send.at[i], f_recv.at[g, 0, 0], {"groups": u}
            ).wait_send()
        span = pl.ds(0, (sects - 1) * w_cols)
        side = w_all.at[:, pl.ds(0, part), span]
        remote(side, side, w_send.at[0], w_recv.at[0, 0], across).wait_send()

    def own_w(q):
        return pltpu.make_async_copy(w_piece(s, q), w_place(g, s, q), own_w_sem.at[q])

    def start_own(q):
        for i, u in enumerate(group_peers):
            remote(
                w_piece(s, q), w_place(g, s, q), f_send.at[i], f_recv.at[g, q, 0], {"groups": u}
            ).start()
        own_w(q).start()

    def start_weight(q, targets):
        for t in targets:
            remote(
                w_piece(t, q),
                w_place(g, s, q, t - lax.rem(t, team)),
                w_send.at[0],
                w_recv.at[q, s],
                {"sect": t},
            ).start()

    inside = [teammate(i) for i in range(1, team)]
    outside = [opposite(i) for i in range(team)]
    mixed = [outside[0]]
    for i in range(1, team):
        mixed += [inside[i - 1], outside[i]]
    ends = [jnp.where(base > 0, i, halves - 1 - i) for i in range(line)]
    far = [2 * z + y for z in ends for y in (low, 1 - low)]
    w_sources = far[:1] + [teammate(-i) for i in range(1, team)] + far[1:]

    near = [teammate(-i) for i in range(1, team)]

    def inner(t):
        return int(any(t is u for u in near))

    def forward_weight(q, t):
        which = 1 - inner(t)
        remote(
            w_piece(t, q), w_place(g, t, q), w_send.at[0], w_recv.at[q, t], {"sect": t}
        ).wait_recv()
        for i, u in enumerate(group_peers):
            remote(
                w_place(g, t, q),
                w_place(g, t, q),
                f_send.at[i],
                f_recv.at[g, q, which],
                {"groups": u},
            ).start()

    def wait_weight(q, which):
        for u in group_peers:
            remote(
                w_half(g, q, which),
                w_half(u, q, which),
                f_send.at[0],
                f_recv.at[u, q, which],
                {"groups": u},
            ).wait_recv()
        if which == 0:
            own_w(q).wait()

    loads = [
        pltpu.make_async_copy(src.at[0], dst, w_sems.at[i])
        for i, (src, dst) in enumerate(
            ((gate_hbm, gate_ref), (up_hbm, up_ref), (down_hbm, down_ref))
        )
    ]
    for load in loads:
        load.start()

    for q in range(pieces):
        start_own(q)
    start_weight(0, inside)
    start_weight(0, outside)
    for copy in inputs:
        copy.wait()
    row_of = lax.broadcasted_iota(jnp.int32, (rows, rows), 0)
    col_of = lax.broadcasted_iota(jnp.int32, (rows, rows), 1)
    seg_q = jnp.sum(
        jnp.where(row_of == col_of, seg_ref[s].astype(jnp.float32), 0.0), axis=1, keepdims=True
    )
    for b in range(blocks):
        behind = (s - first - b) * rows + row_of - col_of
        same = seg_q == seg_ref[first + b].astype(jnp.float32)
        bias[:, b * rows : (b + 1) * rows] = jnp.where(
            jnp.logical_and(same, behind >= 0), 0.0, MASKED
        )

        @pl.when(first + b > 2 * h + 1)
        def _(b=b):
            kv_all[first + b] = jnp.zeros(kv_all.shape[1:], kv_all.dtype)

    def relay_kv(i):
        remote(
            kv_ref, kv_all.at[s - 2 * i], kz_send.at[i], kz_recv.at[i], across
        ).wait_recv()
        kv_over(i).start()

    for i in range(1, reach + 1):
        pl.when(h - i >= 0)(functools.partial(relay_kv, i))

    def wait_kv(i):
        row = 2 * (h - i) + 1 - low
        remote(kv_ref, kv_all.at[row], ky_send.at[i], ky_recv.at[i], across).wait_recv()

    waiting = [(q, t) for q in range(pieces) for t in near]
    waiting += [(q, t) for q in range(pieces) for t in far]
    for i in range(reach + 1):
        pl.when(h - i >= 0)(functools.partial(wait_kv, i))
    if pieces > 1:
        start_weight(1, inside)
        start_weight(1, outside)
    own_kv.wait()

    scale = 1.0 / math.sqrt(HEAD_WIDTH)
    kv_width = kv_heads * HEAD_WIDTH
    per_kv = q_ref.shape[1] // kv_heads
    per, step_cols = att.shape[1], att.shape[3]
    cols = per * step_cols

    def attend(i):
        t = lax.rem(j + 1 + i // per, team)
        u = lax.rem(i, per)
        at = t * cols + u * step_cols
        kv_head = at // per_kv
        k_col = pl.multiple_of(kv_head * HEAD_WIDTH, HEAD_WIDTH)
        v_col = pl.multiple_of(kv_width + kv_head * HEAD_WIDTH, HEAD_WIDTH)
        span = pl.ds(first, blocks)
        keys = kv_all[span, :, pl.ds(k_col, HEAD_WIDTH)].reshape(window, HEAD_WIDTH)
        vals = kv_all[span, :, pl.ds(v_col, HEAD_WIDTH)].reshape(window, HEAD_WIDTH)
        for k in range(step_cols // HEAD_WIDTH):
            q_col = pl.multiple_of(at + k * HEAD_WIDTH, HEAD_WIDTH)
            q = q_ref[:, pl.ds(q_col, HEAD_WIDTH)]
            scores = lax.dot_general(
                q, keys, (((1,), (1,)), ((), ())), preferred_element_type=jnp.float32
            )
            scores = scores * scale + bias[...]
            top = jnp.max(scores, axis=1, keepdims=True)
            weights = jnp.exp(scores - top).astype(jnp.bfloat16)
            total = jnp.sum(weights.astype(jnp.float32), axis=1, keepdims=True)
            mixed = jnp.dot(weights, vals, preferred_element_type=jnp.float32)
            att[t, u, :, k * HEAD_WIDTH : (k + 1) * HEAD_WIDTH] = (mixed / total).astype(
                jnp.bfloat16
            )

    def a_place(t, u):
        return a_ref.at[
            pl.ds(pl.multiple_of(t * rows, rows), rows),
            pl.ds(pl.multiple_of(u * step_cols, step_cols), step_cols),
        ]

    def a_copy(t, u):
        return remote(
            att.at[t, u], a_place(j, u), a_send.at[0], a_recv.at[j, u], {"sect": base + t}
        )

    def step(i, carry):
        attend(i)
        last = i - 1

        @pl.when(jnp.logical_and(last >= 0, last < (team - 1) * per))
        def _():
            a_copy(lax.rem(j + 1 + last // per, team), lax.rem(last, per)).start()

        return carry

    steps = team * per
    segments = 4 if steps % 4 == 0 else 1
    for i in range(segments):
        lax.fori_loop(i * steps // segments, (i + 1) * steps // segments, step, 0)
        if i + 1 < segments:
            for _ in range(2):
                forward_weight(*waiting.pop(0))
    own_a = [
        pltpu.make_async_copy(att.at[j, u], a_place(j, u), own_a_sem.at[u]) for u in range(per)
    ]
    for copy in own_a:
        copy.start()
    while len(waiting) > (pieces - 1) * len(far):
        forward_weight(*waiting.pop(0))

    for _ in range(min(2, len(waiting))):
        forward_weight(*waiting.pop(0))
    team_peers = [lax.rem(j + i, team) for i in range(1, team)]
    for t in team_peers:
        for u in range(per):
            remote(
                att.at[t, u], a_place(t, u), a_send.at[0], a_recv.at[t, u], across
            ).wait_recv()
    for copy in own_a:
        copy.wait()

    span = team * w_cols

    def project(t, q, cut):
        left = a_ref[pl.ds(pl.multiple_of(t * chunk, chunk), chunk), :]
        which = cut.start // w_width
        at = cut.start - which * w_width
        part = jnp.dot(
            left, w_all[which, :, at : at + span], preferred_element_type=jnp.float32
        )
        p_first[pl.ds(2 * t, 2), :, :, cut] = part.astype(jnp.bfloat16).reshape(
            2, 2, moe_rows, span
        )

    enter, cross, along, collect, drain_first = reducer(
        place,
        line_at,
        lambda t: base + 2 * t + low,
        p_first,
        acc,
        rp_first,
        *[first_bufs.at[k] for k in range(4)],
        [tx_sems.at[pl.ds(0, 1)], rx_first.at[0]]
        + [tx_sems.at[pl.ds(1, 1)], rx_first.at[1]]
        + [tx_sems.at[pl.ds(2, 1)], rx_first.at[2]],
    )
    def items_of(q, which):
        start = q * w_width + which * span
        cut = slice(start, start + span)
        return [(t, 2 * q + which, cut) for t in line_others + [line_at]]

    def begin(items):
        for i, item in enumerate(items):
            project(*item)
            enter(*item)

    def forward(count):
        for _ in range(min(count, len(waiting))):
            forward_weight(*waiting.pop(0))

    behind = []
    for q in range(pieces):
        wait_weight(q, 0)
        behind += items_of(q, 0)
    begin(behind)
    for item in behind:
        cross(*item)
    forward(1)
    for q in range(pieces):
        if q + 1 == pieces:
            forward(len(waiting))
        items = items_of(q, 1)
        wait_weight(q, 1)
        begin(items)
        if q + 1 < pieces:
            for item in items:
                cross(*item)
            behind += items
    n = len(behind)
    for i, item in enumerate(items):
        cross(*item)
        for other in behind[i * n // len(items) : (i + 1) * n // len(items)]:
            along(*other)
    for item in items:
        along(*item)
    for item in behind + items:
        collect(*item)

    def columns(swap):
        order = [(t + swap) % sects for t in range(sects)]
        return jnp.concatenate(
            [
                acc[:, q * w_width + t * w_cols : q * w_width + (t + 1) * w_cols]
                for t in order
                for q in range(pieces)
            ],
            axis=1,
        )

    summed = jnp.where(base == 0, columns(0), columns(team))
    mid = (res_ref[...].astype(jnp.float32) + summed).astype(jnp.bfloat16)
    out_ref[0] = mid
    wide = mid.astype(jnp.float32)
    inverse = lax.rsqrt(jnp.mean(wide * wide, axis=1, keepdims=True) + NORM_EPS)
    normed = wide * inverse * gain_ref[...].astype(jnp.float32).reshape(1, width)
    lanes = xg.shape[3] - width
    lane = lax.broadcasted_iota(jnp.int32, (moe_rows, lanes), 1)
    place_of = lax.broadcasted_iota(jnp.int32, (lanes, moe_rows), 0)
    route = route_ref[...]
    route = route / jnp.sum(route, axis=0, keepdims=True)
    share = jnp.zeros((lanes, moe_rows), jnp.float32)
    for k in range(route.shape[0]):
        ids = ids_ref[k : k + 1, :]
        named = jnp.logical_or(place_of == ids, place_of == ids + experts)
        share = share + jnp.where(named, route[k : k + 1, :], 0.0)
    share = share.T
    high = share.astype(jnp.bfloat16).astype(jnp.float32)
    xg[s, c, :, width:] = jnp.where(lane < experts, high, share - high).astype(jnp.bfloat16)
    xg[s, c, :, :width] = normed.astype(jnp.bfloat16)

    guarded = []
    total = xg.shape[3]
    middle = total // 256 * 128
    row_cuts = [slice(0, middle), slice(middle, total)]

    def hop(t, p, slot, step):
        block = xg.at[2 * t + low, c, :, row_cuts[p]]
        return remote(
            block, block, row_tx_along.at[p, slot], row_along.at[p, t], {"sect": s + step}
        )

    def over(t, p):
        block = xg.at[2 * t + low, c, :, row_cuts[p]]
        return remote(block, block, row_tx.at[0], row_over.at[p, t], across)

    def to_pair(row):
        block = xg.at[row, c]
        remote(block, block, row_tx.at[1], row_pair.at[row], partner).start()

    def from_pair(row):
        block = xg.at[row, 1 - c]
        remote(block, block, row_tx.at[1], row_pair.at[row], partner).wait_recv()

    def from_over(t):
        for p, cut in enumerate(row_cuts):
            block = xg.at[2 * t + 1 - low, c, :, cut]
            remote(block, block, row_tx.at[0], row_over.at[p, t], across).wait_recv()

    paired = jnp.minimum(h, halves - 1 - h)
    away = jnp.where(2 * h < halves - 1, 1, -1)
    order = [h]
    hops = [0]
    for k in range(1, halves):
        near = (k + 1) // 2 * (-1 if k % 2 else 1)
        order.append(h + away * jnp.where(k <= 2 * paired, near, k - paired))
        hops.append(jnp.where(k <= 2 * paired, (k + 1) // 2, k - paired))

    def onward(k, p):
        t = order[k]
        return [
            (jnp.logical_and(t < h, h + 1 < halves), hop(t, p, t, 2)),
            (jnp.logical_and(t > h, h >= 1), hop(t, p, t, -2)),
        ]

    def relay_rows(k):
        t = order[k]
        for p in range(2):
            block = xg.at[2 * t + low, c, :, row_cuts[p]]
            remote(
                block, block, row_tx_along.at[p, t], row_along.at[p, t], across
            ).wait_recv()
            for when, copy in onward(k, p):
                pl.when(when)(copy.start)
            over(t, p).start()
        to_pair(2 * t + low)

    for k in range(1, halves):
        for p in range(2):
            guarded.extend(onward(k, p))

    def relay_step(i):
        for k in range(i + 1, halves):
            if (k + 1) // 2 <= i + 1:
                pl.when(hops[k] == i + 1)(functools.partial(relay_rows, k))

    for p in range(2):
        for when, copy in (
            (h + 1 < halves, hop(h, p, h, 2)),
            (h >= 1, hop(h, p, halves + h, -2)),
        ):
            pl.when(when)(copy.start)
            guarded.append((when, copy))
        over(h, p).start()
    to_pair(s)
    for load in loads:
        load.wait()

    def experts_of(i, t, q, cut):
        if q == 0:
            hidden_of(i, t)
        tile = min(512, width)
        for n in range(cut.start, cut.stop, tile):
            part = jnp.dot(
                hidden[...], down_ref[:, n : n + tile], preferred_element_type=jnp.float32
            )
            p_second[pl.ds(2 * t, 2), :, :, n : n + tile] = (
                (part * own_share(t)).astype(jnp.bfloat16).reshape(2, 2, moe_rows, tile)
            )

    def own_share(t):
        pair = xg[pl.ds(2 * t, 2), :, :, width:].astype(jnp.float32).reshape(chunk, lanes)
        expert = s * 2 + c
        at = lax.broadcasted_iota(jnp.int32, (chunk, lanes), 1)
        mine = jnp.logical_or(at == expert, at == expert + experts)
        return jnp.sum(jnp.where(mine, pair, 0.0), axis=1, keepdims=True)

    def hidden_of(i, t):
        relay_step(i)
        from_over(t)
        to_pair(2 * t + 1 - low)
        for row in (2 * t + low, 2 * t + 1 - low):
            from_pair(row)
        x = xg[pl.ds(2 * t, 2), :, :, :width].reshape(chunk, width)
        step = 256
        for n in range(0, hidden.shape[1], step):
            gate_act = jnp.dot(
                x, gate_ref[:, n : n + step], preferred_element_type=jnp.float32
            )
            up_act = jnp.dot(x, up_ref[:, n : n + step], preferred_element_type=jnp.float32)
            silu = gate_act / (1.0 + jnp.exp(-gate_act))
            hidden[:, n : n + step] = (silu * up_act).astype(jnp.bfloat16)

    cs, ry, zs = [cross_bufs.at[k, pl.ds(0, halves)] for k in range(3)]
    rz = cross_bufs.at[3]
    y_send, y_recv = tx_sems.at[pl.ds(4, 1)], rx_second.at[1]
    z_send, z_recv = tx_sems.at[pl.ds(5, 1)], z_second
    sems = [tx_sems.at[pl.ds(3, 1)], rx_second.at[0], y_send, y_recv, z_send, z_recv]
    enter, cross, _, _, drain_second = reducer(
        place, h, None, p_second, acc, rp_second, cs, ry, zs, rz, sems
    )
    parts = 2 if width % 1024 == 0 else 1
    size = width // parts
    cuts_of = [(q, slice(q * size, (q + 1) * size)) for q in range(parts)]

    def own_sum(t, q, cut):
        return (
            p_second[2 * t + low, c, :, cut].astype(jnp.float32)
            + rp_second[t, low, :, cut].astype(jnp.float32)
            + ry[t, :, cut].astype(jnp.float32)
        )

    def wait_across(t, q, cut):
        remote(
            cs.at[t, :, cut], ry.at[t, :, cut], y_send.at[0], y_recv.at[q, t], across
        ).wait_recv()

    def wait_along(slot, row, t, q, cut):
        remote(
            zs.at[t, :, cut], rz.at[slot, :, cut], z_send.at[0], z_recv.at[row, t], across
        ).wait_recv()

    def chain(t, q, cut):
        wait_across(t, q, cut)
        joined = jnp.where(t > h, h >= 1, h + 1 < halves)

        @pl.when(jnp.logical_not(joined))
        def _():
            zs[t, :, cut] = own_sum(t, q, cut).astype(jnp.bfloat16)

        @pl.when(joined)
        def _():
            wait_along(t, q, t, q, cut)
            zs[t, :, cut] = (
                own_sum(t, q, cut) + rz[t, :, cut].astype(jnp.float32)
            ).astype(jnp.bfloat16)

        landed = h - 1 == t
        remote(
            zs.at[t, :, cut],
            rz.at[jnp.where(landed, halves, t), :, cut],
            z_send.at[0],
            z_recv.at[q + jnp.where(landed, parts, 0), t],
            {"sect": s + jnp.where(t > h, 2, -2)},
        ).start()

    def finish(q, cut):
        wait_across(h, q, cut)
        acc[:, cut] = own_sum(h, q, cut)

        @pl.when(h >= 1)
        def _():
            wait_along(h, q, h, q, cut)
            acc[:, cut] += rz[h, :, cut].astype(jnp.float32)

        @pl.when(h + 1 < halves)
        def _():
            wait_along(halves, q + parts, h, q, cut)
            acc[:, cut] += rz[halves, :, cut].astype(jnp.float32)

    lower = h < halves // 2
    targets = [
        jnp.where(lower, halves // 2 + i, halves // 2 - 1 - i) for i in range(halves // 2)
    ]
    targets += [h - line_at + t for t in line_others]

    def each(step, t):
        for q, cut in cuts_of:
            step(t, q, cut)

    for i, t in enumerate(order):
        for q, cut in cuts_of:
            experts_of(i, t, q, cut)
            enter(t, q, cut)
        if i == halves - 2:
            each(cross, targets[0])
    for i, t in enumerate(targets[1:] + [h]):
        each(cross, t)
        if i < 0:
            each(chain, targets[i])
    for t in targets[0:]:
        each(chain, t)
    for q, cut in cuts_of:
        finish(q, cut)
    out_ref[1] = acc[...].astype(jnp.bfloat16)
    for i in range(1, reach + 1):
        pl.when(h + i < halves)(kv_up(i).wait_send)
    for i in range(reach + 1):
        pl.when(h - i >= 0)(kv_over(i).wait_send)
    some = pl.ds(0, team - 1)
    remote(att.at[some], att.at[some], a_send.at[0], a_recv.at[0, 0], across).wait_send()
    rows_sent = xg.at[pl.ds(0, halves), c]
    remote(rows_sent, rows_sent, row_tx.at[0], row_over.at[0, 0], across).wait_send()
    rows_sent = xg.at[:, c]
    remote(rows_sent, rows_sent, row_tx.at[1], row_pair.at[0], partner).wait_send()
    drain_weight()
    drain_first()
    drain_second()
    for when, copy in guarded:
        pl.when(when)(copy.wait_send)
    for copy in started:
        copy.wait_send()

def fused_layer(
    queries, keys, values, segments, proj, residual, gain, ids, route, gate, up, down
):
    groups = lax.axis_size("groups")
    sects = lax.axis_size("sect")
    heads = lax.axis_size("head")
    rows = queries.shape[0]
    team = sects // 2
    cols = queries.shape[1] // team
    step_cols = min(cols, 4 * HEAD_WIDTH)
    per = cols // step_cols
    pieces = 2 if proj.shape[1] % 256 == 0 else 1
    w_rows = proj.shape[0] // team
    blocks = min(sects, -(-segments.shape[0] // (2 * rows)) + 1)
    halves = sects // 2
    block = residual.shape
    lanes = -(-2 * sects * heads // 128) * 128
    bf16 = jnp.bfloat16
    kv_shape = (rows, 2 * keys.shape[1])
    operands = (
        queries,
        keys,
        values,
        segments.reshape(sects, 1, rows),
        proj,
        residual,
        gain,
        ids.T,
        route.T,
        gate,
        up,
        down,
    )
    both = pl.pallas_call(
        functools.partial(layer_kernel, groups, sects, keys.shape[1] // HEAD_WIDTH),
        out_shape=jax.ShapeDtypeStruct((2,) + block, bf16),
        in_specs=[pl.BlockSpec(memory_space=pltpu.HBM)] * len(operands),
        out_specs=VMEM_SPEC,
        scratch_shapes=[
            pltpu.VMEM(queries.shape, bf16),
            pltpu.VMEM((sects, 1, rows), jnp.int32),
            pltpu.VMEM(block, bf16),
            pltpu.VMEM(gain.shape, bf16),
            pltpu.VMEM(ids.shape[::-1], jnp.int32),
            pltpu.VMEM(route.shape[::-1], jnp.float32),
            DMA((6,)),
            pltpu.VMEM(gate.shape[1:], bf16),
            pltpu.VMEM(up.shape[1:], bf16),
            pltpu.VMEM(down.shape[1:], bf16),
            pltpu.VMEM((4 * block[0], gate.shape[2]), bf16),
            pltpu.VMEM((sects, heads, block[0], block[1] + lanes), bf16),
            pltpu.VMEM(block, jnp.float32),
            pltpu.VMEM((team, heads) + block, bf16),
            pltpu.VMEM((sects, heads) + block, bf16),
            pltpu.VMEM((team // 2, 2) + block, bf16),
            pltpu.VMEM((halves, 2) + block, bf16),
            pltpu.VMEM((4, team // 2) + block, bf16),
            pltpu.VMEM((4, halves + 1) + block, bf16),
            DMA((2,)),
            DMA((sects,)),
            DMA((2, halves)),
            DMA((2, sects)),
            DMA((2, halves)),
            DMA((6,)),
            DMA((3, 2 * pieces, team // 2)),
            DMA((2, 2, halves)),
            DMA((4, halves)),
            DMA((3,)),
            pltpu.VMEM((rows * team, cols), bf16),
            pltpu.VMEM((pieces, w_rows, proj.shape[1] // pieces * sects), bf16),
            pltpu.VMEM(kv_shape, bf16),
            pltpu.VMEM((sects,) + kv_shape, bf16),
            pltpu.VMEM((team, per, rows, step_cols), bf16),
            pltpu.VMEM((rows, blocks * rows), jnp.float32),
            DMA((halves,)),
            DMA((halves,)),
            DMA((halves,)),
            DMA((halves,)),
            DMA((1,)),
            DMA((team, per)),
            DMA((1,)),
            DMA((pieces, sects)),
            DMA((groups,)),
            DMA((groups, pieces, 2)),
            DMA((3,)),
            DMA((pieces,)),
            DMA((per,)),
        ],
        compiler_params=pltpu.CompilerParams(
            collective_id=4, has_side_effects=True, vmem_limit_bytes=LAYER_ROOM
        ),
        name="layer",
    )(*[pltpu.with_memory_space_constraint(x, pltpu.HBM) for x in operands])
    return both[0], both[1]

def shards(
    queries,
    packed_key_rows,
    values,
    segments,
    proj_weight,
    residual,
    norm_gain,
    expert_ids,
    route_weights,
    gate_weight,
    up_weight,
    down_weight,
):
    sects = lax.axis_size("sect")
    heads = lax.axis_size("head")
    s = lax.axis_index("sect")
    c = lax.axis_index("head")
    experts = sects * heads
    moe_rows, width = residual.shape
    fits = experts * moe_rows * width * 24 <= VMEM_ROOM
    if fits and sects % 4 == 0 and proj_weight.shape[1] % 128 == 0:
        return fused_layer(
            queries,
            packed_key_rows,
            values,
            segments,
            proj_weight,
            residual,
            norm_gain,
            expert_ids,
            route_weights,
            gate_weight,
            up_weight,
            down_weight,
        )
    attended, weight = exchange_attention(
        queries, packed_key_rows, values, segments, proj_weight
    )
    partial_rows = jnp.dot(attended, weight, preferred_element_type=jnp.float32)
    projected = sum_scatter(partial_rows.astype(jnp.bfloat16), moe_rows, 1)

    hidden_mid = (residual.astype(jnp.float32) + projected).astype(jnp.bfloat16)
    mid_float = lax.optimization_barrier(hidden_mid).astype(jnp.float32)
    inverse = lax.rsqrt(jnp.mean(mid_float * mid_float, axis=1, keepdims=True) + NORM_EPS)
    normed = (mid_float * inverse * norm_gain.astype(jnp.float32)[None, :]).astype(jnp.bfloat16)

    route_share = route_weights / jnp.sum(route_weights, axis=1, keepdims=True)
    named = expert_ids[:, :, None] == jnp.arange(experts, dtype=jnp.int32)[None, None, :]
    share = jnp.sum(jnp.where(named, route_share[:, :, None], 0.0), axis=1)
    share_high = lax.reduce_precision(share, 8, 7)
    share_low = (share - share_high).astype(jnp.bfloat16)
    pad = -(2 * experts) % 128
    sent = jnp.concatenate(
        [
            normed,
            share_high.astype(jnp.bfloat16),
            share_low,
            jnp.zeros((moe_rows, pad), jnp.bfloat16),
        ],
        axis=1,
    )
    gathered = gather_rows(sent, 2)
    expert = s * heads + c
    all_rows = gathered[:, :width]
    pair = gathered[:, width:].astype(jnp.float32)
    lane = jnp.arange(pair.shape[1], dtype=jnp.int32)[None, :]
    mine = jnp.logical_or(lane == expert, lane == expert + experts)
    own_share = jnp.sum(jnp.where(mine, pair, 0.0), axis=1, keepdims=True)
    gate_act = jnp.dot(all_rows, gate_weight[0], preferred_element_type=jnp.float32)
    up_act = jnp.dot(all_rows, up_weight[0], preferred_element_type=jnp.float32)
    hidden = (jax.nn.silu(gate_act) * up_act).astype(jnp.bfloat16)
    result = jnp.dot(hidden, down_weight[0], preferred_element_type=jnp.float32)
    mixed = (result * own_share).astype(jnp.bfloat16)
    mixture = sum_scatter(mixed, moe_rows, 3)
    return (hidden_mid, mixture.astype(jnp.bfloat16))

def solution(mesh):
    rows = P(("groups", "sect", "head"), None)
    split = P(("groups", "sect"), "head")
    expert = P(("sect", "head"), None, None)
    placed = (
        split,
        split,
        split,
        P("groups"),
        P("head", "sect"),
        rows,
        P(),
        rows,
        rows,
        expert,
        expert,
        expert,
    )
    return jax.shard_map(
        shards, mesh=mesh, in_specs=placed, out_specs=(rows, rows), check_vma=False
    )
```

```python
import functools
import math

import jax
import jax.numpy as jnp
from jax import lax
from jax.experimental import pallas as pl
from jax.experimental.pallas import tpu as pltpu
from jax.sharding import PartitionSpec as P

HEAD_WIDTH = 128
MASKED = -1e30
NORM_EPS = 1e-06
VMEM_ROOM = 64 << 20
LAYER_ROOM = 52 << 20

MESH = pl.DeviceIdType.MESH
VMEM_SPEC = pl.BlockSpec(memory_space=pltpu.VMEM)
ANY_SPEC = pl.BlockSpec(memory_space=pl.ANY)
DMA = pltpu.SemaphoreType.DMA

def greet(devices):
    barrier = pltpu.get_barrier_semaphore()
    for device in devices:
        pl.semaphore_signal(barrier, inc=1, device_id=device, device_id_type=MESH)
    pl.semaphore_wait(barrier, len(devices))

def remote(src, dst, send_sem, recv_sem, device):
    return pltpu.make_async_remote_copy(
        src_ref=src,
        dst_ref=dst,
        send_sem=send_sem,
        recv_sem=recv_sem,
        device_id=device,
        device_id_type=MESH,
    )

def attention_body(
    extra,
    groups,
    sects,
    kv_heads,
    q_ref,
    k_ref,
    v_ref,
    seg_ref,
    w_ref,
    a_out,
    w_out,
    kv_ref,
    kv_all,
    att,
    bias,
    kz_send,
    kz_recv,
    ky_send,
    ky_recv,
    a_send,
    a_recv,
    w_send,
    w_recv,
    f_send,
    f_recv,
    local_sem,
):
    g = lax.axis_index("groups")
    s = lax.axis_index("sect")
    halves = sects // 2
    h = s // 2
    low = lax.rem(s, 2)
    rows = q_ref.shape[0]
    cols = q_ref.shape[1] // sects
    w_cols = w_ref.shape[1]
    w_rows = w_ref.shape[0] // sects
    part = w_rows // groups
    other_y = 2 * h + 1 - low
    sect_peers = [lax.rem(s + i, sects) for i in range(1, sects)]
    group_peers = [lax.rem(g + i, groups) for i in range(1, groups)]
    half = k_ref.shape[1]
    own_k = pltpu.make_async_copy(k_ref, kv_ref.at[:, pl.ds(0, half)], local_sem.at[3])
    own_v = pltpu.make_async_copy(v_ref, kv_ref.at[:, pl.ds(half, half)], local_sem.at[4])
    own_k.start()
    own_v.start()
    greet(
        [{"sect": t} for t in sect_peers] + [{"groups": t} for t in group_peers] + extra
    )
    started = []
    own_k.wait()
    own_v.wait()

    def kv_cross(t):
        return remote(
            kv_ref if t is None else kv_all.at[2 * t + low],
            kv_all.at[s if t is None else 2 * t + low],
            ky_send.at[h if t is None else t],
            ky_recv.at[h if t is None else t],
            {"sect": other_y},
        )

    for i in range(1, halves):
        t = lax.rem(h + i, halves)
        copy = remote(
            kv_ref, kv_all.at[s], kz_send.at[t], kz_recv.at[h], {"sect": 2 * t + low}
        )
        copy.start()
        started.append(copy)
    copy = kv_cross(None)
    copy.start()
    started.append(copy)
    own_kv = pltpu.make_async_copy(kv_ref, kv_all.at[s], local_sem.at[0])
    own_kv.start()

    def w_piece(t):
        return w_ref.at[pl.ds(pl.multiple_of(t * w_rows + g * part, part), part), :]

    def w_place(group, t):
        span = pl.ds(pl.multiple_of(group * part, part), part)
        if len(w_out.shape) == 3:
            return w_out.at[t, span, :]
        return w_out.at[span, pl.ds(pl.multiple_of(t * w_cols, w_cols), w_cols)]

    for t in sect_peers:
        copy = remote(
            w_piece(t), w_place(g, s), w_send.at[t], w_recv.at[s], {"sect": t}
        )
        copy.start()
        started.append(copy)
    own_w = pltpu.make_async_copy(w_piece(s), w_place(g, s), local_sem.at[1])
    own_w.start()
    for i, t in enumerate(group_peers):
        copy = remote(
            w_piece(s), w_place(g, s), f_send.at[i, s], f_recv.at[g, s], {"groups": t}
        )
        copy.start()
        started.append(copy)

    for i in range(1, halves):
        t = lax.rem(h + i, halves)
        remote(
            kv_ref, kv_all.at[2 * t + low], kz_send.at[t], kz_recv.at[t], {"sect": 2 * t + low}
        ).wait_recv()
        copy = kv_cross(t)
        copy.start()
        started.append(copy)

    window = bias.shape[1]
    blocks = window // rows
    first = jnp.maximum(s - (blocks - 1), 0)
    row_of = lax.broadcasted_iota(jnp.int32, (rows, rows), 0)
    col_of = lax.broadcasted_iota(jnp.int32, (rows, rows), 1)
    seg_q = jnp.sum(
        jnp.where(row_of == col_of, seg_ref[s].astype(jnp.float32), 0.0), axis=1, keepdims=True
    )
    for b in range(blocks):
        behind = (s - first - b) * rows + row_of - col_of
        same = seg_q == seg_ref[first + b].astype(jnp.float32)
        bias[:, b * rows : (b + 1) * rows] = jnp.where(
            jnp.logical_and(same, behind >= 0), 0.0, MASKED
        )

    for i in range(halves):
        t = lax.rem(h + i, halves)
        remote(
            kv_ref, kv_all.at[2 * t + 1 - low], ky_send.at[t], ky_recv.at[t], {"sect": other_y}
        ).wait_recv()
    own_kv.wait()

    scale = 1.0 / math.sqrt(HEAD_WIDTH)
    kv_width = kv_heads * HEAD_WIDTH
    per_kv = q_ref.shape[1] // kv_heads

    def attend(i, carry):
        t = lax.rem(s + 1 + i, sects)
        kv_head = (t * cols) // per_kv
        k_col = pl.multiple_of(kv_head * HEAD_WIDTH, HEAD_WIDTH)
        v_col = pl.multiple_of(kv_width + kv_head * HEAD_WIDTH, HEAD_WIDTH)
        span = pl.ds(first, blocks)
        keys = kv_all[span, :, pl.ds(k_col, HEAD_WIDTH)].reshape(window, HEAD_WIDTH)
        vals = kv_all[span, :, pl.ds(v_col, HEAD_WIDTH)].reshape(window, HEAD_WIDTH)
        for j in range(cols // HEAD_WIDTH):
            q_col = pl.multiple_of(t * cols + j * HEAD_WIDTH, HEAD_WIDTH)
            q = q_ref[:, pl.ds(q_col, HEAD_WIDTH)]
            scores = lax.dot_general(
                q, keys, (((1,), (1,)), ((), ())), preferred_element_type=jnp.float32
            )
            scores = scores * scale + bias[...]
            top = jnp.max(scores, axis=1, keepdims=True)
            weights = jnp.exp(scores - top).astype(jnp.bfloat16)
            total = jnp.sum(weights.astype(jnp.float32), axis=1, keepdims=True)
            mixed = jnp.dot(weights, vals, preferred_element_type=jnp.float32)
            att[t, :, j * HEAD_WIDTH : (j + 1) * HEAD_WIDTH] = (mixed / total).astype(
                jnp.bfloat16
            )
        return carry

    def a_place(t):
        return a_out.at[pl.ds(pl.multiple_of(t * rows, rows), rows), :]

    def a_copy(t):
        return remote(att.at[t], a_place(s), a_send.at[t], a_recv.at[s], {"sect": t})

    def step(i, carry):
        attend(i, carry)

        @pl.when(i >= 1)
        def _():
            a_copy(lax.rem(s + i, sects)).start()

        return carry

    lax.fori_loop(0, sects, step, 0)
    own_a = pltpu.make_async_copy(att.at[s], a_place(s), local_sem.at[2])
    own_a.start()

    for t in sect_peers:
        remote(
            w_piece(s), w_place(g, t), w_send.at[t], w_recv.at[t], {"sect": t}
        ).wait_recv()
        for i, u in enumerate(group_peers):
            copy = remote(
                w_place(g, t), w_place(g, t), f_send.at[i, t], f_recv.at[g, t], {"groups": u}
            )
            copy.start()
            started.append(copy)

    def wait_rows(t):
        remote(att.at[t], a_place(t), a_send.at[t], a_recv.at[t], {"sect": t}).wait_recv()

    def wait_weight():
        for u in group_peers:
            for t in [s] + sect_peers:
                remote(
                    w_place(g, t),
                    w_place(u, t),
                    f_send.at[0, t],
                    f_recv.at[u, t],
                    {"groups": u},
                ).wait_recv()
        own_w.wait()

    def drain():
        for copy in started:
            copy.wait_send()
        for t in sect_peers:
            a_copy(t).wait_send()

    return sect_peers, wait_rows, wait_weight, own_a.wait, drain

def attention_kernel(*arguments):
    sect_peers, wait_rows, wait_weight, wait_own, drain = attention_body([], *arguments)
    for t in sect_peers:
        wait_rows(t)
    wait_weight()
    wait_own()
    drain()

def attention_scratch(groups, sects, rows, cols, kv_shape, window):
    return [
        pltpu.VMEM(kv_shape, jnp.bfloat16),
        pltpu.VMEM((sects,) + kv_shape, jnp.bfloat16),
        pltpu.VMEM((sects, rows, cols), jnp.bfloat16),
        pltpu.VMEM((rows, window), jnp.float32),
        DMA((sects // 2,)),
        DMA((sects // 2,)),
        DMA((sects // 2,)),
        DMA((sects // 2,)),
        DMA((sects,)),
        DMA((sects,)),
        DMA((sects,)),
        DMA((sects,)),
        DMA((groups, sects)),
        DMA((groups, sects)),
        DMA((5,)),
    ]

def exchange_attention(queries, keys, values, segments, proj_weight):
    kv_heads = keys.shape[1] // HEAD_WIDTH
    groups = lax.axis_size("groups")
    sects = lax.axis_size("sect")
    rows, width = queries.shape
    cols = width // sects
    w_rows = proj_weight.shape[0] // sects
    w_cols = proj_weight.shape[1]
    blocks = min(sects, -(-segments.shape[0] // (2 * rows)) + 1)
    kv_shape = (rows, 2 * keys.shape[1])
    aligned = w_cols % 128 == 0
    w_shape = (w_rows, w_cols * sects) if aligned else (sects, w_rows, w_cols)
    attended, weight = pl.pallas_call(
        functools.partial(attention_kernel, groups, sects, kv_heads),
        out_shape=(
            jax.ShapeDtypeStruct((rows * sects, cols), jnp.bfloat16),
            jax.ShapeDtypeStruct(w_shape, jnp.bfloat16),
        ),
        in_specs=[VMEM_SPEC, VMEM_SPEC, VMEM_SPEC, VMEM_SPEC, ANY_SPEC],
        out_specs=(ANY_SPEC, ANY_SPEC),
        scratch_shapes=attention_scratch(groups, sects, rows, cols, kv_shape, blocks * rows),
        compiler_params=pltpu.CompilerParams(collective_id=0, has_side_effects=True),
        name="attention",
    )(queries, keys, values, segments.reshape(sects, 1, rows), proj_weight)
    if not aligned:
        weight = weight.transpose(1, 0, 2).reshape(w_rows, w_cols * sects)
    return attended, weight

def positions():
    s = lax.axis_index("sect")
    c = lax.axis_index("head")
    halves = lax.axis_size("sect") // 2
    h = s // 2
    low = lax.rem(s, 2)
    partner = {"head": 1 - c}
    across = {"sect": 2 * h + 1 - low}
    others = [lax.rem(h + i, halves) for i in range(1, halves)]
    return s, c, h, low, halves, partner, across, others

def sum_kernel(
    p_ref, o_ref, rp, cs, ry, zs, rz, p_send, p_recv, y_send, y_recv, z_send, z_recv
):
    s, c, h, low, halves, partner, across, others = positions()
    greet([partner, across] + [{"sect": 2 * t + low} for t in others])
    order = others + [h]
    started = []

    def widen(x):
        return x.astype(jnp.float32)

    for t in order:
        copy = remote(
            p_ref.at[pl.ds(2 * t, 2), 1 - c], rp.at[t], p_send.at[t], p_recv.at[t], partner
        )
        copy.start()
        started.append(copy)
    for t in order:
        remote(
            p_ref.at[pl.ds(2 * t, 2), 1 - c], rp.at[t], p_send.at[t], p_recv.at[t], partner
        ).wait_recv()
        cs[t] = (widen(p_ref[2 * t + 1 - low, c]) + widen(rp[t, 1 - low])).astype(jnp.bfloat16)
        copy = remote(cs.at[t], ry.at[t], y_send.at[t], y_recv.at[t], across)
        copy.start()
        started.append(copy)
    for t in order:
        remote(cs.at[t], ry.at[t], y_send.at[t], y_recv.at[t], across).wait_recv()
        total = widen(p_ref[2 * t + low, c]) + widen(rp[t, low]) + widen(ry[t])
        if t is h:
            o_ref[...] = total
        else:
            zs[t] = total.astype(jnp.bfloat16)
            copy = remote(
                zs.at[t], rz.at[h], z_send.at[t], z_recv.at[h], {"sect": 2 * t + low}
            )
            copy.start()
            started.append(copy)
    for t in others:
        remote(
            zs.at[t], rz.at[t], z_send.at[t], z_recv.at[t], {"sect": 2 * t + low}
        ).wait_recv()
        o_ref[...] += widen(rz[t])
    for copy in started:
        copy.wait_send()

def sum_scatter(partial_rows, moe_rows, collective_id):
    sects = lax.axis_size("sect")
    heads = lax.axis_size("head")
    width = partial_rows.shape[1]
    halves = sects // 2
    block = (moe_rows, width)
    return pl.pallas_call(
        sum_kernel,
        out_shape=jax.ShapeDtypeStruct(block, jnp.float32),
        in_specs=[VMEM_SPEC],
        out_specs=VMEM_SPEC,
        scratch_shapes=[
            pltpu.VMEM((halves, 2) + block, jnp.bfloat16),
            pltpu.VMEM((halves,) + block, jnp.bfloat16),
            pltpu.VMEM((halves,) + block, jnp.bfloat16),
            pltpu.VMEM((halves,) + block, jnp.bfloat16),
            pltpu.VMEM((halves,) + block, jnp.bfloat16),
        ]
        + [DMA((halves,))] * 6,
        compiler_params=pltpu.CompilerParams(
            collective_id=collective_id, has_side_effects=True
        ),
        name="sum_scatter",
    )(partial_rows.reshape((sects, heads) + block))

def gather_kernel(
    x_ref, o_ref, p_send, p_recv, y_send, y_recv, z_send, z_recv, local_sem
):
    s, c, h, low, halves, partner, across, others = positions()
    greet([partner, across] + [{"sect": 2 * t + low} for t in others])
    started = []

    def send(src, row, send_sem, recv_sem, device):
        copy = remote(src, o_ref.at[row, c], send_sem, recv_sem, device)
        copy.start()
        started.append(copy)

    for t in others:
        send(x_ref, s, z_send.at[t], z_recv.at[h], {"sect": 2 * t + low})
    send(x_ref, s, y_send.at[h], y_recv.at[h], across)
    send(x_ref, s, p_send.at[s], p_recv.at[s], partner)
    own = pltpu.make_async_copy(x_ref, o_ref.at[s, c], local_sem)
    own.start()
    for t in others:
        row = 2 * t + low
        remote(x_ref, o_ref.at[row, c], z_send.at[t], z_recv.at[t], {"sect": row}).wait_recv()
        send(o_ref.at[row, c], row, y_send.at[t], y_recv.at[t], across)
        send(o_ref.at[row, c], row, p_send.at[row], p_recv.at[row], partner)
    for t in [h] + others:
        row = 2 * t + 1 - low
        remote(x_ref, o_ref.at[row, c], y_send.at[t], y_recv.at[t], across).wait_recv()
        send(o_ref.at[row, c], row, p_send.at[row], p_recv.at[row], partner)
    for t in [h] + others:
        for row in (2 * t + low, 2 * t + 1 - low):
            remote(
                x_ref, o_ref.at[row, 1 - c], p_send.at[row], p_recv.at[row], partner
            ).wait_recv()
    own.wait()
    for copy in started:
        copy.wait_send()

def gather_rows(x, collective_id):
    sects = lax.axis_size("sect")
    heads = lax.axis_size("head")
    halves = sects // 2
    out = pl.pallas_call(
        gather_kernel,
        out_shape=jax.ShapeDtypeStruct((sects, heads) + x.shape, x.dtype),
        in_specs=[VMEM_SPEC],
        out_specs=VMEM_SPEC,
        scratch_shapes=[
            DMA((sects,)),
            DMA((sects,)),
            DMA((halves,)),
            DMA((halves,)),
            DMA((halves,)),
            DMA((halves,)),
            DMA,
        ],
        compiler_params=pltpu.CompilerParams(
            collective_id=collective_id, has_side_effects=True
        ),
        name="gather_rows",
    )(x)
    return out.reshape(-1, x.shape[1])

def reducer(place, mine, sect_of, p_ref, acc, rp, cs, ry, zs, rz, sems):
    s, c, h, low, halves, partner, across, others = place
    p_send, p_recv, y_send, y_recv, z_send, z_recv = sems

    def widen(x):
        return x.astype(jnp.float32)

    def to_partner(t, q, cut):
        return remote(
            p_ref.at[pl.ds(2 * t, 2), 1 - c, :, cut],
            rp.at[t, :, :, cut],
            p_send.at[0],
            p_recv.at[q, t],
            partner,
        )

    def to_across(t, q, cut):
        return remote(
            cs.at[t, :, cut], ry.at[t, :, cut], y_send.at[0], y_recv.at[q, t], across
        )

    def enter(t, q, cut):
        to_partner(t, q, cut).start()

    def cross(t, q, cut):
        to_partner(t, q, cut).wait_recv()
        cs[t, :, cut] = (
            widen(p_ref[2 * t + 1 - low, c, :, cut]) + widen(rp[t, 1 - low, :, cut])
        ).astype(jnp.bfloat16)
        to_across(t, q, cut).start()

    def along(t, q, cut):
        to_across(t, q, cut).wait_recv()
        total = (
            widen(p_ref[2 * t + low, c, :, cut])
            + widen(rp[t, low, :, cut])
            + widen(ry[t, :, cut])
        )
        if t is mine:
            acc[:, cut] = total
        else:
            zs[t, :, cut] = total.astype(jnp.bfloat16)
            remote(
                zs.at[t, :, cut],
                rz.at[mine, :, cut],
                z_send.at[0],
                z_recv.at[q, mine],
                {"sect": sect_of(t)},
            ).start()

    def collect(t, q, cut):
        if t is mine:
            return
        remote(
            zs.at[t, :, cut],
            rz.at[t, :, cut],
            z_send.at[0],
            z_recv.at[q, t],
            {"sect": sect_of(t)},
        ).wait_recv()
        acc[:, cut] += widen(rz[t, :, cut])

    def drain():
        remote(
            p_ref.at[:, 1 - c], p_ref.at[:, c], p_send.at[0], p_recv.at[0, 0], partner
        ).wait_send()
        remote(cs, ry, y_send.at[0], y_recv.at[0, 0], across).wait_send()
        some = pl.ds(0, cs.shape[0] - 1)
        remote(zs.at[some], rz.at[some], z_send.at[0], z_recv.at[0, 0], across).wait_send()

    return enter, cross, along, collect, drain

def layer_kernel(
    groups,
    sects,
    kv_heads,
    q_hbm,
    k_hbm,
    v_hbm,
    seg_hbm,
    proj_ref,
    res_hbm,
    gain_hbm,
    ids_hbm,
    route_hbm,
    gate_hbm,
    up_hbm,
    down_hbm,
    out_ref,
    q_ref,
    seg_ref,
    res_ref,
    gain_ref,
    ids_ref,
    route_ref,
    in_sems,
    gate_ref,
    up_ref,
    down_ref,
    hidden,
    xg,
    acc,
    p_first,
    p_second,
    rp_first,
    rp_second,
    first_bufs,
    cross_bufs,
    row_tx,
    row_pair,
    row_over,
    row_tx_along,
    row_along,
    tx_sems,
    rx_first,
    rx_second,
    z_second,
    w_sems,
    a_ref,
    w_all,
    kv_ref,
    kv_all,
    att,
    bias,
    kz_send,
    kz_recv,
    ky_send,
    ky_recv,
    a_send,
    a_recv,
    w_send,
    w_recv,
    f_send,
    f_recv,
    local_sem,
    own_w_sem,
    own_a_sem,
):
    place = positions()
    s, c, h, low, halves, partner, across, others = place
    g = lax.axis_index("groups")
    experts = lax.axis_size("sect") * lax.axis_size("head")
    moe_rows, width = res_ref.shape
    rows = q_ref.shape[0]
    chunk = 4 * moe_rows
    team = sects // 2
    line = team // 2
    j = lax.rem(s, team)
    base = s - j
    line_at = lax.rem(h, line)
    line_others = [lax.rem(line_at + i, line) for i in range(1, line)]
    sect_peers = [lax.rem(s + i, sects) for i in range(1, sects)]
    group_peers = [lax.rem(g + i, groups) for i in range(1, groups)]

    def teammate(i):
        return base + lax.rem(j + team + i, team)

    def opposite(i):
        return team - base + lax.rem(j + team + i, team)

    half = k_hbm.shape[1]
    own_k = pltpu.make_async_copy(k_hbm, kv_ref.at[:, pl.ds(0, half)], local_sem.at[0])
    own_v = pltpu.make_async_copy(v_hbm, kv_ref.at[:, pl.ds(half, half)], local_sem.at[1])
    own_k.start()
    own_v.start()
    inputs = [
        pltpu.make_async_copy(src, dst, in_sems.at[i])
        for i, (src, dst) in enumerate(
            (
                (seg_hbm, seg_ref),
                (q_hbm, q_ref),
                (res_hbm, res_ref),
                (gain_hbm, gain_ref),
                (ids_hbm, ids_ref),
                (route_hbm, route_ref),
            )
        )
    ]
    for copy in inputs:
        copy.start()
    greet(
        [{"sect": t} for t in sect_peers] + [{"groups": t} for t in group_peers] + [partner]
    )
    started = []

    def send(copy):
        copy.start()
        started.append(copy)

    own_k.wait()
    own_v.wait()

    window = bias.shape[1]
    blocks = window // rows
    first = jnp.maximum(s - (blocks - 1), 0)
    reach = min(blocks // 2, halves - 1)

    def kv_up(i):
        return remote(
            kv_ref, kv_all.at[s], kz_send.at[i], kz_recv.at[i], {"sect": s + 2 * i}
        )

    def kv_over(i):
        row = s - 2 * i
        return remote(
            kv_ref if i == 0 else kv_all.at[row],
            kv_all.at[row],
            ky_send.at[i],
            ky_recv.at[i],
            across,
        )

    for i in range(1, reach + 1):
        pl.when(h + i < halves)(kv_up(i).start)
    kv_over(0).start()
    own_kv = pltpu.make_async_copy(kv_ref, kv_all.at[s], local_sem.at[2])
    own_kv.start()

    pieces, w_rows, w_width = w_all.shape
    part = w_rows // groups
    w_cols = w_width // sects

    def w_piece(t, q):
        start = pl.multiple_of(lax.rem(t, team) * w_rows + g * part, part)
        return proj_ref.at[pl.ds(start, part), pl.ds(q * w_cols, w_cols)]

    def w_place(group, t, q, home=base):
        return w_all.at[
            q,
            pl.ds(pl.multiple_of(group * part, part), part),
            pl.ds(pl.multiple_of(lax.rem(t - home + sects, sects) * w_cols, w_cols), w_cols),
        ]

    def w_side(group):
        return w_all.at[:, pl.ds(pl.multiple_of(group * part, part), part), :]

    def w_half(group, q, which):
        return w_all.at[
            q,
            pl.ds(pl.multiple_of(group * part, part), part),
            pl.ds(which * team * w_cols, team * w_cols),
        ]

    def drain_weight():
        for i, u in enumerate(group_peers):
            remote(
                w_side(g), w_side(u), f_send.at[i], f_recv.at[g, 0, 0], {"groups": u}
            ).wait_send()
        span = pl.ds(0, (sects - 1) * w_cols)
        side = w_all.at[:, pl.ds(0, part), span]
        remote(side, side, w_send.at[0], w_recv.at[0, 0], across).wait_send()

    def own_w(q):
        return pltpu.make_async_copy(w_piece(s, q), w_place(g, s, q), own_w_sem.at[q])

    def start_own(q):
        for i, u in enumerate(group_peers):
            remote(
                w_piece(s, q), w_place(g, s, q), f_send.at[i], f_recv.at[g, q, 0], {"groups": u}
            ).start()
        own_w(q).start()

    def start_weight(q, targets):
        for t in targets:
            remote(
                w_piece(t, q),
                w_place(g, s, q, t - lax.rem(t, team)),
                w_send.at[0],
                w_recv.at[q, s],
                {"sect": t},
            ).start()

    inside = [teammate(i) for i in range(1, team)]
    outside = [opposite(i) for i in range(team)]
    mixed = [outside[0]]
    for i in range(1, team):
        mixed += [inside[i - 1], outside[i]]
    ends = [jnp.where(base > 0, i, halves - 1 - i) for i in range(line)]
    far = [2 * z + y for z in ends for y in (low, 1 - low)]
    w_sources = far[:1] + [teammate(-i) for i in range(1, team)] + far[1:]

    near = [teammate(-i) for i in range(1, team)]

    def inner(t):
        return int(any(t is u for u in near))

    def forward_weight(q, t):
        which = 1 - inner(t)
        remote(
            w_piece(t, q), w_place(g, t, q), w_send.at[0], w_recv.at[q, t], {"sect": t}
        ).wait_recv()
        for i, u in enumerate(group_peers):
            remote(
                w_place(g, t, q),
                w_place(g, t, q),
                f_send.at[i],
                f_recv.at[g, q, which],
                {"groups": u},
            ).start()

    def wait_weight(q, which):
        for u in group_peers:
            remote(
                w_half(g, q, which),
                w_half(u, q, which),
                f_send.at[0],
                f_recv.at[u, q, which],
                {"groups": u},
            ).wait_recv()
        if which == 0:
            own_w(q).wait()

    loads = [
        pltpu.make_async_copy(src.at[0], dst, w_sems.at[i])
        for i, (src, dst) in enumerate(
            ((gate_hbm, gate_ref), (up_hbm, up_ref), (down_hbm, down_ref))
        )
    ]
    for load in loads:
        load.start()

    for q in range(pieces):
        start_own(q)
    start_weight(0, inside)
    start_weight(0, outside)
    for copy in inputs:
        copy.wait()
    row_of = lax.broadcasted_iota(jnp.int32, (rows, rows), 0)
    col_of = lax.broadcasted_iota(jnp.int32, (rows, rows), 1)
    seg_q = jnp.sum(
        jnp.where(row_of == col_of, seg_ref[s].astype(jnp.float32), 0.0), axis=1, keepdims=True
    )
    for b in range(blocks):
        behind = (s - first - b) * rows + row_of - col_of
        same = seg_q == seg_ref[first + b].astype(jnp.float32)
        bias[:, b * rows : (b + 1) * rows] = jnp.where(
            jnp.logical_and(same, behind >= 0), 0.0, MASKED
        )

        @pl.when(first + b > 2 * h + 1)
        def _(b=b):
            kv_all[first + b] = jnp.zeros(kv_all.shape[1:], kv_all.dtype)

    def relay_kv(i):
        remote(
            kv_ref, kv_all.at[s - 2 * i], kz_send.at[i], kz_recv.at[i], across
        ).wait_recv()
        kv_over(i).start()

    for i in range(1, reach + 1):
        pl.when(h - i >= 0)(functools.partial(relay_kv, i))

    def wait_kv(i):
        row = 2 * (h - i) + 1 - low
        remote(kv_ref, kv_all.at[row], ky_send.at[i], ky_recv.at[i], across).wait_recv()

    waiting = [(q, t) for q in range(pieces) for t in near]
    waiting += [(q, t) for q in range(pieces) for t in far]
    for i in range(reach + 1):
        pl.when(h - i >= 0)(functools.partial(wait_kv, i))
    if pieces > 1:
        start_weight(1, inside)
        start_weight(1, outside)
    own_kv.wait()

    scale = 1.0 / math.sqrt(HEAD_WIDTH)
    kv_width = kv_heads * HEAD_WIDTH
    per_kv = q_ref.shape[1] // kv_heads
    per, step_cols = att.shape[1], att.shape[3]
    cols = per * step_cols

    def attend(i):
        t = lax.rem(j + 1 + i // per, team)
        u = lax.rem(i, per)
        at = t * cols + u * step_cols
        kv_head = at // per_kv
        k_col = pl.multiple_of(kv_head * HEAD_WIDTH, HEAD_WIDTH)
        v_col = pl.multiple_of(kv_width + kv_head * HEAD_WIDTH, HEAD_WIDTH)
        span = pl.ds(first, blocks)
        keys = kv_all[span, :, pl.ds(k_col, HEAD_WIDTH)].reshape(window, HEAD_WIDTH)
        vals = kv_all[span, :, pl.ds(v_col, HEAD_WIDTH)].reshape(window, HEAD_WIDTH)
        for k in range(step_cols // HEAD_WIDTH):
            q_col = pl.multiple_of(at + k * HEAD_WIDTH, HEAD_WIDTH)
            q = q_ref[:, pl.ds(q_col, HEAD_WIDTH)]
            scores = lax.dot_general(
                q, keys, (((1,), (1,)), ((), ())), preferred_element_type=jnp.float32
            )
            scores = scores * scale + bias[...]
            top = jnp.max(scores, axis=1, keepdims=True)
            weights = jnp.exp(scores - top).astype(jnp.bfloat16)
            total = jnp.sum(weights.astype(jnp.float32), axis=1, keepdims=True)
            mixed = jnp.dot(weights, vals, preferred_element_type=jnp.float32)
            att[t, u, :, k * HEAD_WIDTH : (k + 1) * HEAD_WIDTH] = (mixed / total).astype(
                jnp.bfloat16
            )

    def a_place(t, u):
        return a_ref.at[
            pl.ds(pl.multiple_of(t * rows, rows), rows),
            pl.ds(pl.multiple_of(u * step_cols, step_cols), step_cols),
        ]

    def a_copy(t, u):
        return remote(
            att.at[t, u], a_place(j, u), a_send.at[0], a_recv.at[j, u], {"sect": base + t}
        )

    def step(i, carry):
        attend(i)
        last = i - 1

        @pl.when(jnp.logical_and(last >= 0, last < (team - 1) * per))
        def _():
            a_copy(lax.rem(j + 1 + last // per, team), lax.rem(last, per)).start()

        return carry

    steps = team * per
    segments = 4 if steps % 4 == 0 else 1
    for i in range(segments):
        lax.fori_loop(i * steps // segments, (i + 1) * steps // segments, step, 0)
        if i + 1 < segments:
            for _ in range(2):
                forward_weight(*waiting.pop(0))
    own_a = [
        pltpu.make_async_copy(att.at[j, u], a_place(j, u), own_a_sem.at[u]) for u in range(per)
    ]
    for copy in own_a:
        copy.start()
    while len(waiting) > (pieces - 1) * len(far):
        forward_weight(*waiting.pop(0))

    for _ in range(min(3, len(waiting))):
        forward_weight(*waiting.pop(0))
    team_peers = [lax.rem(j + i, team) for i in range(1, team)]
    for t in team_peers:
        for u in range(per):
            remote(
                att.at[t, u], a_place(t, u), a_send.at[0], a_recv.at[t, u], across
            ).wait_recv()
    for copy in own_a:
        copy.wait()

    span = team * w_cols

    def project(t, q, cut):
        left = a_ref[pl.ds(pl.multiple_of(t * chunk, chunk), chunk), :]
        which = cut.start // w_width
        at = cut.start - which * w_width
        part = jnp.dot(
            left, w_all[which, :, at : at + span], preferred_element_type=jnp.float32
        )
        p_first[pl.ds(2 * t, 2), :, :, cut] = part.astype(jnp.bfloat16).reshape(
            2, 2, moe_rows, span
        )

    enter, cross, along, collect, drain_first = reducer(
        place,
        line_at,
        lambda t: base + 2 * t + low,
        p_first,
        acc,
        rp_first,
        *[first_bufs.at[k] for k in range(4)],
        [tx_sems.at[pl.ds(0, 1)], rx_first.at[0]]
        + [tx_sems.at[pl.ds(1, 1)], rx_first.at[1]]
        + [tx_sems.at[pl.ds(2, 1)], rx_first.at[2]],
    )
    def items_of(q, which):
        start = q * w_width + which * span
        cut = slice(start, start + span)
        return [(t, 2 * q + which, cut) for t in line_others + [line_at]]

    def begin(items):
        for i, item in enumerate(items):
            project(*item)
            enter(*item)

    def forward(count):
        for _ in range(min(count, len(waiting))):
            forward_weight(*waiting.pop(0))

    behind = []
    for q in range(pieces):
        wait_weight(q, 0)
        behind += items_of(q, 0)
    begin(behind)
    for item in behind:
        cross(*item)
    forward(1)
    for q in range(pieces):
        if q + 1 == pieces:
            forward(len(waiting))
        items = items_of(q, 1)
        wait_weight(q, 1)
        begin(items)
        if q + 1 < pieces:
            for item in items:
                cross(*item)
            behind += items
    n = len(behind)
    for i, item in enumerate(items):
        cross(*item)
        for other in behind[i * n // len(items) : (i + 1) * n // len(items)]:
            along(*other)
    for item in items:
        along(*item)
    for item in behind + items:
        collect(*item)

    def columns(swap):
        order = [(t + swap) % sects for t in range(sects)]
        return jnp.concatenate(
            [
                acc[:, q * w_width + t * w_cols : q * w_width + (t + 1) * w_cols]
                for t in order
                for q in range(pieces)
            ],
            axis=1,
        )

    summed = jnp.where(base == 0, columns(0), columns(team))
    mid = (res_ref[...].astype(jnp.float32) + summed).astype(jnp.bfloat16)
    out_ref[0] = mid
    wide = mid.astype(jnp.float32)
    inverse = lax.rsqrt(jnp.mean(wide * wide, axis=1, keepdims=True) + NORM_EPS)
    normed = wide * inverse * gain_ref[...].astype(jnp.float32).reshape(1, width)
    lanes = xg.shape[3] - width
    lane = lax.broadcasted_iota(jnp.int32, (moe_rows, lanes), 1)
    place_of = lax.broadcasted_iota(jnp.int32, (lanes, moe_rows), 0)
    route = route_ref[...]
    route = route / jnp.sum(route, axis=0, keepdims=True)
    share = jnp.zeros((lanes, moe_rows), jnp.float32)
    for k in range(route.shape[0]):
        ids = ids_ref[k : k + 1, :]
        named = jnp.logical_or(place_of == ids, place_of == ids + experts)
        share = share + jnp.where(named, route[k : k + 1, :], 0.0)
    share = share.T
    high = share.astype(jnp.bfloat16).astype(jnp.float32)
    xg[s, c, :, width:] = jnp.where(lane < experts, high, share - high).astype(jnp.bfloat16)
    xg[s, c, :, :width] = normed.astype(jnp.bfloat16)

    guarded = []
    total = xg.shape[3]
    middle = total // 256 * 128
    row_cuts = [slice(0, middle), slice(middle, total)]

    def hop(t, p, slot, step):
        block = xg.at[2 * t + low, c, :, row_cuts[p]]
        return remote(
            block, block, row_tx_along.at[p, slot], row_along.at[p, t], {"sect": s + step}
        )

    def over(t, p):
        block = xg.at[2 * t + low, c, :, row_cuts[p]]
        return remote(block, block, row_tx.at[0], row_over.at[p, t], across)

    def to_pair(row):
        block = xg.at[row, c]
        remote(block, block, row_tx.at[1], row_pair.at[row], partner).start()

    def from_pair(row):
        block = xg.at[row, 1 - c]
        remote(block, block, row_tx.at[1], row_pair.at[row], partner).wait_recv()

    def from_over(t):
        for p, cut in enumerate(row_cuts):
            block = xg.at[2 * t + 1 - low, c, :, cut]
            remote(block, block, row_tx.at[0], row_over.at[p, t], across).wait_recv()

    paired = jnp.minimum(h, halves - 1 - h)
    away = jnp.where(2 * h < halves - 1, 1, -1)
    order = [h]
    hops = [0]
    for k in range(1, halves):
        near = (k + 1) // 2 * (-1 if k % 2 else 1)
        order.append(h + away * jnp.where(k <= 2 * paired, near, k - paired))
        hops.append(jnp.where(k <= 2 * paired, (k + 1) // 2, k - paired))

    def onward(k, p):
        t = order[k]
        return [
            (jnp.logical_and(t < h, h + 1 < halves), hop(t, p, t, 2)),
            (jnp.logical_and(t > h, h >= 1), hop(t, p, t, -2)),
        ]

    def relay_rows(k):
        t = order[k]
        for p in range(2):
            block = xg.at[2 * t + low, c, :, row_cuts[p]]
            remote(
                block, block, row_tx_along.at[p, t], row_along.at[p, t], across
            ).wait_recv()
            for when, copy in onward(k, p):
                pl.when(when)(copy.start)
            over(t, p).start()
        to_pair(2 * t + low)

    for k in range(1, halves):
        for p in range(2):
            guarded.extend(onward(k, p))

    def relay_step(i):
        for k in range(i + 1, halves):
            if (k + 1) // 2 <= i + 1:
                pl.when(hops[k] == i + 1)(functools.partial(relay_rows, k))

    for p in range(2):
        for when, copy in (
            (h + 1 < halves, hop(h, p, h, 2)),
            (h >= 1, hop(h, p, halves + h, -2)),
        ):
            pl.when(when)(copy.start)
            guarded.append((when, copy))
        over(h, p).start()
    to_pair(s)
    for load in loads:
        load.wait()

    def experts_of(i, t, q, cut):
        if q == 0:
            hidden_of(i, t)
        tile = min(512, width)
        for n in range(cut.start, cut.stop, tile):
            part = jnp.dot(
                hidden[...], down_ref[:, n : n + tile], preferred_element_type=jnp.float32
            )
            p_second[pl.ds(2 * t, 2), :, :, n : n + tile] = (
                (part * own_share(t)).astype(jnp.bfloat16).reshape(2, 2, moe_rows, tile)
            )

    def own_share(t):
        pair = xg[pl.ds(2 * t, 2), :, :, width:].astype(jnp.float32).reshape(chunk, lanes)
        expert = s * 2 + c
        at = lax.broadcasted_iota(jnp.int32, (chunk, lanes), 1)
        mine = jnp.logical_or(at == expert, at == expert + experts)
        return jnp.sum(jnp.where(mine, pair, 0.0), axis=1, keepdims=True)

    def hidden_of(i, t):
        relay_step(i)
        from_over(t)
        to_pair(2 * t + 1 - low)
        for row in (2 * t + low, 2 * t + 1 - low):
            from_pair(row)
        x = xg[pl.ds(2 * t, 2), :, :, :width].reshape(chunk, width)
        step = 256
        for n in range(0, hidden.shape[1], step):
            gate_act = jnp.dot(
                x, gate_ref[:, n : n + step], preferred_element_type=jnp.float32
            )
            up_act = jnp.dot(x, up_ref[:, n : n + step], preferred_element_type=jnp.float32)
            silu = gate_act / (1.0 + jnp.exp(-gate_act))
            hidden[:, n : n + step] = (silu * up_act).astype(jnp.bfloat16)

    cs, ry, zs = [cross_bufs.at[k, pl.ds(0, halves)] for k in range(3)]
    rz = cross_bufs.at[3]
    y_send, y_recv = tx_sems.at[pl.ds(4, 1)], rx_second.at[1]
    z_send, z_recv = tx_sems.at[pl.ds(5, 1)], z_second
    sems = [tx_sems.at[pl.ds(3, 1)], rx_second.at[0], y_send, y_recv, z_send, z_recv]
    enter, cross, _, _, drain_second = reducer(
        place, h, None, p_second, acc, rp_second, cs, ry, zs, rz, sems
    )
    parts = 2 if width % 1024 == 0 else 1
    size = width // parts
    cuts_of = [(q, slice(q * size, (q + 1) * size)) for q in range(parts)]

    def own_sum(t, q, cut):
        return (
            p_second[2 * t + low, c, :, cut].astype(jnp.float32)
            + rp_second[t, low, :, cut].astype(jnp.float32)
            + ry[t, :, cut].astype(jnp.float32)
        )

    def wait_across(t, q, cut):
        remote(
            cs.at[t, :, cut], ry.at[t, :, cut], y_send.at[0], y_recv.at[q, t], across
        ).wait_recv()

    def wait_along(slot, row, t, q, cut):
        remote(
            zs.at[t, :, cut], rz.at[slot, :, cut], z_send.at[0], z_recv.at[row, t], across
        ).wait_recv()

    def chain(t, q, cut):
        wait_across(t, q, cut)
        joined = jnp.where(t > h, h >= 1, h + 1 < halves)

        @pl.when(jnp.logical_not(joined))
        def _():
            zs[t, :, cut] = own_sum(t, q, cut).astype(jnp.bfloat16)

        @pl.when(joined)
        def _():
            wait_along(t, q, t, q, cut)
            zs[t, :, cut] = (
                own_sum(t, q, cut) + rz[t, :, cut].astype(jnp.float32)
            ).astype(jnp.bfloat16)

        landed = h - 1 == t
        remote(
            zs.at[t, :, cut],
            rz.at[jnp.where(landed, halves, t), :, cut],
            z_send.at[0],
            z_recv.at[q + jnp.where(landed, parts, 0), t],
            {"sect": s + jnp.where(t > h, 2, -2)},
        ).start()

    def finish(q, cut):
        wait_across(h, q, cut)
        acc[:, cut] = own_sum(h, q, cut)

        @pl.when(h >= 1)
        def _():
            wait_along(h, q, h, q, cut)
            acc[:, cut] += rz[h, :, cut].astype(jnp.float32)

        @pl.when(h + 1 < halves)
        def _():
            wait_along(halves, q + parts, h, q, cut)
            acc[:, cut] += rz[halves, :, cut].astype(jnp.float32)

    lower = h < halves // 2
    targets = [
        jnp.where(lower, halves // 2 + i, halves // 2 - 1 - i) for i in range(halves // 2)
    ]
    targets += [h - line_at + t for t in line_others]

    def each(step, t):
        for q, cut in cuts_of:
            step(t, q, cut)

    for i, t in enumerate(order):
        for q, cut in cuts_of:
            experts_of(i, t, q, cut)
            enter(t, q, cut)
        if i == halves - 2:
            each(cross, targets[0])
    for i, t in enumerate(targets[1:] + [h]):
        each(cross, t)
        if i < 0:
            each(chain, targets[i])
    for t in targets[0:]:
        each(chain, t)
    for q, cut in cuts_of:
        finish(q, cut)
    out_ref[1] = acc[...].astype(jnp.bfloat16)
    for i in range(1, reach + 1):
        pl.when(h + i < halves)(kv_up(i).wait_send)
    for i in range(reach + 1):
        pl.when(h - i >= 0)(kv_over(i).wait_send)
    some = pl.ds(0, team - 1)
    remote(att.at[some], att.at[some], a_send.at[0], a_recv.at[0, 0], across).wait_send()
    rows_sent = xg.at[pl.ds(0, halves), c]
    remote(rows_sent, rows_sent, row_tx.at[0], row_over.at[0, 0], across).wait_send()
    rows_sent = xg.at[:, c]
    remote(rows_sent, rows_sent, row_tx.at[1], row_pair.at[0], partner).wait_send()
    drain_weight()
    drain_first()
    drain_second()
    for when, copy in guarded:
        pl.when(when)(copy.wait_send)
    for copy in started:
        copy.wait_send()

def fused_layer(
    queries, keys, values, segments, proj, residual, gain, ids, route, gate, up, down
):
    groups = lax.axis_size("groups")
    sects = lax.axis_size("sect")
    heads = lax.axis_size("head")
    rows = queries.shape[0]
    team = sects // 2
    cols = queries.shape[1] // team
    step_cols = min(cols, 4 * HEAD_WIDTH)
    per = cols // step_cols
    pieces = 2 if proj.shape[1] % 256 == 0 else 1
    w_rows = proj.shape[0] // team
    blocks = min(sects, -(-segments.shape[0] // (2 * rows)) + 1)
    halves = sects // 2
    block = residual.shape
    lanes = -(-2 * sects * heads // 128) * 128
    bf16 = jnp.bfloat16
    kv_shape = (rows, 2 * keys.shape[1])
    operands = (
        queries,
        keys,
        values,
        segments.reshape(sects, 1, rows),
        proj,
        residual,
        gain,
        ids.T,
        route.T,
        gate,
        up,
        down,
    )
    both = pl.pallas_call(
        functools.partial(layer_kernel, groups, sects, keys.shape[1] // HEAD_WIDTH),
        out_shape=jax.ShapeDtypeStruct((2,) + block, bf16),
        in_specs=[pl.BlockSpec(memory_space=pltpu.HBM)] * len(operands),
        out_specs=VMEM_SPEC,
        scratch_shapes=[
            pltpu.VMEM(queries.shape, bf16),
            pltpu.VMEM((sects, 1, rows), jnp.int32),
            pltpu.VMEM(block, bf16),
            pltpu.VMEM(gain.shape, bf16),
            pltpu.VMEM(ids.shape[::-1], jnp.int32),
            pltpu.VMEM(route.shape[::-1], jnp.float32),
            DMA((6,)),
            pltpu.VMEM(gate.shape[1:], bf16),
            pltpu.VMEM(up.shape[1:], bf16),
            pltpu.VMEM(down.shape[1:], bf16),
            pltpu.VMEM((4 * block[0], gate.shape[2]), bf16),
            pltpu.VMEM((sects, heads, block[0], block[1] + lanes), bf16),
            pltpu.VMEM(block, jnp.float32),
            pltpu.VMEM((team, heads) + block, bf16),
            pltpu.VMEM((sects, heads) + block, bf16),
            pltpu.VMEM((team // 2, 2) + block, bf16),
            pltpu.VMEM((halves, 2) + block, bf16),
            pltpu.VMEM((4, team // 2) + block, bf16),
            pltpu.VMEM((4, halves + 1) + block, bf16),
            DMA((2,)),
            DMA((sects,)),
            DMA((2, halves)),
            DMA((2, sects)),
            DMA((2, halves)),
            DMA((6,)),
            DMA((3, 2 * pieces, team // 2)),
            DMA((2, 2, halves)),
            DMA((4, halves)),
            DMA((3,)),
            pltpu.VMEM((rows * team, cols), bf16),
            pltpu.VMEM((pieces, w_rows, proj.shape[1] // pieces * sects), bf16),
            pltpu.VMEM(kv_shape, bf16),
            pltpu.VMEM((sects,) + kv_shape, bf16),
            pltpu.VMEM((team, per, rows, step_cols), bf16),
            pltpu.VMEM((rows, blocks * rows), jnp.float32),
            DMA((halves,)),
            DMA((halves,)),
            DMA((halves,)),
            DMA((halves,)),
            DMA((1,)),
            DMA((team, per)),
            DMA((1,)),
            DMA((pieces, sects)),
            DMA((groups,)),
            DMA((groups, pieces, 2)),
            DMA((3,)),
            DMA((pieces,)),
            DMA((per,)),
        ],
        compiler_params=pltpu.CompilerParams(
            collective_id=4, has_side_effects=True, vmem_limit_bytes=LAYER_ROOM
        ),
        name="layer",
    )(*[pltpu.with_memory_space_constraint(x, pltpu.HBM) for x in operands])
    return both[0], both[1]

def shards(
    queries,
    packed_key_rows,
    values,
    segments,
    proj_weight,
    residual,
    norm_gain,
    expert_ids,
    route_weights,
    gate_weight,
    up_weight,
    down_weight,
):
    sects = lax.axis_size("sect")
    heads = lax.axis_size("head")
    s = lax.axis_index("sect")
    c = lax.axis_index("head")
    experts = sects * heads
    moe_rows, width = residual.shape
    fits = experts * moe_rows * width * 24 <= VMEM_ROOM
    if fits and sects % 4 == 0 and proj_weight.shape[1] % 128 == 0:
        return fused_layer(
            queries,
            packed_key_rows,
            values,
            segments,
            proj_weight,
            residual,
            norm_gain,
            expert_ids,
            route_weights,
            gate_weight,
            up_weight,
            down_weight,
        )
    attended, weight = exchange_attention(
        queries, packed_key_rows, values, segments, proj_weight
    )
    partial_rows = jnp.dot(attended, weight, preferred_element_type=jnp.float32)
    projected = sum_scatter(partial_rows.astype(jnp.bfloat16), moe_rows, 1)

    hidden_mid = (residual.astype(jnp.float32) + projected).astype(jnp.bfloat16)
    mid_float = lax.optimization_barrier(hidden_mid).astype(jnp.float32)
    inverse = lax.rsqrt(jnp.mean(mid_float * mid_float, axis=1, keepdims=True) + NORM_EPS)
    normed = (mid_float * inverse * norm_gain.astype(jnp.float32)[None, :]).astype(jnp.bfloat16)

    route_share = route_weights / jnp.sum(route_weights, axis=1, keepdims=True)
    named = expert_ids[:, :, None] == jnp.arange(experts, dtype=jnp.int32)[None, None, :]
    share = jnp.sum(jnp.where(named, route_share[:, :, None], 0.0), axis=1)
    share_high = lax.reduce_precision(share, 8, 7)
    share_low = (share - share_high).astype(jnp.bfloat16)
    pad = -(2 * experts) % 128
    sent = jnp.concatenate(
        [
            normed,
            share_high.astype(jnp.bfloat16),
            share_low,
            jnp.zeros((moe_rows, pad), jnp.bfloat16),
        ],
        axis=1,
    )
    gathered = gather_rows(sent, 2)
    expert = s * heads + c
    all_rows = gathered[:, :width]
    pair = gathered[:, width:].astype(jnp.float32)
    lane = jnp.arange(pair.shape[1], dtype=jnp.int32)[None, :]
    mine = jnp.logical_or(lane == expert, lane == expert + experts)
    own_share = jnp.sum(jnp.where(mine, pair, 0.0), axis=1, keepdims=True)
    gate_act = jnp.dot(all_rows, gate_weight[0], preferred_element_type=jnp.float32)
    up_act = jnp.dot(all_rows, up_weight[0], preferred_element_type=jnp.float32)
    hidden = (jax.nn.silu(gate_act) * up_act).astype(jnp.bfloat16)
    result = jnp.dot(hidden, down_weight[0], preferred_element_type=jnp.float32)
    mixed = (result * own_share).astype(jnp.bfloat16)
    mixture = sum_scatter(mixed, moe_rows, 3)
    return (hidden_mid, mixture.astype(jnp.bfloat16))

def solution(mesh):
    rows = P(("groups", "sect", "head"), None)
    split = P(("groups", "sect"), "head")
    expert = P(("sect", "head"), None, None)
    placed = (
        split,
        split,
        split,
        P("groups"),
        P("head", "sect"),
        rows,
        P(),
        rows,
        rows,
        expert,
        expert,
        expert,
    )
    return jax.shard_map(
        shards, mesh=mesh, in_specs=placed, out_specs=(rows, rows), check_vma=False
    )
```
